512 devices in a mesh: lon: 32 (over x, y, z_hi), lat: 16 (over z_lo, core).
Axes of the slice: x: 4, y: 4, z: 16 (z_hi: 2, z_lo: 8; z = z_hi * 8 + z_lo), core: 2. Of those that a mesh axis runs over, the one named last changes fastest.
Arguments:
- cells: bfloat16 [1024, 2048, 128], P('lat', 'lon'), may hold values from -6 to 6
- ocean_mask: int32 [1024, 2048], P('lat', 'lon'), may hold values from 0 to 1, as said below
- cotangent: bfloat16 [1024, 2048, 128], P('lat', 'lon'), may hold values from -6 to 6
- kernel: float32 [7, 7, 128], replicated, may hold values from -0.875 to 0.875
- conv_bias: float32 [128], replicated, may hold values from -3 to 3
- gain: float32 [128], replicated, may hold values from 0.1 to 1.9
- shift: float32 [128], replicated, may hold values from -3 to 3
- w_in: bfloat16 [128, 512], replicated, may hold values from -0.5 to 0.5
- b_in: float32 [512], replicated, may hold values from -3 to 3
- w_out: bfloat16 [512, 128], replicated, may hold values from -0.25 to 0.25
Outputs:
- cells_grad: bfloat16 [1024, 2048, 128], P('lat', 'lon')
- grad_kernel: float32 [7, 7, 128], replicated
- grad_bias: float32 [128], replicated
- grad_gain: float32 [128], replicated
- grad_shift: float32 [128], replicated
- grad_in: float32 [128, 512], replicated
- grad_b: float32 [512], replicated
- grad_out: float32 [512, 128], replicated
The draws below stay inside these ranges and needn't reach their ends.
Inputs may be any that keep to these rules, and one draw needn't show every extreme that they name: `ocean_mask`: within each aligned 64 x 64 block the ocean cells are either all cells, none, or those on one side of a straight line; some blocks are all land and some all ocean.
All inputs are finite; a program needn't handle non-finite values.
Results may differ from the reference program's by a relative error of at most 0.006.
Values may be sent and summed in bfloat16 or wider, within the bound.
No kernel may reach another device: no remote copies, remote signals or barrier semaphores. Data moves between devices by JAX's collectives and lax.ppermute only.
A program may use at most 128 MiB of HBM per device.

```python
import jax
import jax.numpy as jnp
from jax import lax

BS = 64
C = 128
HID = 512
KS = 7
HALF = 3
LATC = 1024
LONC = 2048


def draw_ocean_mask(key, part):
    rows_b = LATC // BS
    cols_b = LONC // BS
    key_kind, key_first, key_second, key_offset = jax.random.split(key, 4)
    kinds = jax.random.randint(key_kind, (rows_b, cols_b), 0, 4)
    eastern = (jnp.arange(cols_b, dtype=jnp.int32) >= cols_b // 2)[None, :]
    kinds = jnp.where(eastern & (kinds == 0), 1, kinds)
    kinds = kinds.at[0, 0].set(0).at[0, 1].set(1).at[0, cols_b // 2].set(1)
    slope_row = jax.random.randint(key_first, (rows_b, cols_b), -3, 4)
    slope_col = jax.random.randint(key_second, (rows_b, cols_b), -3, 4)
    offsets = jax.random.randint(key_offset, (rows_b, cols_b), -2 * BS, 2 * BS)

    def expand(table):
        return jnp.repeat(jnp.repeat(table, BS, axis=0), BS, axis=1)
    local_row = (jnp.arange(LATC, dtype=jnp.int32) % BS - BS // 2)[:, None]
    local_col = (jnp.arange(LONC, dtype=jnp.int32) % BS - BS // 2)[None, :]
    coast = (expand(slope_row) * local_row + expand(slope_col) * local_col > expand(offsets)).astype(jnp.int32)
    kind_cells = expand(kinds)
    return jnp.where(kind_cells == 0, 0, jnp.where(kind_cells == 1, 1, coast)).astype(jnp.int32)


def steps_of(stream_key, shape, pieces, least, high):
    factor_of, own = 1.0, jax.random.fold_in(stream_key, 6)
    for position, shards_of in pieces:
        steps = jnp.exp(jax.random.uniform(jax.random.fold_in(own, position), (shards_of,), jnp.float32, least / len(pieces), high / len(pieces)))
        factor_of = factor_of * jnp.repeat(steps, shape[position] // shards_of).reshape([-1 if axis == position else 1 for axis in range(len(shape))])
    return factor_of


def scatter_about(key, shape, width, most, pieces=(), kind=jnp.bfloat16):
    values = jax.random.normal(key, shape, jnp.float32) * width
    if len(pieces) > 0:
        values = steps_of(key, shape, pieces, -0.22, 0.18) * values
    return jnp.clip(values, min=-most, max=most).astype(kind)


def setup_inputs(seed: int = 0) -> dict:
    splits = jax.random.split(jax.random.key(seed), 11)
    cells = scatter_about(splits[0], (LATC, LONC, C), 1.0, 6.0, ((0, 16), (1, 32)))
    ocean_mask = draw_ocean_mask(jax.random.fold_in(splits[10], 71), 0)
    cotangent = scatter_about(splits[2], (LATC, LONC, C), 1.0, 6.0, ((0, 16), (1, 32)))
    kernel = scatter_about(splits[3], (KS, KS, C), (KS * KS) ** -0.5, 0.875, (), jnp.float32)
    conv_bias = scatter_about(splits[4], (C,), 0.5, 3.0, (), jnp.float32)
    gain = jnp.clip(1.0 + 0.18 * jax.random.normal(splits[5], (C,), jnp.float32), 0.1, 1.9)
    shift = scatter_about(splits[6], (C,), 0.5, 3.0, (), jnp.float32)
    w_in = scatter_about(splits[7], (C, HID), C ** -0.5, 0.5)
    b_in = scatter_about(splits[8], (HID,), 0.5, 3.0, (), jnp.float32)
    w_out = scatter_about(splits[9], (HID, C), HID ** -0.5, 0.25)
    return dict(cells=cells, ocean_mask=ocean_mask, cotangent=cotangent, kernel=kernel, conv_bias=conv_bias, gain=gain, shift=shift, w_in=w_in, b_in=b_in, w_out=w_out)


def depthwise(padded, kernel, height, across):
    summed = jnp.zeros((height, across, padded.shape[2]), jnp.float32)
    for row_off in range(KS):
        for col_off in range(KS):
            summed = summed + kernel[row_off, col_off] * padded[row_off:row_off + height, col_off:col_off + across].astype(jnp.float32)
    return summed

def transposed(padded, kernel, height, across):
    summed = jnp.zeros((height, across, padded.shape[2]), jnp.float32)
    for row_off in range(KS):
        for col_off in range(KS):
            first_row = KS - 1 - row_off
            first_col = KS - 1 - col_off
            summed = summed + kernel[row_off, col_off] * padded[first_row:first_row + height, first_col:first_col + across].astype(jnp.float32)
    return summed

def gelu_tanh(value):
    return jax.nn.gelu(value, approximate=True)

def forward_part(padded, ocean, cotangent, kernel, conv_bias, gain, shift, w_in, b_in, w_out):
    height, across, channels = cotangent.shape
    conv = depthwise(padded, kernel, height, across) + conv_bias
    average = lax.optimization_barrier(jnp.mean(conv, axis=-1, keepdims=True))
    centred = conv - average
    variance = lax.optimization_barrier(jnp.mean(centred * centred, axis=-1, keepdims=True))
    inverse_std = lax.rsqrt(variance + 1e-06)
    scaled = centred * inverse_std
    normed = (scaled * gain + shift).astype(jnp.bfloat16).reshape(height * across, channels)
    preact = jnp.dot(normed, w_in, preferred_element_type=jnp.float32) + b_in
    activation = gelu_tanh(preact).astype(jnp.bfloat16)
    out_grad = (cotangent * ocean).reshape(height * across, channels)
    grad_out = lax.dot_general(activation, out_grad, (((0,), (0,)), ((), ())), preferred_element_type=jnp.float32)
    act_grad = lax.dot_general(out_grad, w_out, (((1,), (1,)), ((), ())), preferred_element_type=jnp.float32)
    hidden_grad = jax.vjp(gelu_tanh, preact)[1](act_grad)[0].astype(jnp.bfloat16)
    return (normed, scaled, inverse_std, hidden_grad, grad_out)

def backward_part(padded, normed, scaled, inverse_std, hidden_grad, gain, w_in):
    height, across, channels = scaled.shape
    grad_in = lax.dot_general(normed, hidden_grad, (((0,), (0,)), ((), ())), preferred_element_type=jnp.float32)
    grad_b = lax.optimization_barrier(jnp.sum(hidden_grad.astype(jnp.float32), axis=0))
    norm_grad = lax.dot_general(hidden_grad, w_in, (((1,), (1,)), ((), ())), preferred_element_type=jnp.float32).reshape(height, across, channels)
    grad_gain = lax.optimization_barrier(jnp.sum(norm_grad * scaled, axis=(0, 1)))
    grad_shift = lax.optimization_barrier(jnp.sum(norm_grad, axis=(0, 1)))
    weighted = norm_grad * gain
    conv_grad = (inverse_std * (weighted - lax.optimization_barrier(jnp.mean(weighted, axis=-1, keepdims=True)) - scaled * lax.optimization_barrier(jnp.mean(weighted * scaled, axis=-1, keepdims=True)))).astype(jnp.bfloat16)
    conv_wide = conv_grad.astype(jnp.float32)
    grad_bias = lax.optimization_barrier(jnp.sum(conv_wide, axis=(0, 1)))
    rows_list = []
    for row_off in range(KS):
        cols_list = []
        for col_off in range(KS):
            window = padded[row_off:row_off + height, col_off:col_off + across].astype(jnp.float32)
            cols_list.append(lax.optimization_barrier(jnp.sum(conv_wide * window, axis=(0, 1))))
        rows_list.append(jnp.stack(cols_list))
    grad_kernel = jnp.stack(rows_list)
    return (conv_grad, grad_kernel, grad_bias, grad_gain, grad_shift, grad_in, grad_b)

def pad_grid(field):
    wrapped = jnp.concatenate([field[:, -HALF:], field, field[:, :HALF]], axis=1)
    return jnp.pad(wrapped, ((HALF, HALF), (0, 0), (0, 0)))

def reference(cells, ocean_mask, cotangent, kernel, conv_bias, gain, shift, w_in, b_in, w_out):
    ocean = ocean_mask.astype(jnp.bfloat16)[..., None]
    masked = cells * ocean
    padded = pad_grid(masked)
    slabs = LATC // BS

    def one_slab(running, slab):
        first_row = slab * BS
        window = lax.dynamic_slice_in_dim(padded, first_row, BS + 2 * HALF, 0)
        cot_slab = lax.dynamic_slice_in_dim(cotangent, first_row, BS, 0)
        ocean_slab = lax.dynamic_slice_in_dim(ocean, first_row, BS, 0)
        normed, scaled, inverse_std, hidden_grad, grad_out = forward_part(window, ocean_slab, cot_slab, kernel, conv_bias, gain, shift, w_in, b_in, w_out)
        results = backward_part(window, normed, scaled, inverse_std, hidden_grad, gain, w_in)
        partial_value = tuple(results[1:]) + (grad_out,)
        return (jax.tree.map(lambda left, right: left + right, running, partial_value), results[0])
    start = (jnp.zeros((KS, KS, C), jnp.float32), jnp.zeros((C,), jnp.float32), jnp.zeros((C,), jnp.float32), jnp.zeros((C,), jnp.float32), jnp.zeros((C, HID), jnp.float32), jnp.zeros((HID,), jnp.float32), jnp.zeros((HID, C), jnp.float32))
    totals, conv_grads = lax.scan(one_slab, start, jnp.arange(slabs, dtype=jnp.int32))
    conv_grad = conv_grads.reshape(LATC, LONC, C)
    grad_padded = pad_grid(conv_grad)

    def back_slab(slab):
        first_row = slab * BS
        window = lax.dynamic_slice_in_dim(grad_padded, first_row, BS + 2 * HALF, 0)
        cot_slab = lax.dynamic_slice_in_dim(cotangent, first_row, BS, 0)
        ocean_slab = lax.dynamic_slice_in_dim(ocean, first_row, BS, 0)
        spread_back = transposed(window, kernel, BS, LONC)
        return ((cot_slab.astype(jnp.float32) + spread_back) * ocean_slab.astype(jnp.float32)).astype(jnp.bfloat16)
    cells_grad = lax.map(back_slab, jnp.arange(slabs, dtype=jnp.int32)).reshape(LATC, LONC, C)
    factor = lax.rsqrt(jnp.float32(LATC * LONC))
    grad_kernel, grad_bias, grad_gain, grad_shift, grad_in, grad_b, grad_out = [entry * factor for entry in totals]
    return (cells_grad, grad_kernel, grad_bias, grad_gain, grad_shift, grad_in, grad_b, grad_out)
```

```python
import functools

import jax
import jax.numpy as jnp
from jax import lax
from jax.experimental import pallas as pl
from jax.experimental.pallas import tpu as pltpu
from jax.sharding import PartitionSpec as P

KS = 7
HALF = 3
SUB = 8
ROOT = 0.7978845608028654
CUBE = 0.044715
VMEM = pl.BlockSpec(memory_space=pltpu.VMEM)


def spread_rows(src_ref, tiles_ref, buf_ref, rows, taps):
    across = src_ref.shape[1]

    def one(row, _):
        buf_ref[0:across, :] = src_ref[row].astype(jnp.float32)
        for tap in range(taps):
            tiles_ref[row, tap] = buf_ref[pl.ds(tap, SUB, stride=SUB), :]
        return 0

    lax.fori_loop(0, rows, one, 0)


def conv_row(tiles_ref, kernel_ref, row, flip):
    total = [None] * SUB
    for a in range(KS):
        cells = [tiles_ref[row + a, t] for t in range(SUB + KS - 1)]
        for b in range(KS):
            ka, kb = (KS - 1 - a, KS - 1 - b) if flip else (a, b)
            weight = jnp.broadcast_to(kernel_ref[ka, kb : kb + 1, :], (SUB, 128))
            for t in range(SUB):
                term = weight * cells[t + b]
                total[t] = term if total[t] is None else total[t] + term
    return total


def gather_row(tiles, buf_ref):
    for t in range(SUB):
        buf_ref[pl.ds(t, SUB, stride=SUB), :] = tiles[t]
    return buf_ref[0 : SUB * SUB, :]


def block_kernel(
    chunk,
    padded_ref, out_grad_ref, kernel_ref, bias_ref, gain_ref, shift_ref, w_in_ref, b_in_ref, w_out_ref,
    conv_grad_ref, grad_bias_ref, grad_gain_ref, grad_shift_ref, grad_in_ref, grad_b_ref, grad_out_ref,
    tiles_ref, buf_ref, og_buf, conv_buf, og_tiles, grad_out_t,
):
    height = out_grad_ref.shape[0]
    cells = chunk * 64
    spread_rows(padded_ref, tiles_ref, buf_ref, height + KS - 1, SUB + KS - 1)
    for ref in (grad_bias_ref, grad_gain_ref, grad_shift_ref, grad_in_ref, grad_b_ref, grad_out_t):
        ref[...] = jnp.zeros_like(ref)
    bias = bias_ref[...]
    gain = gain_ref[...]
    shift = shift_ref[...]
    b_in = b_in_ref[...]

    def one(step, _):
        first = step * chunk

        def conv_one(r, _):
            row = first + r
            total = conv_row(tiles_ref, kernel_ref, row, False)
            for t in range(SUB):
                conv_buf[r, t] = total[t]
            og_buf[0:64, :] = out_grad_ref[row].astype(jnp.float32)
            for t in range(SUB):
                og_tiles[r, t] = og_buf[pl.ds(t, SUB, stride=SUB), :]
            return 0

        lax.fori_loop(0, chunk, conv_one, 0)
        conv = conv_buf[...].reshape(cells, 128) + bias
        out_grad = og_tiles[...].reshape(cells, 128).astype(jnp.bfloat16)
        average = jnp.mean(conv, axis=-1, keepdims=True)
        centred = conv - average
        variance = jnp.mean(centred * centred, axis=-1, keepdims=True)
        inverse = lax.rsqrt(variance + 1e-06)
        scaled = centred * inverse
        normed = (scaled * gain + shift).astype(jnp.bfloat16)
        v = jnp.dot(normed, w_in_ref[...], preferred_element_type=jnp.float32) + b_in
        act_grad = lax.dot_general(
            out_grad, w_out_ref[...], (((1,), (1,)), ((), ())), preferred_element_type=jnp.float32
        )
        square = v * v
        half = 0.5 + 0.5 * jnp.tanh(v * (ROOT + (ROOT * CUBE) * square))
        activation = (v * half).astype(jnp.bfloat16)
        slope = half + (half - half * half) * (v * (2 * ROOT + (6 * ROOT * CUBE) * square))
        hidden = (act_grad * slope).astype(jnp.bfloat16)
        grad_out_t[...] += lax.dot_general(
            out_grad, activation, (((0,), (0,)), ((), ())), preferred_element_type=jnp.float32
        )
        grad_in_ref[...] += lax.dot_general(
            normed, hidden, (((0,), (0,)), ((), ())), preferred_element_type=jnp.float32
        )
        grad_b_ref[...] += jnp.sum(
            hidden.astype(jnp.float32).reshape(cells // SUB, SUB, 512), axis=0
        )
        norm_grad = lax.dot_general(
            hidden, w_in_ref[...], (((1,), (1,)), ((), ())), preferred_element_type=jnp.float32
        )
        grad_gain_ref[...] += jnp.sum((norm_grad * scaled).reshape(-1, SUB, 128), axis=0)
        grad_shift_ref[...] += jnp.sum(norm_grad.reshape(-1, SUB, 128), axis=0)
        weighted = norm_grad * gain
        conv_grad = inverse * (
            weighted
            - jnp.mean(weighted, axis=-1, keepdims=True)
            - scaled * jnp.mean(weighted * scaled, axis=-1, keepdims=True)
        )
        rounded = conv_grad.astype(jnp.bfloat16).astype(jnp.float32).reshape(chunk, SUB, SUB, 128)
        grad_bias_ref[...] += jnp.sum(rounded, axis=(0, 1))
        for r in range(chunk):
            natural = gather_row([rounded[r, t] for t in range(SUB)], og_buf)
            conv_grad_ref[first + r] = natural.astype(jnp.bfloat16)
        return 0

    lax.fori_loop(0, height // chunk, one, 0)
    grad_out_ref[...] = grad_out_t[...].T


def tap_kernel(padded_ref, grad_ref, out_ref, tiles_ref, buf_ref, sums_ref, pair):
    height = grad_ref.shape[0]
    spread_rows(padded_ref, tiles_ref, buf_ref, height + KS - 1, SUB + KS - 1)
    sums_ref[...] = jnp.zeros_like(sums_ref)

    def one(row, _):
        buf_ref[0:64, :] = grad_ref[row].astype(jnp.float32)
        grads = [buf_ref[pl.ds(t, SUB, stride=SUB), :] for t in range(SUB)]
        for a in range(KS):
            cells = [tiles_ref[row + a, t] for t in range(SUB + KS - 1)]
            for b in range(KS):
                total = sums_ref[a, b]
                for t in range(SUB):
                    total = total + grads[t] * cells[t + b]
                sums_ref[a, b] = total
        return 0

    lax.fori_loop(0, height, one, 0)
    out_ref[...] = jnp.sum(sums_ref[...], axis=2)


def back_kernel(padded_ref, cot_ref, mask_ref, kernel_ref, out_ref, tiles_ref, buf_ref):
    height = cot_ref.shape[0]
    spread_rows(padded_ref, tiles_ref, buf_ref, height + KS - 1, SUB + KS - 1)

    def one(row, _):
        total = conv_row(tiles_ref, kernel_ref, row, True)
        spread = gather_row(total, buf_ref)
        out_ref[row] = (
            (cot_ref[row].astype(jnp.float32) + spread) * mask_ref[row].astype(jnp.float32)
        ).astype(jnp.bfloat16)
        return 0

    lax.fori_loop(0, height, one, 0)


def shifted(piece, axis, up, periodic):
    count = lax.axis_size(axis)
    pairs = [(i, i + 1) for i in range(count - 1)]
    if periodic:
        pairs.append((count - 1, 0))
    if not up:
        pairs = [(target, source) for source, target in pairs]
    return lax.ppermute(piece, axis, pairs)


def with_halo(block):
    west = shifted(block[:, -HALF:], "lon", True, True)
    east = shifted(block[:, :HALF], "lon", False, True)
    wide = jnp.concatenate([west, block, east], axis=1)
    south = shifted(wide[-HALF:], "lat", True, False)
    north = shifted(wide[:HALF], "lat", False, False)
    return jnp.concatenate([south, wide, north], axis=0)


def f32(*shape):
    return jax.ShapeDtypeStruct(shape, jnp.float32)


def body(cells, ocean_mask, cotangent, kernel, conv_bias, gain, shift, w_in, b_in, w_out, chunk=4):
    height, across, channels = cells.shape
    ocean = jnp.broadcast_to(ocean_mask.astype(jnp.bfloat16)[..., None], cells.shape)
    masked = cells * ocean
    out_grad = cotangent * ocean
    padded = with_halo(masked)
    tall = height + 2 * HALF
    tiles = pltpu.VMEM((tall, SUB + KS - 1, SUB, channels), jnp.float32)
    row_buf = pltpu.VMEM((72, channels), jnp.float32)
    hidden = w_in.shape[1]
    conv_grad, bias8, gain8, shift8, grad_in, b8, grad_out = pl.pallas_call(
        functools.partial(block_kernel, chunk),
        out_shape=(
            jax.ShapeDtypeStruct(cells.shape, jnp.bfloat16),
            f32(SUB, channels), f32(SUB, channels), f32(SUB, channels),
            f32(channels, hidden), f32(SUB, hidden), f32(hidden, channels),
        ),
        in_specs=[VMEM] * 9,
        out_specs=[VMEM] * 7,
        scratch_shapes=[
            tiles, row_buf, row_buf,
            pltpu.VMEM((chunk, SUB, SUB, channels), jnp.float32),
            pltpu.VMEM((chunk, SUB, SUB, channels), jnp.float32),
            pltpu.VMEM((channels, hidden), jnp.float32),
        ],
        name="block",
    )(
        padded, out_grad, kernel, conv_bias.reshape(1, -1), gain.reshape(1, -1), shift.reshape(1, -1),
        w_in, b_in.reshape(1, -1), w_out,
    )
    grad_padded = with_halo(conv_grad)
    grad_kernel = pl.pallas_call(
        functools.partial(tap_kernel, pair=None),
        out_shape=f32(KS, KS, channels),
        in_specs=[VMEM] * 2,
        out_specs=VMEM,
        scratch_shapes=[tiles, row_buf, pltpu.VMEM((KS, KS, SUB, channels), jnp.float32)],
        name="taps",
    )(padded, conv_grad)
    grads = (
        grad_kernel, jnp.sum(bias8, 0), jnp.sum(gain8, 0), jnp.sum(shift8, 0), grad_in, jnp.sum(b8, 0), grad_out
    )
    grads = lax.psum(grads, ("lon", "lat"))
    cells_grad = pl.pallas_call(
        back_kernel,
        out_shape=jax.ShapeDtypeStruct(cells.shape, jnp.bfloat16),
        in_specs=[VMEM] * 4,
        out_specs=VMEM,
        scratch_shapes=[tiles, row_buf],
        name="back",
    )(grad_padded, cotangent, ocean, kernel)
    factor = lax.rsqrt(jnp.float32(height * across * lax.axis_size("lon") * lax.axis_size("lat")))
    return (cells_grad,) + tuple(g * factor for g in grads)


def solution(mesh):
    whole = P("lat", "lon", None)
    in_specs = (whole, P("lat", "lon"), whole) + (P(),) * 7
    out_specs = (whole,) + (P(),) * 7
    return jax.shard_map(body, mesh=mesh, in_specs=in_specs, out_specs=out_specs, check_vma=False)
```

```python
import functools

import jax
import jax.numpy as jnp
from jax import lax
from jax.experimental import pallas as pl
from jax.experimental.pallas import tpu as pltpu
from jax.sharding import PartitionSpec as P

KS = 7
HALF = 3
SMALL = 64
SUB = 8
ROOT = 0.7978845608028654
CUBE = 0.044715
VMEM = pl.BlockSpec(memory_space=pltpu.VMEM)


def spread_rows(src_ref, tiles_ref, buf_ref, rows, taps):
    across = src_ref.shape[1]

    def one(row, _):
        buf_ref[0:across, :] = src_ref[row].astype(jnp.float32)
        for tap in range(taps):
            tiles_ref[row, tap] = buf_ref[pl.ds(tap, SUB, stride=SUB), :]
        return 0

    lax.fori_loop(0, rows, one, 0)


def conv_row(tiles_ref, kernel_ref, row, flip):
    total = [None] * SUB
    for a in range(KS):
        cells = [tiles_ref[row + a, t] for t in range(SUB + KS - 1)]
        for b in range(KS):
            ka, kb = (KS - 1 - a, KS - 1 - b) if flip else (a, b)
            weight = jnp.broadcast_to(kernel_ref[ka, kb : kb + 1, :], (SUB, 128))
            for t in range(SUB):
                term = weight * cells[t + b]
                total[t] = term if total[t] is None else total[t] + term
    return total


def gather_row(tiles, buf_ref):
    for t in range(SUB):
        buf_ref[pl.ds(t, SUB, stride=SUB), :] = tiles[t]
    return buf_ref[0 : SUB * SUB, :]


def block_kernel(
    chunk,
    padded_ref, out_grad_ref, kernel_ref, bias_ref, gain_ref, shift_ref, w_in_ref, b_in_ref, w_out_ref,
    conv_grad_ref, grad_bias_ref, grad_gain_ref, grad_shift_ref, grad_in_ref, grad_b_ref, grad_out_ref,
    tiles_ref, buf_ref, og_buf, conv_buf, og_tiles, grad_out_t,
):
    height = out_grad_ref.shape[0]
    cells = chunk * 64
    spread_rows(padded_ref, tiles_ref, buf_ref, height + KS - 1, SUB + KS - 1)
    for ref in (grad_bias_ref, grad_gain_ref, grad_shift_ref, grad_in_ref, grad_b_ref, grad_out_t):
        ref[...] = jnp.zeros_like(ref)
    bias = bias_ref[...]
    gain = gain_ref[...]
    shift = shift_ref[...]
    b_in = b_in_ref[...]

    def one(step, _):
        first = step * chunk

        def conv_one(r, _):
            row = first + r
            total = conv_row(tiles_ref, kernel_ref, row, False)
            for t in range(SUB):
                conv_buf[r, t] = total[t]
            og_buf[0:64, :] = out_grad_ref[row].astype(jnp.float32)
            for t in range(SUB):
                og_tiles[r, t] = og_buf[pl.ds(t, SUB, stride=SUB), :]
            return 0

        lax.fori_loop(0, chunk, conv_one, 0)
        conv = conv_buf[...].reshape(cells, 128) + bias
        out_grad = og_tiles[...].reshape(cells, 128).astype(jnp.bfloat16)
        average = jnp.mean(conv, axis=-1, keepdims=True)
        centred = conv - average
        variance = jnp.mean(centred * centred, axis=-1, keepdims=True)
        inverse = lax.rsqrt(variance + 1e-06)
        scaled = centred * inverse
        normed = (scaled * gain + shift).astype(jnp.bfloat16)
        v = jnp.dot(normed, w_in_ref[...], preferred_element_type=jnp.float32) + b_in
        act_grad = lax.dot_general(
            out_grad, w_out_ref[...], (((1,), (1,)), ((), ())), preferred_element_type=jnp.float32
        )
        square = v * v
        half = 0.5 + 0.5 * jnp.tanh(v * (ROOT + (ROOT * CUBE) * square))
        activation = (v * half).astype(jnp.bfloat16)
        slope = half + (half - half * half) * (v * (2 * ROOT + (6 * ROOT * CUBE) * square))
        hidden = (act_grad * slope).astype(jnp.bfloat16)
        grad_out_t[...] += lax.dot_general(
            out_grad, activation, (((0,), (0,)), ((), ())), preferred_element_type=jnp.float32
        )
        grad_in_ref[...] += lax.dot_general(
            normed, hidden, (((0,), (0,)), ((), ())), preferred_element_type=jnp.float32
        )
        grad_b_ref[...] += jnp.sum(
            hidden.astype(jnp.float32).reshape(cells // SUB, SUB, 512), axis=0
        )
        norm_grad = lax.dot_general(
            hidden, w_in_ref[...], (((1,), (1,)), ((), ())), preferred_element_type=jnp.float32
        )
        grad_gain_ref[...] += jnp.sum((norm_grad * scaled).reshape(-1, SUB, 128), axis=0)
        grad_shift_ref[...] += jnp.sum(norm_grad.reshape(-1, SUB, 128), axis=0)
        weighted = norm_grad * gain
        conv_grad = inverse * (
            weighted
            - jnp.mean(weighted, axis=-1, keepdims=True)
            - scaled * jnp.mean(weighted * scaled, axis=-1, keepdims=True)
        )
        rounded = conv_grad.astype(jnp.bfloat16).astype(jnp.float32).reshape(chunk, SUB, SUB, 128)
        grad_bias_ref[...] += jnp.sum(rounded, axis=(0, 1))
        for r in range(chunk):
            natural = gather_row([rounded[r, t] for t in range(SUB)], og_buf)
            conv_grad_ref[first + r] = natural.astype(jnp.bfloat16)
        return 0

    lax.fori_loop(0, height // chunk, one, 0)
    grad_out_ref[...] = grad_out_t[...].T


def tap_kernel(
    padded_ref, grad_ref, grad_in_ref, grad_out_ref, bias_ref, gain_ref, shift_ref, b_ref,
    out_ref, tiles_ref, buf_ref, sums_ref, small_ref,
):
    height = grad_ref.shape[0]
    spread_rows(padded_ref, tiles_ref, buf_ref, height + KS - 1, SUB + KS - 1)
    sums_ref[...] = jnp.zeros_like(sums_ref)

    def one(row, _):
        buf_ref[0:64, :] = grad_ref[row].astype(jnp.float32)
        grads = [buf_ref[pl.ds(t, SUB, stride=SUB), :] for t in range(SUB)]
        for a in range(KS):
            cells = [tiles_ref[row + a, t] for t in range(SUB + KS - 1)]
            for b in range(KS):
                total = sums_ref[a, b]
                for t in range(SUB):
                    total = total + grads[t] * cells[t + b]
                sums_ref[a, b] = total
        return 0

    lax.fori_loop(0, height, one, 0)
    small_ref[...] = jnp.zeros_like(small_ref)
    for a in range(KS):
        for b in range(KS):
            small_ref[a * KS + b] = jnp.sum(sums_ref[a, b], axis=0)
    for at, ref in enumerate((bias_ref, gain_ref, shift_ref)):
        small_ref[KS * KS + at] = jnp.sum(ref[...], axis=0)
    for q in range(4):
        small_ref[KS * KS + 3 + q] = jnp.sum(b_ref[:, q * 128 : (q + 1) * 128], axis=0)
    parts = out_ref.shape[0]
    rows = 1024 // parts
    each = 128 // rows
    for q in range(4):
        block = grad_in_ref[:, q * 128 : (q + 1) * 128].reshape(each, rows, 128)
        out_ref[q * each : (q + 1) * each, 0:rows, :] = block.astype(jnp.bfloat16)
    block = grad_out_ref[...].reshape(parts // 2, rows, 128)
    out_ref[parts // 2 :, 0:rows, :] = block.astype(jnp.bfloat16)
    tail = small_ref[...].reshape(parts, SMALL // parts, 128)
    spare = out_ref.shape[1] - rows - SMALL // parts
    if spare:
        tail = jnp.concatenate([tail, jnp.zeros((parts, spare, 128), jnp.float32)], axis=1)
    out_ref[:, rows:, :] = tail.astype(jnp.bfloat16)


def fold_kernel(parts_ref, out_ref):
    total = jnp.sum(parts_ref[...].astype(jnp.float32), axis=0).astype(jnp.bfloat16)
    out_ref[...] = jnp.broadcast_to(total[None], out_ref.shape)


def unpack_kernel(factor, all_ref, kernel_ref, bias_ref, gain_ref, shift_ref, in_ref, b_ref, out_ref):
    parts = all_ref.shape[0]
    rows = 1024 // parts
    each = 128 // rows
    for q in range(4):
        block = all_ref[q * each : (q + 1) * each, 0:rows, :].astype(jnp.float32)
        in_ref[:, q * 128 : (q + 1) * 128] = block.reshape(128, 128) * factor
    block = all_ref[parts // 2 :, 0:rows, :].astype(jnp.float32)
    out_ref[...] = block.reshape(512, 128) * factor
    small = all_ref[:, rows:, :].astype(jnp.float32) * factor

    def row(r):
        return small[r // (SMALL // parts), r % (SMALL // parts)]

    for a in range(KS):
        for b in range(KS):
            kernel_ref[a, b] = row(a * KS + b)
    for at, ref in enumerate((bias_ref, gain_ref, shift_ref)):
        ref[0] = row(KS * KS + at)
    for q in range(4):
        b_ref[0, q * 128 : (q + 1) * 128] = row(KS * KS + 3 + q)


def groups():
    count_lon, count_lat = lax.axis_size("lon"), lax.axis_size("lat")
    plane = [[[] for _ in range(count_lat // 2)] for _ in range(2)]
    column = [[[] for _ in range(2)] for _ in range(count_lon // 2)]
    for lon in range(count_lon):
        for lat in range(count_lat):
            at = lon * count_lat + lat
            plane[lon % 2][lat // 2].append(at)
            column[lon // 2][lat % 2].append(at)
    return [g for part in plane for g in part], [g for part in column for g in part]


def exchange(parts, members):
    return lax.all_to_all(parts, ("lon", "lat"), 0, 0, tiled=True, axis_index_groups=members)


def summed(packed):
    plane, column = groups()

    def fold(parts, count):
        return pl.pallas_call(
            fold_kernel,
            out_shape=jax.ShapeDtypeStruct((count,) + parts.shape[1:], jnp.bfloat16),
            in_specs=[VMEM],
            out_specs=VMEM,
            name="fold",
        )(parts)

    held = exchange(packed, plane)
    held = exchange(fold(held, len(column[0])), column)
    return exchange(fold(held, len(plane[0])), plane)


def back_kernel(padded_ref, cot_ref, mask_ref, kernel_ref, out_ref, tiles_ref, buf_ref):
    height = cot_ref.shape[0]
    spread_rows(padded_ref, tiles_ref, buf_ref, height + KS - 1, SUB + KS - 1)

    def one(row, _):
        total = conv_row(tiles_ref, kernel_ref, row, True)
        spread = gather_row(total, buf_ref)
        out_ref[row] = (
            (cot_ref[row].astype(jnp.float32) + spread) * mask_ref[row].astype(jnp.float32)
        ).astype(jnp.bfloat16)
        return 0

    lax.fori_loop(0, height, one, 0)


def shifted(piece, axis, up, periodic):
    count = lax.axis_size(axis)
    pairs = [(i, i + 1) for i in range(count - 1)]
    if periodic:
        pairs.append((count - 1, 0))
    if not up:
        pairs = [(target, source) for source, target in pairs]
    return lax.ppermute(piece, axis, pairs)


def with_halo(block):
    west = shifted(block[:, -HALF:], "lon", True, True)
    east = shifted(block[:, :HALF], "lon", False, True)
    wide = jnp.concatenate([west, block, east], axis=1)
    south = shifted(wide[-HALF:], "lat", True, False)
    north = shifted(wide[:HALF], "lat", False, False)
    return jnp.concatenate([south, wide, north], axis=0)


def f32(*shape):
    return jax.ShapeDtypeStruct(shape, jnp.float32)


def body(cells, ocean_mask, cotangent, kernel, conv_bias, gain, shift, w_in, b_in, w_out, chunk=4):
    height, across, channels = cells.shape
    ocean = jnp.broadcast_to(ocean_mask.astype(jnp.bfloat16)[..., None], cells.shape)
    masked = cells * ocean
    out_grad = cotangent * ocean
    padded = with_halo(masked)
    tall = height + 2 * HALF
    tiles = pltpu.VMEM((tall, SUB + KS - 1, SUB, channels), jnp.float32)
    row_buf = pltpu.VMEM((72, channels), jnp.float32)
    hidden = w_in.shape[1]
    conv_grad, bias8, gain8, shift8, grad_in, b8, grad_out = pl.pallas_call(
        functools.partial(block_kernel, chunk),
        out_shape=(
            jax.ShapeDtypeStruct(cells.shape, jnp.bfloat16),
            f32(SUB, channels), f32(SUB, channels), f32(SUB, channels),
            f32(channels, hidden), f32(SUB, hidden), f32(hidden, channels),
        ),
        in_specs=[VMEM] * 9,
        out_specs=[VMEM] * 7,
        scratch_shapes=[
            tiles, row_buf, row_buf,
            pltpu.VMEM((chunk, SUB, SUB, channels), jnp.float32),
            pltpu.VMEM((chunk, SUB, SUB, channels), jnp.float32),
            pltpu.VMEM((channels, hidden), jnp.float32),
        ],
        name="block",
    )(
        padded, out_grad, kernel, conv_bias.reshape(1, -1), gain.reshape(1, -1), shift.reshape(1, -1),
        w_in, b_in.reshape(1, -1), w_out,
    )
    grad_padded = with_halo(conv_grad)
    parts = lax.axis_size("lon")
    packed = pl.pallas_call(
        tap_kernel,
        out_shape=jax.ShapeDtypeStruct((parts, 1024 // parts + max(8, SMALL // parts), channels), jnp.bfloat16),
        in_specs=[VMEM] * 8,
        out_specs=VMEM,
        scratch_shapes=[
            tiles, row_buf, pltpu.VMEM((KS, KS, SUB, channels), jnp.float32),
            pltpu.VMEM((64, channels), jnp.float32),
        ],
        name="taps",
    )(padded, conv_grad, grad_in, grad_out, bias8, gain8, shift8, b8)
    total = summed(packed)
    cells_grad = pl.pallas_call(
        back_kernel,
        out_shape=jax.ShapeDtypeStruct(cells.shape, jnp.bfloat16),
        in_specs=[VMEM] * 4,
        out_specs=VMEM,
        scratch_shapes=[tiles, row_buf],
        name="back",
    )(grad_padded, cotangent, ocean, kernel)
    count = height * across * lax.axis_size("lon") * lax.axis_size("lat")
    gk, gb, gg, gs, gi, gh, go = pl.pallas_call(
        functools.partial(unpack_kernel, count ** -0.5),
        out_shape=(
            f32(KS, KS, channels), f32(1, channels), f32(1, channels), f32(1, channels),
            f32(channels, hidden), f32(1, hidden), f32(hidden, channels),
        ),
        in_specs=[VMEM],
        out_specs=[VMEM] * 7,
        name="unpack",
    )(total)
    return cells_grad, gk, gb[0], gg[0], gs[0], gi, gh[0], go


def solution(mesh):
    whole = P("lat", "lon", None)
    in_specs = (whole, P("lat", "lon"), whole) + (P(),) * 7
    out_specs = (whole,) + (P(),) * 7
    return jax.shard_map(body, mesh=mesh, in_specs=in_specs, out_specs=out_specs, check_vma=False)
```

```python
import functools

import jax
import jax.numpy as jnp
from jax import lax
from jax.experimental import pallas as pl
from jax.experimental.pallas import tpu as pltpu
from jax.sharding import PartitionSpec as P

KS = 7
HALF = 3
SMALL = 64
WIDE = 14
SUB = 8
ROOT = 0.7978845608028654
CUBE = 0.044715
VMEM = pl.BlockSpec(memory_space=pltpu.VMEM)
PARAMS = pltpu.CompilerParams(vmem_limit_bytes=28 << 20)
SMEM = pl.BlockSpec(memory_space=pltpu.SMEM)


def spread_row(row_of, row, tiles_ref, buf_ref):
    buf_ref[HALF : HALF + 64, :] = row_of.astype(jnp.float32)
    for tap in range(WIDE):
        tiles_ref[pl.ds(row * (WIDE * SUB) + tap * SUB, SUB), :] = buf_ref[pl.ds(tap, SUB, stride=SUB), :]


def spread_all(south_ref, block_ref, north_ref, tiles_ref, buf_ref):
    height = block_ref.shape[0]
    buf_ref[...] = jnp.zeros_like(buf_ref)
    for row in range(HALF):
        spread_row(south_ref[row], row, tiles_ref, buf_ref)
        spread_row(north_ref[row], height + HALF + row, tiles_ref, buf_ref)

    def one(row, _):
        spread_row(block_ref[row], row + HALF, tiles_ref, buf_ref)
        return 0

    lax.fori_loop(0, height, one, 0)
    last = (height + 2 * HALF) * WIDE * SUB
    tiles_ref[last:, :] = jnp.zeros((2 * WIDE * SUB, 128), jnp.float32)


def tile(tiles_ref, row, t):
    return tiles_ref[pl.ds(row * (WIDE * SUB) + t * SUB, SUB), :]


def tap_weight(kernel_ref, a, b, flip):
    if flip:
        a, b = KS - 1 - a, KS - 1 - b
    return jnp.broadcast_to(kernel_ref[a, b : b + 1, :], (SUB, 128))


def conv_rows(tiles_ref, kernel_ref, out_ref, height, flip):
    def one(row, _):
        total = [None] * SUB
        for a in range(KS):
            cells = [tile(tiles_ref, row + a, t) for t in range(WIDE)]
            for b in range(KS):
                weight = tap_weight(kernel_ref, a, b, flip)
                for t in range(SUB):
                    term = weight * cells[t + b]
                    total[t] = term if total[t] is None else total[t] + term
        for t in range(SUB):
            out_ref[pl.ds(row * 64 + t * SUB, SUB), :] = total[t]
        return 0

    lax.fori_loop(0, height, one, 0)


def edge_columns(even, keep_ref, got_ref, cols_ref):
    for c in range(HALF):
        keep = keep_ref[c].astype(jnp.float32)
        got = got_ref[c].astype(jnp.float32)
        cols_ref[c] = jnp.where(even, got, keep)
        cols_ref[HALF + c] = jnp.where(even, keep, got)


def add_edges(cols_ref, kernel_ref, out_ref, height, flip):
    for west in (True, False):
        for at in range(HALF):
            t = at if west else SUB - HALF + at
            totals = [None] * (height // SUB)
            for a in range(KS):
                for b in range(KS):
                    c = t + b if west else t + b - SUB
                    if not ((0 <= c < HALF) if west else (HALF <= c < 2 * HALF)):
                        continue
                    weight = tap_weight(kernel_ref, a, b, flip)
                    for block in range(height // SUB):
                        term = weight * cols_ref[c, pl.ds(block * SUB + a, SUB), :]
                        totals[block] = term if totals[block] is None else totals[block] + term
            for block in range(height // SUB):
                place = pl.ds(block * SUB * 64 + t * SUB + (0 if west else SUB - 1), SUB, stride=64)
                out_ref[place, :] = out_ref[place, :] + totals[block]


def gather_row(tiles, buf_ref):
    for t in range(SUB):
        buf_ref[pl.ds(t, SUB, stride=SUB), :] = tiles[t]
    return buf_ref[0 : SUB * SUB, :]


def strip_kernel(even_ref, south_ref, block_ref, north_ref, out_ref, low_ref, high_ref):
    height = block_ref.shape[0]

    def put(at, row_of):
        low_ref[pl.ds(at * SUB, SUB), :] = row_of[0:SUB].astype(jnp.float32)
        high_ref[pl.ds(at * SUB, SUB), :] = row_of[64 - SUB : 64].astype(jnp.float32)

    for row in range(HALF):
        put(row, south_ref[row])
        put(row + height + HALF, north_ref[row])

    def one(step, _):
        for r in range(SUB):
            put(step * SUB + r + HALF, block_ref[step * SUB + r])
        return 0

    lax.fori_loop(0, height // SUB, one, 0)
    tall = height + 2 * HALF + 2
    low_ref[(tall - 2) * SUB :, :] = jnp.zeros((2 * SUB, 128), jnp.float32)
    high_ref[(tall - 2) * SUB :, :] = jnp.zeros((2 * SUB, 128), jnp.float32)
    even = even_ref[0] == 1
    for c in range(HALF):
        west = low_ref[pl.ds(c, tall, stride=SUB), :]
        east = high_ref[pl.ds(SUB - HALF + c, tall, stride=SUB), :]
        out_ref[0, c] = jnp.where(even, east, west).astype(jnp.bfloat16)
        out_ref[1, c] = jnp.where(even, west, east).astype(jnp.bfloat16)


def conv_kernel(flip, keep_tiles, south_ref, block_ref, north_ref, kernel_ref, out_ref, tiles_ref, buf_ref):
    del keep_tiles
    spread_all(south_ref, block_ref, north_ref, tiles_ref, buf_ref)
    conv_rows(tiles_ref, kernel_ref, out_ref, block_ref.shape[0], flip)


def block_kernel(
    chunk,
    even_ref, conv_in, tiles_in, keep_ref, got_ref, out_grad_ref,
    kernel_ref, bias_ref, gain_ref, shift_ref, w_in_ref, b_in_ref, w_out_ref,
    conv_ref, tiles_ref, conv_grad_ref, packed_ref,
    cols_ref, buf_ref, og_tiles, round_ref, taps_ref, small_ref,
    bias_sum, gain_sum, shift_sum, b_sum, grad_in, grad_out,
):
    del conv_in, tiles_in
    height = out_grad_ref.shape[0]
    cells = chunk * 64
    edge_columns(even_ref[0] == 1, keep_ref, got_ref, cols_ref)
    span = WIDE * SUB
    for c in range(HALF):
        for block in range((height + 2 * HALF + 2) // SUB):
            rows = pl.ds(block * SUB, SUB)
            start = block * SUB * span
            tiles_ref[pl.ds(start + c * SUB, SUB, stride=span), :] = cols_ref[c, rows, :]
            tiles_ref[pl.ds(start + (SUB + HALF + c) * SUB + SUB - 1, SUB, stride=span), :] = cols_ref[HALF + c, rows, :]
    add_edges(cols_ref, kernel_ref, conv_ref, height, False)
    for ref in (bias_sum, gain_sum, shift_sum, b_sum, grad_in, grad_out, taps_ref, round_ref):
        ref[...] = jnp.zeros_like(ref)
    bias = bias_ref[...]
    gain = gain_ref[...]
    shift = shift_ref[...]
    b_in = b_in_ref[...]

    def taps(first):
        for r in range(chunk):
            row = first + r
            grads = [round_ref[r * 64 + t * SUB : r * 64 + (t + 1) * SUB, :] for t in range(SUB)]
            for a in range(KS):
                near = [tile(tiles_ref, row + a, t) for t in range(WIDE)]
                for b in range(KS):
                    total = taps_ref[a, b]
                    for t in range(SUB):
                        total = total + grads[t] * near[t + b]
                    taps_ref[a, b] = total

    def one(step, _):
        first = step * chunk
        taps(jnp.maximum(first - chunk, 0))
        for r in range(chunk):
            buf_ref[0:64, :] = out_grad_ref[first + r].astype(jnp.float32)
            for t in range(SUB):
                og_tiles[r, t] = buf_ref[pl.ds(t, SUB, stride=SUB), :]
        conv = conv_ref[pl.ds(first * 64, cells), :] + bias
        out_grad = og_tiles[...].reshape(cells, 128).astype(jnp.bfloat16)
        average = jnp.mean(conv, axis=-1, keepdims=True)
        centred = conv - average
        variance = jnp.mean(centred * centred, axis=-1, keepdims=True)
        inverse = lax.rsqrt(variance + 1e-06)
        scaled = centred * inverse
        normed = (scaled * gain + shift).astype(jnp.bfloat16)
        v = jnp.dot(normed, w_in_ref[...], preferred_element_type=jnp.float32) + b_in
        act_grad = lax.dot_general(
            out_grad, w_out_ref[...], (((1,), (1,)), ((), ())), preferred_element_type=jnp.float32
        )
        square = v * v
        half = 0.5 + 0.5 * jnp.tanh(v * (ROOT + (ROOT * CUBE) * square))
        activation = (v * half).astype(jnp.bfloat16)
        slope = half + (half - half * half) * (v * (2 * ROOT + (6 * ROOT * CUBE) * square))
        hidden = (act_grad * slope).astype(jnp.bfloat16)
        grad_out[...] += lax.dot_general(
            out_grad, activation, (((0,), (0,)), ((), ())), preferred_element_type=jnp.float32
        )
        grad_in[...] += lax.dot_general(
            normed, hidden, (((0,), (0,)), ((), ())), preferred_element_type=jnp.float32
        )
        b_sum[...] += jnp.sum(hidden.astype(jnp.float32).reshape(cells // SUB, SUB, 512), axis=0)
        norm_grad = lax.dot_general(
            hidden, w_in_ref[...], (((1,), (1,)), ((), ())), preferred_element_type=jnp.float32
        )
        gain_sum[...] += jnp.sum((norm_grad * scaled).reshape(-1, SUB, 128), axis=0)
        shift_sum[...] += jnp.sum(norm_grad.reshape(-1, SUB, 128), axis=0)
        weighted = norm_grad * gain
        conv_grad = inverse * (
            weighted
            - jnp.mean(weighted, axis=-1, keepdims=True)
            - scaled * jnp.mean(weighted * scaled, axis=-1, keepdims=True)
        )
        rounded = conv_grad.astype(jnp.bfloat16).astype(jnp.float32)
        bias_sum[...] += jnp.sum(rounded.reshape(-1, SUB, 128), axis=0)
        round_ref[...] = rounded
        for r in range(chunk):
            natural = gather_row(
                [rounded[r * 64 + t * SUB : r * 64 + (t + 1) * SUB] for t in range(SUB)], buf_ref
            )
            conv_grad_ref[first + r] = natural.astype(jnp.bfloat16)
        return 0

    lax.fori_loop(0, height // chunk, one, 0)
    taps(height - chunk)
    pack(taps_ref, bias_sum, gain_sum, shift_sum, b_sum, grad_in, grad_out, packed_ref, small_ref)


def pack(taps_ref, bias_sum, gain_sum, shift_sum, b_sum, grad_in, grad_out, out_ref, small_ref):
    small_ref[...] = jnp.zeros_like(small_ref)
    for a in range(KS):
        for b in range(KS):
            small_ref[a * KS + b] = jnp.sum(taps_ref[a, b], axis=0)
    for at, ref in enumerate((bias_sum, gain_sum, shift_sum)):
        small_ref[KS * KS + at] = jnp.sum(ref[...], axis=0)
    for q in range(4):
        small_ref[KS * KS + 3 + q] = jnp.sum(b_sum[:, q * 128 : (q + 1) * 128], axis=0)
    parts = out_ref.shape[0]
    rows = 1024 // parts
    each = 128 // rows
    for at, ref in ((0, grad_in), (4, grad_out)):
        for q in range(4):
            block = ref[:, q * 128 : (q + 1) * 128].reshape(each, rows, 128)
            out_ref[(at + q) * each : (at + q + 1) * each, 0:rows, :] = block.astype(jnp.bfloat16)
    tail = small_ref[...].reshape(parts, SMALL // parts, 128)
    spare = out_ref.shape[1] - rows - SMALL // parts
    if spare:
        tail = jnp.concatenate([tail, jnp.zeros((parts, spare, 128), jnp.float32)], axis=1)
    out_ref[:, rows:, :] = tail.astype(jnp.bfloat16)


def back_kernel(even_ref, spread_in, keep_ref, got_ref, cot_ref, mask_ref, kernel_ref, spread_ref, out_ref, cols_ref, buf_ref):
    del spread_in
    height = cot_ref.shape[0]
    edge_columns(even_ref[0] == 1, keep_ref, got_ref, cols_ref)
    add_edges(cols_ref, kernel_ref, spread_ref, height, True)

    def one(row, _):
        spread = gather_row([spread_ref[pl.ds(row * 64 + t * SUB, SUB), :] for t in range(SUB)], buf_ref)
        out_ref[row] = (
            (cot_ref[row].astype(jnp.float32) + spread) * mask_ref[row].astype(jnp.float32)
        ).astype(jnp.bfloat16)
        return 0

    lax.fori_loop(0, height, one, 0)


def fold_kernel(parts_ref, out_ref):
    total = jnp.sum(parts_ref[...].astype(jnp.float32), axis=0).astype(jnp.bfloat16)
    out_ref[...] = jnp.broadcast_to(total[None], out_ref.shape)


def unpack_kernel(factor, all_ref, kernel_ref, bias_ref, gain_ref, shift_ref, in_ref, b_ref, out_ref):
    parts = all_ref.shape[0]
    rows = 1024 // parts
    each = 128 // rows
    for q in range(4):
        block = all_ref[q * each : (q + 1) * each, 0:rows, :].astype(jnp.float32)
        in_ref[:, q * 128 : (q + 1) * 128] = block.reshape(128, 128) * factor
    for q in range(4):
        block = all_ref[(4 + q) * each : (5 + q) * each, 0:rows, :].astype(jnp.float32)
        out_ref[q * 128 : (q + 1) * 128, :] = block.reshape(128, 128).T * factor
    small = all_ref[:, rows:, :].astype(jnp.float32) * factor

    def row(r):
        return small[r // (SMALL // parts), r % (SMALL // parts)]

    for a in range(KS):
        for b in range(KS):
            kernel_ref[a, b] = row(a * KS + b)
    for at, ref in enumerate((bias_ref, gain_ref, shift_ref)):
        ref[0] = row(KS * KS + at)
    for q in range(4):
        b_ref[0, q * 128 : (q + 1) * 128] = row(KS * KS + 3 + q)


def groups():
    count_lon, count_lat = lax.axis_size("lon"), lax.axis_size("lat")
    plane = [[[] for _ in range(count_lat // 2)] for _ in range(2)]
    column = [[[] for _ in range(2)] for _ in range(count_lon // 2)]
    for lon in range(count_lon):
        for lat in range(count_lat):
            at = lon * count_lat + lat
            plane[lon % 2][lat // 2].append(at)
            column[lon // 2][lat % 2].append(at)
    return [g for part in plane for g in part], [g for part in column for g in part]


def exchange(parts, members):
    return lax.all_to_all(parts, ("lon", "lat"), 0, 0, tiled=True, axis_index_groups=members)


def summed(packed):
    plane, column = groups()

    def fold(parts, count):
        return pl.pallas_call(
            fold_kernel,
            out_shape=jax.ShapeDtypeStruct((count,) + parts.shape[1:], jnp.bfloat16),
            in_specs=[VMEM],
            out_specs=VMEM,
            name="fold",
        compiler_params=PARAMS,
        )(parts)

    held = exchange(packed, plane)
    held = exchange(fold(held, len(column[0])), column)
    return exchange(fold(held, len(plane[0])), plane)


def lat_halo(block):
    count = lax.axis_size("lat")
    up = [(i, i + 1) for i in range(count - 1)]
    down = [(i + 1, i) for i in range(count - 1)]
    return lax.ppermute(block[-HALF:], "lat", up), lax.ppermute(block[:HALF], "lat", down)


def lon_halo(even, south, block, north):
    count = lax.axis_size("lon")
    tall = block.shape[0] + 2 * HALF + 2
    strips = pl.pallas_call(
        strip_kernel,
        out_shape=jax.ShapeDtypeStruct((2, HALF, tall, 128), jnp.bfloat16),
        in_specs=[SMEM, VMEM, VMEM, VMEM],
        out_specs=VMEM,
        scratch_shapes=[pltpu.VMEM((tall * SUB, 128), jnp.float32)] * 2,
        name="strips",
        compiler_params=PARAMS,
    )(even, south, block, north)
    swapped = lax.ppermute(strips, "lon", [(i, i ^ 1) for i in range(count)])
    onward = [(i, (i + 2) % count) for i in range(0, count, 2)] + [(i, (i - 2) % count) for i in range(1, count, 2)]
    return swapped[0], lax.ppermute(swapped[1], "lon", onward)


def first_conv(flip, south, block, north, kernel, keep_tiles):
    height, across, channels = block.shape
    tiles = (height + 2 * HALF + 2) * WIDE * SUB
    out = (pltpu.VMEM((height * across, channels), jnp.float32),)
    scratch = [pltpu.VMEM((SUB * SUB + 2 * SUB, channels), jnp.float32)]
    if keep_tiles:
        out = out + (pltpu.VMEM((tiles, channels), jnp.float32),)
    else:
        scratch = [pltpu.VMEM((tiles, channels), jnp.float32)] + scratch
    return pl.pallas_call(
        functools.partial(conv_kernel, flip, keep_tiles),
        out_shape=out,
        in_specs=[VMEM] * 4,
        out_specs=[VMEM] * len(out),
        scratch_shapes=scratch,
        name="back_conv" if flip else "conv",
        compiler_params=PARAMS,
    )(south, block, north, kernel)


def f32(*shape):
    return jax.ShapeDtypeStruct(shape, jnp.float32)


def body(cells, ocean_mask, cotangent, kernel, conv_bias, gain, shift, w_in, b_in, w_out, chunk=4):
    height, across, channels = cells.shape
    ocean = jnp.broadcast_to(ocean_mask.astype(jnp.bfloat16)[..., None], cells.shape)
    masked = cells * ocean
    out_grad = cotangent * ocean
    even = (1 - lax.axis_index("lon") % 2).astype(jnp.int32).reshape(1)
    south, north = lat_halo(masked)
    keep, got = lon_halo(even, south, masked, north)
    conv, tiles = first_conv(False, south, masked, north, kernel, True)
    parts = lax.axis_size("lon")
    hidden = w_in.shape[1]
    _, _, conv_grad, packed = pl.pallas_call(
        functools.partial(block_kernel, chunk),
        out_shape=(
            pltpu.VMEM(conv.shape, jnp.float32), pltpu.VMEM(tiles.shape, jnp.float32),
            jax.ShapeDtypeStruct(cells.shape, jnp.bfloat16),
            jax.ShapeDtypeStruct((parts, 1024 // parts + max(8, SMALL // parts), channels), jnp.bfloat16),
        ),
        in_specs=[SMEM] + [VMEM] * 12,
        out_specs=[VMEM] * 4,
        scratch_shapes=[
            pltpu.VMEM((2 * HALF, height + 2 * HALF + 2, channels), jnp.float32),
            pltpu.VMEM((80, channels), jnp.float32),
            pltpu.VMEM((chunk, SUB, SUB, channels), jnp.float32),
            pltpu.VMEM((chunk * 64, channels), jnp.float32),
            pltpu.VMEM((KS, KS, SUB, channels), jnp.float32),
            pltpu.VMEM((SMALL, channels), jnp.float32),
            pltpu.VMEM((SUB, channels), jnp.float32),
            pltpu.VMEM((SUB, channels), jnp.float32),
            pltpu.VMEM((SUB, channels), jnp.float32),
            pltpu.VMEM((SUB, hidden), jnp.float32),
            pltpu.VMEM((channels, hidden), jnp.float32),
            pltpu.VMEM((channels, hidden), jnp.float32),
        ],
        input_output_aliases={1: 0, 2: 1},
        name="block",
        compiler_params=PARAMS,
    )(
        even, *[pltpu.with_memory_space_constraint(x, pltpu.VMEM) for x in (conv, tiles)], keep, got, out_grad, kernel, conv_bias.reshape(1, -1), gain.reshape(1, -1),
        shift.reshape(1, -1), w_in, b_in.reshape(1, -1), w_out,
    )
    total = summed(packed)
    south, north = lat_halo(conv_grad)
    keep, got = lon_halo(even, south, conv_grad, north)
    (spread,) = first_conv(True, south, conv_grad, north, kernel, False)
    _, cells_grad = pl.pallas_call(
        back_kernel,
        out_shape=(pltpu.VMEM(spread.shape, jnp.float32), jax.ShapeDtypeStruct(cells.shape, jnp.bfloat16)),
        in_specs=[SMEM] + [VMEM] * 6,
        out_specs=[VMEM] * 2,
        scratch_shapes=[
            pltpu.VMEM((2 * HALF, height + 2 * HALF + 2, channels), jnp.float32),
            pltpu.VMEM((80, channels), jnp.float32),
        ],
        input_output_aliases={1: 0},
        name="back",
        compiler_params=PARAMS,
    )(even, pltpu.with_memory_space_constraint(spread, pltpu.VMEM), keep, got, cotangent, ocean, kernel)
    count = height * across * lax.axis_size("lon") * lax.axis_size("lat")
    gk, gb, gg, gs, gi, gh, go = pl.pallas_call(
        functools.partial(unpack_kernel, count ** -0.5),
        out_shape=(
            f32(KS, KS, channels), f32(1, channels), f32(1, channels), f32(1, channels),
            f32(channels, hidden), f32(1, hidden), f32(hidden, channels),
        ),
        in_specs=[VMEM],
        out_specs=[VMEM] * 7,
        name="unpack",
        compiler_params=PARAMS,
    )(total)
    return cells_grad, gk, gb[0], gg[0], gs[0], gi, gh[0], go


def solution(mesh):
    whole = P("lat", "lon", None)
    in_specs = (whole, P("lat", "lon"), whole) + (P(),) * 7
    out_specs = (whole,) + (P(),) * 7
    return jax.shard_map(body, mesh=mesh, in_specs=in_specs, out_specs=out_specs, check_vma=False)
```

```python
import functools

import jax
import jax.numpy as jnp
from jax import lax
from jax.experimental import pallas as pl
from jax.experimental.pallas import tpu as pltpu
from jax.sharding import PartitionSpec as P


KS = 7
HALF = 3
SMALL = 64
WIDE = 14
SUB = 8
ROOT = 0.7978845608028654
CUBE = 0.044715
VMEM = pl.BlockSpec(memory_space=pltpu.VMEM)
PARAMS = pltpu.CompilerParams(vmem_limit_bytes=28 << 20)
SMEM = pl.BlockSpec(memory_space=pltpu.SMEM)


def spread_row(row_of, row, tiles_ref, buf_ref):
    buf_ref[HALF : HALF + 64, :] = row_of.astype(jnp.float32)
    for tap in range(WIDE):
        tiles_ref[pl.ds(row * (WIDE * SUB) + tap * SUB, SUB), :] = buf_ref[pl.ds(tap, SUB, stride=SUB), :]


def spread_all(south_ref, block_ref, north_ref, tiles_ref, buf_ref):
    height = block_ref.shape[0]
    buf_ref[...] = jnp.zeros_like(buf_ref)
    for row in range(HALF):
        spread_row(south_ref[row], row, tiles_ref, buf_ref)
        spread_row(north_ref[row], height + HALF + row, tiles_ref, buf_ref)

    def one(row, _):
        spread_row(block_ref[row], row + HALF, tiles_ref, buf_ref)
        return 0

    lax.fori_loop(0, height, one, 0)
    last = (height + 2 * HALF) * WIDE * SUB
    tiles_ref[last:, :] = jnp.zeros((2 * WIDE * SUB, 128), jnp.float32)


def tile(tiles_ref, row, t):
    return tiles_ref[pl.ds(row * (WIDE * SUB) + t * SUB, SUB), :]


def tap_weight(kernel_ref, a, b, flip):
    if flip:
        a, b = KS - 1 - a, KS - 1 - b
    return jnp.broadcast_to(kernel_ref[a, b : b + 1, :], (SUB, 128))


def conv_rows(tiles_ref, kernel_ref, out_ref, height, flip):
    def one(row, _):
        total = [None] * SUB
        for a in range(KS):
            cells = [tile(tiles_ref, row + a, t) for t in range(WIDE)]
            for b in range(KS):
                weight = tap_weight(kernel_ref, a, b, flip)
                for t in range(SUB):
                    term = weight * cells[t + b]
                    total[t] = term if total[t] is None else total[t] + term
        for t in range(SUB):
            out_ref[pl.ds(row * 64 + t * SUB, SUB), :] = total[t]
        return 0

    lax.fori_loop(0, height, one, 0)


def edge_columns(even, keep_ref, got_ref, cols_ref):
    for c in range(HALF):
        keep = keep_ref[c].astype(jnp.float32)
        got = got_ref[c].astype(jnp.float32)
        cols_ref[c] = jnp.where(even, got, keep)
        cols_ref[HALF + c] = jnp.where(even, keep, got)


def add_edges(cols_ref, kernel_ref, out_ref, height, flip):
    for west in (True, False):
        for at in range(HALF):
            t = at if west else SUB - HALF + at
            totals = [None] * (height // SUB)
            for a in range(KS):
                for b in range(KS):
                    c = t + b if west else t + b - SUB
                    if not ((0 <= c < HALF) if west else (HALF <= c < 2 * HALF)):
                        continue
                    weight = tap_weight(kernel_ref, a, b, flip)
                    for block in range(height // SUB):
                        term = weight * cols_ref[c, pl.ds(block * SUB + a, SUB), :]
                        totals[block] = term if totals[block] is None else totals[block] + term
            for block in range(height // SUB):
                place = pl.ds(block * SUB * 64 + t * SUB + (0 if west else SUB - 1), SUB, stride=64)
                out_ref[place, :] = out_ref[place, :] + totals[block]


def gather_row(tiles, buf_ref):
    for t in range(SUB):
        buf_ref[pl.ds(t, SUB, stride=SUB), :] = tiles[t]
    return buf_ref[0 : SUB * SUB, :]


def strip_kernel(even_ref, south_ref, block_ref, north_ref, out_ref, low_ref, high_ref):
    height = block_ref.shape[0]

    def put(at, row_of):
        low_ref[pl.ds(at * SUB, SUB), :] = row_of[0:SUB].astype(jnp.float32)
        high_ref[pl.ds(at * SUB, SUB), :] = row_of[64 - SUB : 64].astype(jnp.float32)

    for row in range(HALF):
        put(row, south_ref[row])
        put(row + height + HALF, north_ref[row])

    def one(step, _):
        for r in range(SUB):
            put(step * SUB + r + HALF, block_ref[step * SUB + r])
        return 0

    lax.fori_loop(0, height // SUB, one, 0)
    tall = height + 2 * HALF + 2
    low_ref[(tall - 2) * SUB :, :] = jnp.zeros((2 * SUB, 128), jnp.float32)
    high_ref[(tall - 2) * SUB :, :] = jnp.zeros((2 * SUB, 128), jnp.float32)
    even = even_ref[0] == 1
    for c in range(HALF):
        west = low_ref[pl.ds(c, tall, stride=SUB), :]
        east = high_ref[pl.ds(SUB - HALF + c, tall, stride=SUB), :]
        out_ref[0, c] = jnp.where(even, east, west).astype(jnp.bfloat16)
        out_ref[1, c] = jnp.where(even, west, east).astype(jnp.bfloat16)


def conv_kernel(flip, keep_tiles, south_ref, block_ref, north_ref, kernel_ref, out_ref, tiles_ref, buf_ref):
    del keep_tiles
    spread_all(south_ref, block_ref, north_ref, tiles_ref, buf_ref)
    conv_rows(tiles_ref, kernel_ref, out_ref, block_ref.shape[0], flip)


def block_kernel(
    chunk,
    even_ref, conv_in, tiles_in, keep_ref, got_ref, out_grad_ref,
    kernel_ref, bias_ref, gain_ref, shift_ref, w_in_ref, b_in_ref, w_out_ref,
    conv_ref, tiles_ref, conv_grad_ref, packed_ref,
    cols_ref, buf_ref, og_tiles, round_ref, taps_ref, small_ref,
    bias_sum, gain_sum, shift_sum, grad_in, grad_out,
):
    del conv_in, tiles_in
    height = out_grad_ref.shape[0]
    cells = chunk * 64
    edge_columns(even_ref[0] == 1, keep_ref, got_ref, cols_ref)
    span = WIDE * SUB
    for c in range(HALF):
        for block in range((height + 2 * HALF + 2) // SUB):
            rows = pl.ds(block * SUB, SUB)
            start = block * SUB * span
            tiles_ref[pl.ds(start + c * SUB, SUB, stride=span), :] = cols_ref[c, rows, :]
            tiles_ref[pl.ds(start + (SUB + HALF + c) * SUB + SUB - 1, SUB, stride=span), :] = cols_ref[HALF + c, rows, :]
    add_edges(cols_ref, kernel_ref, conv_ref, height, False)
    for ref in (bias_sum, gain_sum, shift_sum, grad_in, grad_out, taps_ref):
        ref[...] = jnp.zeros_like(ref)
    bias = bias_ref[...]
    gain = gain_ref[...]
    shift = shift_ref[...]
    b_in = b_in_ref[...]
    w_half = w_out_ref[...] * jnp.bfloat16(0.5)

    ones = jnp.where(
        lax.broadcasted_iota(jnp.int32, (16, cells), 0) == 0, 1.0, 0.0
    ).astype(jnp.bfloat16)

    def taps(first):
        for r in range(chunk):
            row = first + r
            grads = [round_ref[r * 64 + t * SUB : r * 64 + (t + 1) * SUB, :] for t in range(SUB)]
            for a in range(KS):
                near = [tile(tiles_ref, row + a, t) for t in range(WIDE)]
                for b in range(KS):
                    total = taps_ref[a, b]
                    for t in range(SUB):
                        total = total + grads[t] * near[t + b]
                    taps_ref[a, b] = total

    def one(step, pending):
        first = step * chunk
        if pending is not None:
            taps(first - chunk)
        for r in range(chunk):
            buf_ref[0:64, :] = out_grad_ref[first + r].astype(jnp.float32)
            for t in range(SUB):
                og_tiles[r, t] = buf_ref[pl.ds(t, SUB, stride=SUB), :]
        conv = conv_ref[pl.ds(first * 64, cells), :] + bias
        out_grad = og_tiles[...].reshape(cells, 128).astype(jnp.bfloat16)
        average = jnp.mean(conv, axis=-1, keepdims=True)
        centred = conv - average
        variance = jnp.mean(centred * centred, axis=-1, keepdims=True)
        inverse = lax.rsqrt(variance + 1e-06)
        scaled = centred * inverse
        normed = (scaled * gain + shift).astype(jnp.bfloat16)
        v = jnp.dot(normed, w_in_ref[...], preferred_element_type=jnp.float32) + b_in
        act_grad = lax.dot_general(
            out_grad, w_half, (((1,), (1,)), ((), ())), preferred_element_type=jnp.float32
        )
        square = v * v
        curve = jnp.tanh(v * (ROOT + (ROOT * CUBE) * square))
        above = 1.0 + curve
        twice = (v * above).astype(jnp.bfloat16)
        rise = v * (ROOT + (3 * ROOT * CUBE) * square)
        hidden = (act_grad * (above * (1.0 + (1.0 - curve) * rise))).astype(jnp.bfloat16)
        grad_out[...] += lax.dot_general(
            out_grad, twice, (((0,), (0,)), ((), ())), preferred_element_type=jnp.float32
        )
        grad_in[...] += jnp.dot(
            jnp.concatenate([normed.T, ones], axis=0), hidden, preferred_element_type=jnp.float32
        )
        norm_grad = lax.dot_general(
            hidden, w_in_ref[...], (((1,), (1,)), ((), ())), preferred_element_type=jnp.float32
        )
        gain_sum[...] += jnp.sum((norm_grad * scaled).reshape(-1, SUB, 128), axis=0)
        shift_sum[...] += jnp.sum(norm_grad.reshape(-1, SUB, 128), axis=0)
        weighted = norm_grad * gain
        conv_grad = inverse * (
            weighted
            - jnp.mean(weighted, axis=-1, keepdims=True)
            - scaled * jnp.mean(weighted * scaled, axis=-1, keepdims=True)
        )
        rounded = conv_grad.astype(jnp.bfloat16).astype(jnp.float32)
        bias_sum[...] += jnp.sum(rounded.reshape(-1, SUB, 128), axis=0)
        round_ref[...] = rounded
        for r in range(chunk):
            natural = gather_row(
                [rounded[r * 64 + t * SUB : r * 64 + (t + 1) * SUB] for t in range(SUB)], buf_ref
            )
            conv_grad_ref[first + r] = natural.astype(jnp.bfloat16)
        return 0

    one(0, None)
    lax.fori_loop(1, height // chunk, one, 0)
    taps(height - chunk)
    pack(taps_ref, bias_sum, gain_sum, shift_sum, grad_in, grad_out, packed_ref, small_ref)


def pack(taps_ref, bias_sum, gain_sum, shift_sum, grad_in, grad_out, out_ref, small_ref):
    small_ref[...] = jnp.zeros_like(small_ref)
    for a in range(KS):
        for b in range(KS):
            small_ref[a * KS + b] = jnp.sum(taps_ref[a, b], axis=0)
    for at, ref in enumerate((bias_sum, gain_sum, shift_sum)):
        small_ref[KS * KS + at] = jnp.sum(ref[...], axis=0)
    for q in range(4):
        small_ref[KS * KS + 3 + q] = grad_in[128, q * 128 : (q + 1) * 128]
    parts = out_ref.shape[0]
    rows = 1024 // parts
    each = 128 // rows
    for at, ref, scale in ((0, grad_in, 1.0), (4, grad_out, 0.5)):
        for q in range(4):
            block = ref[0:128, q * 128 : (q + 1) * 128].reshape(each, rows, 128)
            out_ref[(at + q) * each : (at + q + 1) * each, 0:rows, :] = (block * scale).astype(jnp.bfloat16)
    tail = small_ref[...].reshape(parts, SMALL // parts, 128)
    spare = out_ref.shape[1] - rows - SMALL // parts
    if spare:
        tail = jnp.concatenate([tail, jnp.zeros((parts, spare, 128), jnp.float32)], axis=1)
    out_ref[:, rows:, :] = tail.astype(jnp.bfloat16)


def back_kernel(even_ref, spread_in, keep_ref, got_ref, cot_ref, mask_ref, kernel_ref, spread_ref, out_ref, cols_ref, buf_ref):
    del spread_in
    height = cot_ref.shape[0]
    edge_columns(even_ref[0] == 1, keep_ref, got_ref, cols_ref)
    add_edges(cols_ref, kernel_ref, spread_ref, height, True)

    def one(row, _):
        spread = gather_row([spread_ref[pl.ds(row * 64 + t * SUB, SUB), :] for t in range(SUB)], buf_ref)
        out_ref[row] = (
            (cot_ref[row].astype(jnp.float32) + spread) * mask_ref[row].astype(jnp.float32)
        ).astype(jnp.bfloat16)
        return 0

    lax.fori_loop(0, height, one, 0)


def fold_kernel(parts_ref, out_ref):
    total = jnp.sum(parts_ref[...].astype(jnp.float32), axis=0).astype(jnp.bfloat16)
    out_ref[...] = jnp.broadcast_to(total[None], out_ref.shape)


def unpack_kernel(factor, all_ref, kernel_ref, bias_ref, gain_ref, shift_ref, in_ref, b_ref, out_ref):
    parts = all_ref.shape[0]
    rows = 1024 // parts
    each = 128 // rows
    for q in range(4):
        block = all_ref[q * each : (q + 1) * each, 0:rows, :].astype(jnp.float32)
        in_ref[:, q * 128 : (q + 1) * 128] = block.reshape(128, 128) * factor
    for q in range(4):
        block = all_ref[(4 + q) * each : (5 + q) * each, 0:rows, :].astype(jnp.float32)
        out_ref[q * 128 : (q + 1) * 128, :] = block.reshape(128, 128).T * factor
    small = all_ref[:, rows:, :].astype(jnp.float32) * factor

    def row(r):
        return small[r // (SMALL // parts), r % (SMALL // parts)]

    for a in range(KS):
        for b in range(KS):
            kernel_ref[a, b] = row(a * KS + b)
    for at, ref in enumerate((bias_ref, gain_ref, shift_ref)):
        ref[0] = row(KS * KS + at)
    for q in range(4):
        b_ref[0, q * 128 : (q + 1) * 128] = row(KS * KS + 3 + q)


def groups():
    count_lon, count_lat = lax.axis_size("lon"), lax.axis_size("lat")
    plane = [[[] for _ in range(count_lat // 2)] for _ in range(2)]
    column = [[[] for _ in range(2)] for _ in range(count_lon // 2)]
    for lon in range(count_lon):
        for lat in range(count_lat):
            at = lon * count_lat + lat
            plane[lon % 2][lat // 2].append(at)
            column[lon // 2][lat % 2].append(at)
    return [g for part in plane for g in part], [g for part in column for g in part]


def exchange(parts, members):
    return lax.all_to_all(parts, ("lon", "lat"), 0, 0, tiled=True, axis_index_groups=members)


def summed(packed):
    plane, column = groups()

    def fold(parts, count):
        return pl.pallas_call(
            fold_kernel,
            out_shape=jax.ShapeDtypeStruct((count,) + parts.shape[1:], jnp.bfloat16),
            in_specs=[VMEM],
            out_specs=VMEM,
            name="fold",
        compiler_params=PARAMS,
        )(parts)

    held = exchange(packed, plane)
    held = fold(held, len(column[0]))
    held = exchange(held, column)
    held = fold(held, len(plane[0]))
    return exchange(held, plane)


def lat_halo(block):
    count = lax.axis_size("lat")
    up = [(i, i + 1) for i in range(count - 1)]
    down = [(i + 1, i) for i in range(count - 1)]
    south = lax.ppermute(block[-HALF:], "lat", up)
    north = lax.ppermute(block[:HALF], "lat", down)
    return south, north


def lon_halo(even, south, block, north):
    count = lax.axis_size("lon")
    tall = block.shape[0] + 2 * HALF + 2
    strips = pl.pallas_call(
        strip_kernel,
        out_shape=jax.ShapeDtypeStruct((2, HALF, tall, 128), jnp.bfloat16),
        in_specs=[SMEM, VMEM, VMEM, VMEM],
        out_specs=VMEM,
        scratch_shapes=[pltpu.VMEM((tall * SUB, 128), jnp.float32)] * 2,
        name="strips",
        compiler_params=PARAMS,
    )(even, south, block, north)
    swapped = lax.ppermute(strips, "lon", [(i, i ^ 1) for i in range(count)])
    onward = [(i, (i + 2) % count) for i in range(0, count, 2)] + [(i, (i - 2) % count) for i in range(1, count, 2)]
    got = lax.ppermute(swapped[1], "lon", onward)
    return swapped[0], got


def first_conv(flip, south, block, north, kernel, keep_tiles):
    height, across, channels = block.shape
    tiles = (height + 2 * HALF + 2) * WIDE * SUB
    out = (pltpu.VMEM((height * across, channels), jnp.float32),)
    scratch = [pltpu.VMEM((SUB * SUB + 2 * SUB, channels), jnp.float32)]
    if keep_tiles:
        out = out + (pltpu.VMEM((tiles, channels), jnp.float32),)
    else:
        scratch = [pltpu.VMEM((tiles, channels), jnp.float32)] + scratch
    return pl.pallas_call(
        functools.partial(conv_kernel, flip, keep_tiles),
        out_shape=out,
        in_specs=[VMEM] * 4,
        out_specs=[VMEM] * len(out),
        scratch_shapes=scratch,
        name="back_conv" if flip else "conv",
        compiler_params=PARAMS,
    )(south, block, north, kernel)


def f32(*shape):
    return jax.ShapeDtypeStruct(shape, jnp.float32)


def body(cells, ocean_mask, cotangent, kernel, conv_bias, gain, shift, w_in, b_in, w_out, chunk=8):
    height, across, channels = cells.shape
    ocean = jnp.broadcast_to(ocean_mask.astype(jnp.bfloat16)[..., None], cells.shape)
    masked = cells * ocean
    out_grad = cotangent * ocean
    even = (1 - lax.axis_index("lon") % 2).astype(jnp.int32).reshape(1)
    south, north = lat_halo(masked)
    keep, got = lon_halo(even, south, masked, north)
    conv, tiles = first_conv(False, south, masked, north, kernel, True)
    parts = lax.axis_size("lon")
    hidden = w_in.shape[1]
    _, _, conv_grad, packed = pl.pallas_call(
        functools.partial(block_kernel, chunk),
        out_shape=(
            pltpu.VMEM(conv.shape, jnp.float32), pltpu.VMEM(tiles.shape, jnp.float32),
            jax.ShapeDtypeStruct(cells.shape, jnp.bfloat16),
            jax.ShapeDtypeStruct((parts, 1024 // parts + max(8, SMALL // parts), channels), jnp.bfloat16),
        ),
        in_specs=[SMEM] + [VMEM] * 12,
        out_specs=[VMEM] * 4,
        scratch_shapes=[
            pltpu.VMEM((2 * HALF, height + 2 * HALF + 2, channels), jnp.float32),
            pltpu.VMEM((80, channels), jnp.float32),
            pltpu.VMEM((chunk, SUB, SUB, channels), jnp.float32),
            pltpu.VMEM((chunk * 64, channels), jnp.float32),
            pltpu.VMEM((KS, KS, SUB, channels), jnp.float32),
            pltpu.VMEM((SMALL, channels), jnp.float32),
            pltpu.VMEM((SUB, channels), jnp.float32),
            pltpu.VMEM((SUB, channels), jnp.float32),
            pltpu.VMEM((SUB, channels), jnp.float32),
            pltpu.VMEM((channels + 16, hidden), jnp.float32),
            pltpu.VMEM((channels, hidden), jnp.float32),
        ],
        input_output_aliases={1: 0, 2: 1},
        name="block",
        compiler_params=PARAMS,
    )(
        even, *[pltpu.with_memory_space_constraint(x, pltpu.VMEM) for x in (conv, tiles)], keep, got, out_grad, kernel, conv_bias.reshape(1, -1), gain.reshape(1, -1),
        shift.reshape(1, -1), w_in, b_in.reshape(1, -1), w_out,
    )
    total = summed(packed)
    south, north = lat_halo(conv_grad)
    keep, got = lon_halo(even, south, conv_grad, north)
    (spread,) = first_conv(True, south, conv_grad, north, kernel, False)
    _, cells_grad = pl.pallas_call(
        back_kernel,
        out_shape=(pltpu.VMEM(spread.shape, jnp.float32), jax.ShapeDtypeStruct(cells.shape, jnp.bfloat16)),
        in_specs=[SMEM] + [VMEM] * 6,
        out_specs=[VMEM] * 2,
        scratch_shapes=[
            pltpu.VMEM((2 * HALF, height + 2 * HALF + 2, channels), jnp.float32),
            pltpu.VMEM((80, channels), jnp.float32),
        ],
        input_output_aliases={1: 0},
        name="back",
        compiler_params=PARAMS,
    )(even, pltpu.with_memory_space_constraint(spread, pltpu.VMEM), keep, got, cotangent, ocean, kernel)
    count = height * across * lax.axis_size("lon") * lax.axis_size("lat")
    gk, gb, gg, gs, gi, gh, go = pl.pallas_call(
        functools.partial(unpack_kernel, count ** -0.5),
        out_shape=(
            f32(KS, KS, channels), f32(1, channels), f32(1, channels), f32(1, channels),
            f32(channels, hidden), f32(1, hidden), f32(hidden, channels),
        ),
        in_specs=[VMEM],
        out_specs=[VMEM] * 7,
        name="unpack",
        compiler_params=PARAMS,
    )(total)
    return cells_grad, gk, gb[0], gg[0], gs[0], gi, gh[0], go


def solution(mesh):
    whole = P("lat", "lon", None)
    in_specs = (whole, P("lat", "lon"), whole) + (P(),) * 7
    out_specs = (whole,) + (P(),) * 7
    return jax.shard_map(body, mesh=mesh, in_specs=in_specs, out_specs=out_specs, check_vma=False)
```

```python
import functools

import jax
import jax.numpy as jnp
from jax import lax
from jax.experimental import pallas as pl
from jax.experimental.pallas import tpu as pltpu
from jax.sharding import PartitionSpec as P


KS = 7
HALF = 3
SMALL = 64
WIDE = 14
DEEP = 8
SUB = 8
ROOT = 0.7978845608028654
CUBE = 0.044715
VMEM = pl.BlockSpec(memory_space=pltpu.VMEM)
PARAMS = pltpu.CompilerParams(vmem_limit_bytes=28 << 20)
SMEM = pl.BlockSpec(memory_space=pltpu.SMEM)


def spread_row(row_of, row, tiles_ref, buf_ref):
    buf_ref[HALF : HALF + 64, :] = row_of.astype(jnp.float32)
    for tap in range(WIDE):
        tiles_ref[pl.ds(row * (WIDE * SUB) + tap * SUB, SUB), :] = buf_ref[pl.ds(tap, SUB, stride=SUB), :]


def spread_all(south_ref, block_ref, north_ref, tiles_ref, buf_ref):
    height = block_ref.shape[0]
    buf_ref[...] = jnp.zeros_like(buf_ref)
    for row in range(HALF):
        spread_row(south_ref[row], row, tiles_ref, buf_ref)
        spread_row(north_ref[row], height + HALF + row, tiles_ref, buf_ref)

    def one(row, _):
        spread_row(block_ref[row], row + HALF, tiles_ref, buf_ref)
        return 0

    lax.fori_loop(0, height, one, 0)
    last = (height + 2 * HALF) * WIDE * SUB
    tiles_ref[last:, :] = jnp.zeros((2 * WIDE * SUB, 128), jnp.float32)


def tile(tiles_ref, row, t):
    return tiles_ref[pl.ds(row * (WIDE * SUB) + t * SUB, SUB), :]


def tap_weight(kernel_ref, a, b, flip):
    if flip:
        a, b = KS - 1 - a, KS - 1 - b
    return jnp.broadcast_to(kernel_ref[a, b : b + 1, :], (SUB, 128))


def conv_rows(tiles_ref, kernel_ref, out_ref, start, stop, flip):
    def one(row, _):
        total = [None] * SUB
        for a in range(KS):
            cells = [tile(tiles_ref, row + a, t) for t in range(WIDE)]
            for b in range(KS):
                weight = tap_weight(kernel_ref, a, b, flip)
                for t in range(SUB):
                    term = weight * cells[t + b]
                    total[t] = term if total[t] is None else total[t] + term
        for t in range(SUB):
            out_ref[pl.ds(row * 64 + t * SUB, SUB), :] = total[t]
        return 0

    lax.fori_loop(start, stop, one, 0)


def edge_columns(even, keep_ref, got_ref, cols_ref):
    for c in range(HALF):
        keep = keep_ref[c].astype(jnp.float32)
        got = got_ref[c].astype(jnp.float32)
        cols_ref[c] = jnp.where(even, got, keep)
        cols_ref[HALF + c] = jnp.where(even, keep, got)


def add_edges(cols_ref, kernel_ref, out_ref, height, flip, depth=SUB):
    for west in (True, False):
        for at in range(HALF):
            across = 64 // depth
            first = at * depth if west else (across - HALF + at) * depth + depth - 1
            totals = [None] * (height // SUB)
            for a in range(KS):
                for b in range(KS):
                    c = at + b if west else at + b - HALF
                    if not ((0 <= c < HALF) if west else (HALF <= c < 2 * HALF)):
                        continue
                    weight = tap_weight(kernel_ref, a, b, flip)
                    for block in range(height // SUB):
                        term = weight * cols_ref[c, pl.ds(block * SUB + a, SUB), :]
                        totals[block] = term if totals[block] is None else totals[block] + term
            for block in range(height // SUB):
                place = pl.ds(block * SUB * 64 + first, SUB, stride=64)
                out_ref[place, :] = out_ref[place, :] + totals[block]


def gather_row(tiles, buf_ref):
    for t in range(SUB):
        buf_ref[pl.ds(t, SUB, stride=SUB), :] = tiles[t]
    return buf_ref[0 : SUB * SUB, :]


def put_sides(low_ref, high_ref, out_ref, rows):
    for c in range(HALF):
        west = low_ref[pl.ds(c, rows, stride=SUB), :].astype(jnp.bfloat16)
        east = high_ref[pl.ds(SUB - HALF + c, rows, stride=SUB), :].astype(jnp.bfloat16)
        for member in range(2):
            out_ref[member, 0, c] = west
            out_ref[member, 1, c] = east


def strip_kernel(even_ref, south_ref, block_ref, north_ref, out_ref, low_ref, high_ref):
    height = block_ref.shape[0]

    def put(at, row_of):
        low_ref[pl.ds(at * SUB, SUB), :] = row_of[0:SUB].astype(jnp.float32)
        high_ref[pl.ds(at * SUB, SUB), :] = row_of[64 - SUB : 64].astype(jnp.float32)

    for row in range(HALF):
        put(row, south_ref[row])
        put(row + height + HALF, north_ref[row])

    def one(step, _):
        for r in range(SUB):
            put(step * SUB + r + HALF, block_ref[step * SUB + r])
        return 0

    lax.fori_loop(0, height // SUB, one, 0)
    tall = height + 2 * HALF + 2
    low_ref[(tall - 2) * SUB :, :] = jnp.zeros((2 * SUB, 128), jnp.float32)
    high_ref[(tall - 2) * SUB :, :] = jnp.zeros((2 * SUB, 128), jnp.float32)
    even = even_ref[0] == 1
    for c in range(HALF):
        west = low_ref[pl.ds(c, tall, stride=SUB), :]
        east = high_ref[pl.ds(SUB - HALF + c, tall, stride=SUB), :]
        out_ref[0, c] = jnp.where(even, east, west).astype(jnp.bfloat16)
        out_ref[1, c] = jnp.where(even, west, east).astype(jnp.bfloat16)


def back_conv_kernel(south_ref, block_ref, north_ref, kernel_ref, out_ref, tiles_ref, buf_ref):
    spread_all(south_ref, block_ref, north_ref, tiles_ref, buf_ref)
    conv_rows(tiles_ref, kernel_ref, out_ref, 0, block_ref.shape[0], True)


def side_kernel(block_ref, out_ref, low_ref, high_ref):
    height = block_ref.shape[0]

    def one(step, _):
        for r in range(SUB):
            row_of = block_ref[step * SUB + r]
            at = pl.ds((step * SUB + r) * SUB, SUB)
            low_ref[at, :] = row_of[0:SUB].astype(jnp.float32)
            high_ref[at, :] = row_of[64 - SUB : 64].astype(jnp.float32)
        return 0

    lax.fori_loop(0, height // SUB, one, 0)
    put_sides(low_ref, high_ref, out_ref, height)


def tall_kernel(even_ref, body_ref, south_ref, north_ref, keep_ref, pass_ref, buf_ref):
    height = body_ref.shape[3]
    even = even_ref[0] == 1
    buf_ref[...] = jnp.zeros_like(buf_ref)
    for at, ref in enumerate((keep_ref, pass_ref)):
        for c in range(HALF):
            def pick(of_ref):
                return jnp.where(even, of_ref[1, at, c].astype(jnp.float32), of_ref[0, 1 - at, c].astype(jnp.float32))

            buf_ref[0:HALF, :] = pick(south_ref)
            buf_ref[HALF : HALF + height, :] = pick(body_ref)
            buf_ref[HALF + height : 2 * HALF + height, :] = pick(north_ref)
            ref[c] = buf_ref[...].astype(jnp.bfloat16)


def rest_kernel(start, conv_in, tiles_ref, kernel_ref, out_ref):
    del conv_in
    conv_rows(tiles_ref, kernel_ref, out_ref, start, out_ref.shape[0] // 64, False)


def conv_kernel(rows, south_ref, block_ref, north_ref, kernel_ref, out_ref, tiles_ref, buf_ref):
    spread_all(south_ref, block_ref, north_ref, tiles_ref, buf_ref)
    conv_rows(tiles_ref, kernel_ref, out_ref, 0, rows, False)


def block_kernel(
    chunk,
    even_ref, conv_in, tiles_in, keep_ref, got_ref, out_grad_ref,
    kernel_ref, bias_ref, gain_ref, shift_ref, w_in_ref, b_in_ref, w_out_ref,
    conv_ref, tiles_ref, conv_grad_ref, packed_ref,
    cols_ref, buf_ref, og_tiles, round_ref, taps_ref, small_ref,
    bias_sum, gain_sum, shift_sum, grad_in, grad_out,
):
    del conv_in, tiles_in
    height = out_grad_ref.shape[0]
    cells = chunk * 64
    edge_columns(even_ref[0] == 1, keep_ref, got_ref, cols_ref)
    span = WIDE * SUB
    for c in range(HALF):
        for block in range((height + 2 * HALF + 2) // SUB):
            rows = pl.ds(block * SUB, SUB)
            start = block * SUB * span
            tiles_ref[pl.ds(start + c * SUB, SUB, stride=span), :] = cols_ref[c, rows, :]
            tiles_ref[pl.ds(start + (SUB + HALF + c) * SUB + SUB - 1, SUB, stride=span), :] = cols_ref[HALF + c, rows, :]
    add_edges(cols_ref, kernel_ref, conv_ref, height, False)
    for ref in (bias_sum, gain_sum, shift_sum, grad_in, grad_out, taps_ref):
        ref[...] = jnp.zeros_like(ref)
    bias = bias_ref[...]
    gain = gain_ref[...]
    shift = shift_ref[...]
    b_in = b_in_ref[...]
    w_half = w_out_ref[...] * jnp.bfloat16(0.5)

    ones = jnp.where(
        lax.broadcasted_iota(jnp.int32, (16, cells), 0) == 0, 1.0, 0.0
    ).astype(jnp.bfloat16)

    def taps(first):
        for r in range(chunk):
            row = first + r
            grads = [round_ref[r * 64 + t * SUB : r * 64 + (t + 1) * SUB, :] for t in range(SUB)]
            for a in range(KS):
                near = [tile(tiles_ref, row + a, t) for t in range(WIDE)]
                for b in range(KS):
                    total = taps_ref[a, b]
                    for t in range(SUB):
                        total = total + grads[t] * near[t + b]
                    taps_ref[a, b] = total

    def one(step, pending):
        first = step * chunk
        if pending is not None:
            taps(first - chunk)
        for r in range(chunk):
            buf_ref[0:64, :] = out_grad_ref[first + r].astype(jnp.float32)
            for t in range(SUB):
                og_tiles[r, t] = buf_ref[pl.ds(t, SUB, stride=SUB), :]
        conv = conv_ref[pl.ds(first * 64, cells), :] + bias
        out_grad = og_tiles[...].reshape(cells, 128).astype(jnp.bfloat16)
        average = jnp.mean(conv, axis=-1, keepdims=True)
        centred = conv - average
        variance = jnp.mean(centred * centred, axis=-1, keepdims=True)
        inverse = lax.rsqrt(variance + 1e-06)
        scaled = centred * inverse
        normed = (scaled * gain + shift).astype(jnp.bfloat16)
        v = jnp.dot(normed, w_in_ref[...], preferred_element_type=jnp.float32) + b_in
        act_grad = lax.dot_general(
            out_grad, w_half, (((1,), (1,)), ((), ())), preferred_element_type=jnp.float32
        )
        square = v * v
        curve = jnp.tanh(v * (ROOT + (ROOT * CUBE) * square))
        above = 1.0 + curve
        twice = (v * above).astype(jnp.bfloat16)
        rise = v * (ROOT + (3 * ROOT * CUBE) * square)
        hidden = (act_grad * (above * (1.0 + (1.0 - curve) * rise))).astype(jnp.bfloat16)
        grad_out[...] += lax.dot_general(
            out_grad, twice, (((0,), (0,)), ((), ())), preferred_element_type=jnp.float32
        )
        grad_in[...] += jnp.dot(
            jnp.concatenate([normed.T, ones], axis=0), hidden, preferred_element_type=jnp.float32
        )
        norm_grad = lax.dot_general(
            hidden, w_in_ref[...], (((1,), (1,)), ((), ())), preferred_element_type=jnp.float32
        )
        gain_sum[...] += jnp.sum((norm_grad * scaled).reshape(-1, SUB, 128), axis=0)
        shift_sum[...] += jnp.sum(norm_grad.reshape(-1, SUB, 128), axis=0)
        weighted = norm_grad * gain
        conv_grad = inverse * (
            weighted
            - jnp.mean(weighted, axis=-1, keepdims=True)
            - scaled * jnp.mean(weighted * scaled, axis=-1, keepdims=True)
        )
        rounded = conv_grad.astype(jnp.bfloat16).astype(jnp.float32)
        bias_sum[...] += jnp.sum(rounded.reshape(-1, SUB, 128), axis=0)
        round_ref[...] = rounded
        for r in range(chunk):
            natural = gather_row(
                [rounded[r * 64 + t * SUB : r * 64 + (t + 1) * SUB] for t in range(SUB)], buf_ref
            )
            conv_grad_ref[first + r] = natural.astype(jnp.bfloat16)
        return 0

    one(0, None)
    lax.fori_loop(1, height // chunk, one, 0)
    taps(height - chunk)
    pack(taps_ref, bias_sum, gain_sum, shift_sum, grad_in, grad_out, packed_ref, small_ref)


def pack(taps_ref, bias_sum, gain_sum, shift_sum, grad_in, grad_out, out_ref, small_ref):
    small_ref[...] = jnp.zeros_like(small_ref)
    for a in range(KS):
        for b in range(KS):
            small_ref[a * KS + b] = jnp.sum(taps_ref[a, b], axis=0)
    for at, ref in enumerate((bias_sum, gain_sum, shift_sum)):
        small_ref[KS * KS + at] = jnp.sum(ref[...], axis=0)
    for q in range(4):
        small_ref[KS * KS + 3 + q] = grad_in[128, q * 128 : (q + 1) * 128]
    parts = out_ref.shape[0]
    rows = 1024 // parts
    each = 128 // rows
    for at, ref, scale in ((0, grad_in, 1.0), (4, grad_out, 0.5)):
        for q in range(4):
            block = ref[0:128, q * 128 : (q + 1) * 128].reshape(each, rows, 128)
            out_ref[(at + q) * each : (at + q + 1) * each, 0:rows, :] = (block * scale).astype(jnp.bfloat16)
    per = SMALL // parts
    spare = out_ref.shape[1] - rows - 2 * per
    small = small_ref[...].reshape(parts, per, 128)
    high = small.astype(jnp.bfloat16).astype(jnp.float32)
    pieces = [high, small - high] + ([jnp.zeros((parts, spare, 128), jnp.float32)] if spare else [])
    out_ref[:, rows:, :] = jnp.concatenate(pieces, axis=1).astype(jnp.bfloat16)


def back_kernel(even_ref, spread_in, keep_ref, got_ref, cot_ref, mask_ref, kernel_ref, spread_ref, out_ref, cols_ref, buf_ref):
    del spread_in
    height = cot_ref.shape[0]
    edge_columns(even_ref[0] == 1, keep_ref, got_ref, cols_ref)
    add_edges(cols_ref, kernel_ref, spread_ref, height, True, DEEP)

    def one(row, _):
        for t in range(64 // DEEP):
            buf_ref[pl.ds(t, DEEP, stride=64 // DEEP), :] = spread_ref[pl.ds(row * 64 + t * DEEP, DEEP), :]
        spread = buf_ref[0:64, :]
        out_ref[row] = (
            (cot_ref[row].astype(jnp.float32) + spread) * mask_ref[row].astype(jnp.float32)
        ).astype(jnp.bfloat16)
        return 0

    lax.fori_loop(0, height, one, 0)


def fold_kernel(rows, per, parts_ref, out_ref):
    total = jnp.sum(parts_ref[...].astype(jnp.float32), axis=0)
    small = total[rows : rows + per] + total[rows + per : rows + 2 * per]
    high = small.astype(jnp.bfloat16).astype(jnp.float32)
    pieces = [total[0:rows], high, small - high]
    if total.shape[0] > rows + 2 * per:
        pieces.append(jnp.zeros((total.shape[0] - rows - 2 * per, 128), jnp.float32))
    total = jnp.concatenate(pieces, axis=0).astype(jnp.bfloat16)
    out_ref[...] = jnp.broadcast_to(total[None], out_ref.shape)


def unpack_kernel(factor, all_ref, kernel_ref, bias_ref, gain_ref, shift_ref, in_ref, b_ref, out_ref):
    parts = all_ref.shape[0]
    rows = 1024 // parts
    each = 128 // rows
    for q in range(4):
        block = all_ref[q * each : (q + 1) * each, 0:rows, :].astype(jnp.float32)
        in_ref[:, q * 128 : (q + 1) * 128] = block.reshape(128, 128) * factor
    for q in range(4):
        block = all_ref[(4 + q) * each : (5 + q) * each, 0:rows, :].astype(jnp.float32)
        out_ref[q * 128 : (q + 1) * 128, :] = block.reshape(128, 128).T * factor
    per = SMALL // parts
    both = all_ref[:, rows:, :].astype(jnp.float32)
    small = (both[:, 0:per] + both[:, per : 2 * per]) * factor

    def row(r):
        return small[r // (SMALL // parts), r % (SMALL // parts)]

    for a in range(KS):
        for b in range(KS):
            kernel_ref[a, b] = row(a * KS + b)
    for at, ref in enumerate((bias_ref, gain_ref, shift_ref)):
        ref[0] = row(KS * KS + at)
    for q in range(4):
        b_ref[0, q * 128 : (q + 1) * 128] = row(KS * KS + 3 + q)


def groups():
    count_lon, count_lat = lax.axis_size("lon"), lax.axis_size("lat")
    plane = [[[] for _ in range(count_lat // 2)] for _ in range(2)]
    column = [[[] for _ in range(2)] for _ in range(count_lon // 2)]
    for lon in range(count_lon):
        for lat in range(count_lat):
            at = lon * count_lat + lat
            plane[lon % 2][lat // 2].append(at)
            column[lon // 2][lat % 2].append(at)
    return [g for part in plane for g in part], [g for part in column for g in part]


def exchange(parts, members):
    return lax.all_to_all(parts, ("lon", "lat"), 0, 0, tiled=True, axis_index_groups=members)


def summed(packed):
    count_lon = lax.axis_size("lon")
    plane, column = groups()

    def fold(parts, count):
        return pl.pallas_call(
            functools.partial(fold_kernel, 1024 // count_lon, SMALL // count_lon),
            out_shape=jax.ShapeDtypeStruct((count,) + parts.shape[1:], jnp.bfloat16),
            in_specs=[VMEM],
            out_specs=VMEM,
            name="fold",
        compiler_params=PARAMS,
        )(parts)

    held = exchange(packed, plane)
    held = fold(held, len(column[0]))
    held = exchange(held, column)
    held = fold(held, len(plane[0]))
    return exchange(held, plane)


def lat_halo(top, bottom):
    count = lax.axis_size("lat")
    up = [(i, i + 1) for i in range(count - 1)]
    down = [(i + 1, i) for i in range(count - 1)]
    south = lax.ppermute(top, "lat", up)
    north = lax.ppermute(bottom, "lat", down)
    return south, north


def swap(sides):
    pairs = [[i, i + 1] for i in range(0, lax.axis_size("lon"), 2)]
    return lax.all_to_all(sides, "lon", 0, 0, tiled=True, axis_index_groups=pairs)


def onward_pairs():
    count = lax.axis_size("lon")
    return [(i, (i + 2) % count) for i in range(0, count, 2)] + [(i, (i - 2) % count) for i in range(1, count, 2)]


def lon_halo(even, south, block, north):
    tall = block.shape[0] + 2 * HALF + 2
    strips = pl.pallas_call(
        strip_kernel,
        out_shape=jax.ShapeDtypeStruct((2, HALF, tall, 128), jnp.bfloat16),
        in_specs=[SMEM, VMEM, VMEM, VMEM],
        out_specs=VMEM,
        scratch_shapes=[pltpu.VMEM((tall * SUB, 128), jnp.float32)] * 2,
        name="strips",
        compiler_params=PARAMS,
    )(even, south, block, north)
    swapped = lax.ppermute(strips, "lon", [(i, i ^ 1) for i in range(lax.axis_size("lon"))])
    got = lax.ppermute(swapped[1], "lon", onward_pairs())
    return swapped[0], got


def first_conv(south, block, north, kernel, rows):
    height, across, channels = block.shape
    tiles = (height + 2 * HALF + 2) * WIDE * SUB
    return pl.pallas_call(
        functools.partial(conv_kernel, rows),
        out_shape=(
            pltpu.VMEM((height * across, channels), jnp.float32),
            pltpu.VMEM((tiles, channels), jnp.float32),
        ),
        in_specs=[VMEM] * 4,
        out_specs=[VMEM] * 2,
        scratch_shapes=[pltpu.VMEM((SUB * SUB + 2 * SUB, channels), jnp.float32)],
        compiler_params=PARAMS,
        name="conv",
    )(south, block, north, kernel)


def f32(*shape):
    return jax.ShapeDtypeStruct(shape, jnp.float32)


def body(cells, ocean_mask, cotangent, kernel, conv_bias, gain, shift, w_in, b_in, w_out, chunk=8):
    height, across, channels = cells.shape
    ocean = jnp.broadcast_to(ocean_mask.astype(jnp.bfloat16)[..., None], cells.shape)
    masked = cells * ocean
    out_grad = cotangent * ocean
    even = (1 - lax.axis_index("lon") % 2).astype(jnp.int32).reshape(1)
    south, north = lat_halo(cells[-HALF:] * ocean[-HALF:], cells[:HALF] * ocean[:HALF])
    sides = pl.pallas_call(
        side_kernel,
        out_shape=jax.ShapeDtypeStruct((2, 2, HALF, height, channels), jnp.bfloat16),
        in_specs=[VMEM],
        out_specs=VMEM,
        scratch_shapes=[pltpu.VMEM((height * SUB, channels), jnp.float32)] * 2,
        compiler_params=PARAMS,
        name="sides",
    )(masked)
    swapped = swap(sides)
    corner_south, corner_north = lat_halo(swapped[..., -HALF:, :], swapped[..., :HALF, :])
    tall = jax.ShapeDtypeStruct((HALF, height + 2 * HALF + 2, channels), jnp.bfloat16)
    keep, onward = pl.pallas_call(
        tall_kernel,
        out_shape=(tall, tall),
        in_specs=[SMEM] + [VMEM] * 3,
        out_specs=[VMEM] * 2,
        scratch_shapes=[pltpu.VMEM(tall.shape[1:], jnp.float32)],
        compiler_params=PARAMS,
        name="tall",
    )(even, swapped, corner_south, corner_north)
    got = lax.ppermute(onward, "lon", onward_pairs())
    early = height * 3 // 4
    conv, tiles = first_conv(south, masked, north, kernel, early)
    conv = pl.pallas_call(
        functools.partial(rest_kernel, early),
        out_shape=pltpu.VMEM(conv.shape, jnp.float32),
        in_specs=[VMEM] * 3,
        out_specs=VMEM,
        input_output_aliases={0: 0},
        compiler_params=PARAMS,
        name="rest",
    )(*[pltpu.with_memory_space_constraint(x, pltpu.VMEM) for x in (conv, tiles)], kernel)
    parts = lax.axis_size("lon")
    hidden = w_in.shape[1]
    _, _, conv_grad, packed = pl.pallas_call(
        functools.partial(block_kernel, chunk),
        out_shape=(
            pltpu.VMEM(conv.shape, jnp.float32), pltpu.VMEM(tiles.shape, jnp.float32),
            jax.ShapeDtypeStruct(cells.shape, jnp.bfloat16),
            jax.ShapeDtypeStruct((parts, 1024 // parts + max(8, 2 * SMALL // parts), channels), jnp.bfloat16),
        ),
        in_specs=[SMEM] + [VMEM] * 12,
        out_specs=[VMEM] * 4,
        scratch_shapes=[
            pltpu.VMEM((2 * HALF, height + 2 * HALF + 2, channels), jnp.float32),
            pltpu.VMEM((80, channels), jnp.float32),
            pltpu.VMEM((chunk, SUB, SUB, channels), jnp.float32),
            pltpu.VMEM((chunk * 64, channels), jnp.float32),
            pltpu.VMEM((KS, KS, SUB, channels), jnp.float32),
            pltpu.VMEM((SMALL, channels), jnp.float32),
            pltpu.VMEM((SUB, channels), jnp.float32),
            pltpu.VMEM((SUB, channels), jnp.float32),
            pltpu.VMEM((SUB, channels), jnp.float32),
            pltpu.VMEM((channels + 16, hidden), jnp.float32),
            pltpu.VMEM((channels, hidden), jnp.float32),
        ],
        input_output_aliases={1: 0, 2: 1},
        name="block",
        compiler_params=PARAMS,
    )(
        even, *[pltpu.with_memory_space_constraint(x, pltpu.VMEM) for x in (conv, tiles)], keep, got, out_grad, kernel, conv_bias.reshape(1, -1), gain.reshape(1, -1),
        shift.reshape(1, -1), w_in, b_in.reshape(1, -1), w_out,
    )
    total = summed(packed)
    south, north = lat_halo(conv_grad[-HALF:], conv_grad[:HALF])
    keep, got = lon_halo(even, south, conv_grad, north)
    spread = pl.pallas_call(
        back_conv_kernel,
        out_shape=pltpu.VMEM((height * across, channels), jnp.float32),
        in_specs=[VMEM] * 4,
        out_specs=VMEM,
        scratch_shapes=[
            pltpu.VMEM(((height + 2 * HALF + 2) * WIDE * SUB, channels), jnp.float32),
            pltpu.VMEM((SUB * SUB + 2 * SUB, channels), jnp.float32),
        ],
        compiler_params=PARAMS,
        name="back_conv",
    )(south, conv_grad, north, kernel)
    _, cells_grad = pl.pallas_call(
        back_kernel,
        out_shape=(pltpu.VMEM(spread.shape, jnp.float32), jax.ShapeDtypeStruct(cells.shape, jnp.bfloat16)),
        in_specs=[SMEM] + [VMEM] * 6,
        out_specs=[VMEM] * 2,
        scratch_shapes=[
            pltpu.VMEM((2 * HALF, height + 2 * HALF + 2, channels), jnp.float32),
            pltpu.VMEM((80, channels), jnp.float32),
        ],
        input_output_aliases={1: 0},
        name="back",
        compiler_params=PARAMS,
    )(even, pltpu.with_memory_space_constraint(spread, pltpu.VMEM), keep, got, cotangent, ocean, kernel)
    count = height * across * lax.axis_size("lon") * lax.axis_size("lat")
    gk, gb, gg, gs, gi, gh, go = pl.pallas_call(
        functools.partial(unpack_kernel, count ** -0.5),
        out_shape=(
            f32(KS, KS, channels), f32(1, channels), f32(1, channels), f32(1, channels),
            f32(channels, hidden), f32(1, hidden), f32(hidden, channels),
        ),
        in_specs=[VMEM],
        out_specs=[VMEM] * 7,
        name="unpack",
        compiler_params=PARAMS,
    )(total)
    return cells_grad, gk, gb[0], gg[0], gs[0], gi, gh[0], go


def solution(mesh):
    whole = P("lat", "lon", None)
    in_specs = (whole, P("lat", "lon"), whole) + (P(),) * 7
    out_specs = (whole,) + (P(),) * 7
    return jax.shard_map(body, mesh=mesh, in_specs=in_specs, out_specs=out_specs, check_vma=False)
```

```python
import functools

import jax
import jax.numpy as jnp
from jax import lax
from jax.experimental import pallas as pl
from jax.experimental.pallas import tpu as pltpu
from jax.sharding import PartitionSpec as P


KS = 7
HALF = 3
SMALL = 64
WIDE = 14
DEEP = 8
SUB = 8
ROOT = 0.7978845608028654
CUBE = 0.044715
VMEM = pl.BlockSpec(memory_space=pltpu.VMEM)
PARAMS = pltpu.CompilerParams(vmem_limit_bytes=28 << 20)
SMEM = pl.BlockSpec(memory_space=pltpu.SMEM)


def spread_row(row_of, row, tiles_ref, buf_ref):
    buf_ref[HALF : HALF + 64, :] = row_of.astype(jnp.float32)
    for tap in range(WIDE):
        tiles_ref[pl.ds(row * (WIDE * SUB) + tap * SUB, SUB), :] = buf_ref[pl.ds(tap, SUB, stride=SUB), :]


def spread_all(south_ref, block_ref, north_ref, tiles_ref, buf_ref):
    height = block_ref.shape[0]
    buf_ref[...] = jnp.zeros_like(buf_ref)
    for row in range(HALF):
        spread_row(south_ref[row], row, tiles_ref, buf_ref)
        spread_row(north_ref[row], height + HALF + row, tiles_ref, buf_ref)

    def one(row, _):
        spread_row(block_ref[row], row + HALF, tiles_ref, buf_ref)
        return 0

    lax.fori_loop(0, height, one, 0)
    last = (height + 2 * HALF) * WIDE * SUB
    tiles_ref[last:, :] = jnp.zeros((2 * WIDE * SUB, 128), jnp.float32)


def tile(tiles_ref, row, t):
    return tiles_ref[pl.ds(row * (WIDE * SUB) + t * SUB, SUB), :]


def tap_weight(kernel_ref, a, b, flip):
    if flip:
        a, b = KS - 1 - a, KS - 1 - b
    return jnp.broadcast_to(kernel_ref[a, b : b + 1, :], (SUB, 128))


def conv_rows(tiles_ref, kernel_ref, out_ref, start, stop, flip):
    def one(row, _):
        total = [None] * SUB
        for a in range(KS):
            cells = [tile(tiles_ref, row + a, t) for t in range(WIDE)]
            for b in range(KS):
                weight = tap_weight(kernel_ref, a, b, flip)
                for t in range(SUB):
                    term = weight * cells[t + b]
                    total[t] = term if total[t] is None else total[t] + term
        for t in range(SUB):
            out_ref[pl.ds(row * 64 + t * SUB, SUB), :] = total[t]
        return 0

    lax.fori_loop(start, stop, one, 0)


def edge_columns(even, keep_ref, got_ref, cols_ref):
    for c in range(HALF):
        keep = keep_ref[c].astype(jnp.float32)
        got = got_ref[c].astype(jnp.float32)
        cols_ref[c] = jnp.where(even, got, keep)
        cols_ref[HALF + c] = jnp.where(even, keep, got)


def add_edges(cols_ref, kernel_ref, out_ref, height, flip, depth=SUB):
    for west in (True, False):
        for at in range(HALF):
            across = 64 // depth
            first = at * depth if west else (across - HALF + at) * depth + depth - 1
            totals = [None] * (height // SUB)
            for a in range(KS):
                for b in range(KS):
                    c = at + b if west else at + b - HALF
                    if not ((0 <= c < HALF) if west else (HALF <= c < 2 * HALF)):
                        continue
                    weight = tap_weight(kernel_ref, a, b, flip)
                    for block in range(height // SUB):
                        term = weight * cols_ref[c, pl.ds(block * SUB + a, SUB), :]
                        totals[block] = term if totals[block] is None else totals[block] + term
            for block in range(height // SUB):
                place = pl.ds(block * SUB * 64 + first, SUB, stride=64)
                out_ref[place, :] = out_ref[place, :] + totals[block]


def gather_row(tiles, buf_ref):
    for t in range(SUB):
        buf_ref[pl.ds(t, SUB, stride=SUB), :] = tiles[t]
    return buf_ref[0 : SUB * SUB, :]


def strip_kernel(even_ref, south_ref, block_ref, north_ref, out_ref, low_ref, high_ref):
    height = block_ref.shape[0]

    def put(at, row_of):
        low_ref[pl.ds(at * SUB, SUB), :] = row_of[0:SUB].astype(jnp.float32)
        high_ref[pl.ds(at * SUB, SUB), :] = row_of[64 - SUB : 64].astype(jnp.float32)

    for row in range(HALF):
        put(row, south_ref[row])
        put(row + height + HALF, north_ref[row])

    def one(step, _):
        for r in range(SUB):
            put(step * SUB + r + HALF, block_ref[step * SUB + r])
        return 0

    lax.fori_loop(0, height // SUB, one, 0)
    tall = height + 2 * HALF + 2
    low_ref[(tall - 2) * SUB :, :] = jnp.zeros((2 * SUB, 128), jnp.float32)
    high_ref[(tall - 2) * SUB :, :] = jnp.zeros((2 * SUB, 128), jnp.float32)
    even = even_ref[0] == 1
    for c in range(HALF):
        west = low_ref[pl.ds(c, tall, stride=SUB), :]
        east = high_ref[pl.ds(SUB - HALF + c, tall, stride=SUB), :]
        out_ref[0, c] = jnp.where(even, east, west).astype(jnp.bfloat16)
        out_ref[1, c] = jnp.where(even, west, east).astype(jnp.bfloat16)


def back_conv_kernel(south_ref, block_ref, north_ref, kernel_ref, out_ref, tiles_ref, buf_ref):
    spread_all(south_ref, block_ref, north_ref, tiles_ref, buf_ref)
    conv_rows(tiles_ref, kernel_ref, out_ref, 0, block_ref.shape[0], True)


def rest_kernel(start, conv_in, tiles_ref, kernel_ref, out_ref):
    del conv_in
    conv_rows(tiles_ref, kernel_ref, out_ref, start, out_ref.shape[0] // 64, False)


def conv_kernel(rows, south_ref, block_ref, north_ref, kernel_ref, out_ref, tiles_ref, buf_ref):
    spread_all(south_ref, block_ref, north_ref, tiles_ref, buf_ref)
    conv_rows(tiles_ref, kernel_ref, out_ref, 0, rows, False)


def block_kernel(
    chunk,
    even_ref, conv_in, tiles_in, keep_ref, got_ref, out_grad_ref,
    kernel_ref, bias_ref, gain_ref, shift_ref, w_in_ref, b_in_ref, w_out_ref,
    conv_ref, tiles_ref, conv_grad_ref, packed_ref,
    cols_ref, buf_ref, og_tiles, round_ref, taps_ref, small_ref,
    bias_sum, gain_sum, shift_sum, grad_in, grad_out,
):
    del conv_in, tiles_in
    height = out_grad_ref.shape[0]
    cells = chunk * 64
    edge_columns(even_ref[0] == 1, keep_ref, got_ref, cols_ref)
    span = WIDE * SUB
    for c in range(HALF):
        for block in range((height + 2 * HALF + 2) // SUB):
            rows = pl.ds(block * SUB, SUB)
            start = block * SUB * span
            tiles_ref[pl.ds(start + c * SUB, SUB, stride=span), :] = cols_ref[c, rows, :]
            tiles_ref[pl.ds(start + (SUB + HALF + c) * SUB + SUB - 1, SUB, stride=span), :] = cols_ref[HALF + c, rows, :]
    add_edges(cols_ref, kernel_ref, conv_ref, height, False)
    for ref in (bias_sum, gain_sum, shift_sum, grad_in, grad_out, taps_ref):
        ref[...] = jnp.zeros_like(ref)
    bias = bias_ref[...]
    gain = gain_ref[...]
    shift = shift_ref[...]
    b_in = b_in_ref[...]
    w_half = w_out_ref[...] * jnp.bfloat16(0.5)

    ones = jnp.where(
        lax.broadcasted_iota(jnp.int32, (16, cells), 0) == 0, 1.0, 0.0
    ).astype(jnp.bfloat16)

    def taps(first):
        for r in range(chunk):
            row = first + r
            grads = [round_ref[r * 64 + t * SUB : r * 64 + (t + 1) * SUB, :] for t in range(SUB)]
            for a in range(KS):
                near = [tile(tiles_ref, row + a, t) for t in range(WIDE)]
                for b in range(KS):
                    total = taps_ref[a, b]
                    for t in range(SUB):
                        total = total + grads[t] * near[t + b]
                    taps_ref[a, b] = total

    def one(step, pending):
        first = step * chunk
        if pending is not None:
            taps(first - chunk)
        for r in range(chunk):
            buf_ref[0:64, :] = out_grad_ref[first + r].astype(jnp.float32)
            for t in range(SUB):
                og_tiles[r, t] = buf_ref[pl.ds(t, SUB, stride=SUB), :]
        conv = conv_ref[pl.ds(first * 64, cells), :] + bias
        out_grad = og_tiles[...].reshape(cells, 128).astype(jnp.bfloat16)
        average = jnp.mean(conv, axis=-1, keepdims=True)
        centred = conv - average
        variance = jnp.mean(centred * centred, axis=-1, keepdims=True)
        inverse = lax.rsqrt(variance + 1e-06)
        scaled = centred * inverse
        normed = (scaled * gain + shift).astype(jnp.bfloat16)
        v = jnp.dot(normed, w_in_ref[...], preferred_element_type=jnp.float32) + b_in
        act_grad = lax.dot_general(
            out_grad, w_half, (((1,), (1,)), ((), ())), preferred_element_type=jnp.float32
        )
        square = v * v
        curve = jnp.tanh(v * (ROOT + (ROOT * CUBE) * square))
        above = 1.0 + curve
        twice = (v * above).astype(jnp.bfloat16)
        rise = v * (ROOT + (3 * ROOT * CUBE) * square)
        hidden = (act_grad * (above * (1.0 + (1.0 - curve) * rise))).astype(jnp.bfloat16)
        grad_out[...] += lax.dot_general(
            out_grad, twice, (((0,), (0,)), ((), ())), preferred_element_type=jnp.float32
        )
        grad_in[...] += jnp.dot(
            jnp.concatenate([normed.T, ones], axis=0), hidden, preferred_element_type=jnp.float32
        )
        norm_grad = lax.dot_general(
            hidden, w_in_ref[...], (((1,), (1,)), ((), ())), preferred_element_type=jnp.float32
        )
        gain_sum[...] += jnp.sum((norm_grad * scaled).reshape(-1, SUB, 128), axis=0)
        shift_sum[...] += jnp.sum(norm_grad.reshape(-1, SUB, 128), axis=0)
        weighted = norm_grad * gain
        conv_grad = inverse * (
            weighted
            - jnp.mean(weighted, axis=-1, keepdims=True)
            - scaled * jnp.mean(weighted * scaled, axis=-1, keepdims=True)
        )
        rounded = conv_grad.astype(jnp.bfloat16).astype(jnp.float32)
        bias_sum[...] += jnp.sum(rounded.reshape(-1, SUB, 128), axis=0)
        round_ref[...] = rounded
        for r in range(chunk):
            natural = gather_row(
                [rounded[r * 64 + t * SUB : r * 64 + (t + 1) * SUB] for t in range(SUB)], buf_ref
            )
            conv_grad_ref[first + r] = natural.astype(jnp.bfloat16)
        return 0

    one(0, None)
    lax.fori_loop(1, height // chunk, one, 0)
    taps(height - chunk)
    pack(taps_ref, bias_sum, gain_sum, shift_sum, grad_in, grad_out, packed_ref, small_ref)


def pack(taps_ref, bias_sum, gain_sum, shift_sum, grad_in, grad_out, out_ref, small_ref):
    small_ref[...] = jnp.zeros_like(small_ref)
    for a in range(KS):
        for b in range(KS):
            small_ref[a * KS + b] = jnp.sum(taps_ref[a, b], axis=0)
    for at, ref in enumerate((bias_sum, gain_sum, shift_sum)):
        small_ref[KS * KS + at] = jnp.sum(ref[...], axis=0)
    for q in range(4):
        small_ref[KS * KS + 3 + q] = grad_in[128, q * 128 : (q + 1) * 128]
    parts = out_ref.shape[0]
    rows = 1024 // parts
    each = 128 // rows
    for at, ref, scale in ((0, grad_in, 1.0), (4, grad_out, 0.5)):
        for q in range(4):
            block = ref[0:128, q * 128 : (q + 1) * 128].reshape(each, rows, 128)
            out_ref[(at + q) * each : (at + q + 1) * each, 0:rows, :] = (block * scale).astype(jnp.bfloat16)
    per = SMALL // parts
    spare = out_ref.shape[1] - rows - 2 * per
    small = small_ref[...].reshape(parts, per, 128)
    high = small.astype(jnp.bfloat16).astype(jnp.float32)
    pieces = [high, small - high] + ([jnp.zeros((parts, spare, 128), jnp.float32)] if spare else [])
    out_ref[:, rows:, :] = jnp.concatenate(pieces, axis=1).astype(jnp.bfloat16)


def back_kernel(even_ref, spread_in, keep_ref, got_ref, cot_ref, mask_ref, kernel_ref, spread_ref, out_ref, cols_ref, buf_ref):
    del spread_in
    height = cot_ref.shape[0]
    edge_columns(even_ref[0] == 1, keep_ref, got_ref, cols_ref)
    add_edges(cols_ref, kernel_ref, spread_ref, height, True, DEEP)

    def one(row, _):
        for t in range(64 // DEEP):
            buf_ref[pl.ds(t, DEEP, stride=64 // DEEP), :] = spread_ref[pl.ds(row * 64 + t * DEEP, DEEP), :]
        spread = buf_ref[0:64, :]
        out_ref[row] = (
            (cot_ref[row].astype(jnp.float32) + spread) * mask_ref[row].astype(jnp.float32)
        ).astype(jnp.bfloat16)
        return 0

    lax.fori_loop(0, height, one, 0)


def fold_kernel(rows, per, parts_ref, out_ref):
    total = jnp.sum(parts_ref[...].astype(jnp.float32), axis=0)
    small = total[rows : rows + per] + total[rows + per : rows + 2 * per]
    high = small.astype(jnp.bfloat16).astype(jnp.float32)
    pieces = [total[0:rows], high, small - high]
    if total.shape[0] > rows + 2 * per:
        pieces.append(jnp.zeros((total.shape[0] - rows - 2 * per, 128), jnp.float32))
    total = jnp.concatenate(pieces, axis=0).astype(jnp.bfloat16)
    out_ref[...] = jnp.broadcast_to(total[None], out_ref.shape)


def unpack_kernel(factor, all_ref, kernel_ref, bias_ref, gain_ref, shift_ref, in_ref, b_ref, out_ref):
    parts = all_ref.shape[0]
    rows = 1024 // parts
    each = 128 // rows
    for q in range(4):
        block = all_ref[q * each : (q + 1) * each, 0:rows, :].astype(jnp.float32)
        in_ref[:, q * 128 : (q + 1) * 128] = block.reshape(128, 128) * factor
    for q in range(4):
        block = all_ref[(4 + q) * each : (5 + q) * each, 0:rows, :].astype(jnp.float32)
        out_ref[q * 128 : (q + 1) * 128, :] = block.reshape(128, 128).T * factor
    per = SMALL // parts
    both = all_ref[:, rows:, :].astype(jnp.float32)
    small = (both[:, 0:per] + both[:, per : 2 * per]) * factor

    def row(r):
        return small[r // (SMALL // parts), r % (SMALL // parts)]

    for a in range(KS):
        for b in range(KS):
            kernel_ref[a, b] = row(a * KS + b)
    for at, ref in enumerate((bias_ref, gain_ref, shift_ref)):
        ref[0] = row(KS * KS + at)
    for q in range(4):
        b_ref[0, q * 128 : (q + 1) * 128] = row(KS * KS + 3 + q)


def groups():
    count_lon, count_lat = lax.axis_size("lon"), lax.axis_size("lat")
    plane = [[[] for _ in range(count_lat // 2)] for _ in range(2)]
    column = [[[] for _ in range(2)] for _ in range(count_lon // 2)]
    for lon in range(count_lon):
        for lat in range(count_lat):
            at = lon * count_lat + lat
            plane[lon % 2][lat // 2].append(at)
            column[lon // 2][lat % 2].append(at)
    return [g for part in plane for g in part], [g for part in column for g in part]


def exchange(parts, members):
    return lax.all_to_all(parts, ("lon", "lat"), 0, 0, tiled=True, axis_index_groups=members)


def summed(packed):
    count_lon = lax.axis_size("lon")
    plane, column = groups()

    def fold(parts, count):
        return pl.pallas_call(
            functools.partial(fold_kernel, 1024 // count_lon, SMALL // count_lon),
            out_shape=jax.ShapeDtypeStruct((count,) + parts.shape[1:], jnp.bfloat16),
            in_specs=[VMEM],
            out_specs=VMEM,
            name="fold",
        compiler_params=PARAMS,
        )(parts)

    held = exchange(packed, plane)
    held = fold(held, len(column[0]))
    held = exchange(held, column)
    held = fold(held, len(plane[0]))
    return exchange(held, plane)


def lat_halo(top, bottom):
    count = lax.axis_size("lat")
    up = [(i, i + 1) for i in range(count - 1)]
    down = [(i + 1, i) for i in range(count - 1)]
    south = lax.ppermute(top, "lat", up)
    north = lax.ppermute(bottom, "lat", down)
    return south, north


def onward_pairs():
    count = lax.axis_size("lon")
    return [(i, (i + 2) % count) for i in range(0, count, 2)] + [(i, (i - 2) % count) for i in range(1, count, 2)]


def lon_halo(even, south, block, north):
    tall = block.shape[0] + 2 * HALF + 2
    strips = pl.pallas_call(
        strip_kernel,
        out_shape=jax.ShapeDtypeStruct((2, HALF, tall, 128), jnp.bfloat16),
        in_specs=[SMEM, VMEM, VMEM, VMEM],
        out_specs=VMEM,
        scratch_shapes=[pltpu.VMEM((tall * SUB, 128), jnp.float32)] * 2,
        name="strips",
        compiler_params=PARAMS,
    )(even, south, block, north)
    swapped = lax.ppermute(strips, "lon", [(i, i ^ 1) for i in range(lax.axis_size("lon"))])
    got = lax.ppermute(swapped[1], "lon", onward_pairs())
    return swapped[0], got


def first_conv(south, block, north, kernel, rows):
    height, across, channels = block.shape
    tiles = (height + 2 * HALF + 2) * WIDE * SUB
    return pl.pallas_call(
        functools.partial(conv_kernel, rows),
        out_shape=(
            pltpu.VMEM((height * across, channels), jnp.float32),
            pltpu.VMEM((tiles, channels), jnp.float32),
        ),
        in_specs=[VMEM] * 4,
        out_specs=[VMEM] * 2,
        scratch_shapes=[pltpu.VMEM((SUB * SUB + 2 * SUB, channels), jnp.float32)],
        compiler_params=PARAMS,
        name="conv",
    )(south, block, north, kernel)


def f32(*shape):
    return jax.ShapeDtypeStruct(shape, jnp.float32)


def body(cells, ocean_mask, cotangent, kernel, conv_bias, gain, shift, w_in, b_in, w_out, chunk=8):
    height, across, channels = cells.shape
    ocean = jnp.broadcast_to(ocean_mask.astype(jnp.bfloat16)[..., None], cells.shape)
    masked = cells * ocean
    out_grad = cotangent * ocean
    even = (1 - lax.axis_index("lon") % 2).astype(jnp.int32).reshape(1)
    south, north = lat_halo(masked[-HALF:], masked[:HALF])
    keep, got = lon_halo(even, south, masked, north)
    early = height * 9 // 16
    conv, tiles = first_conv(south, masked, north, kernel, early)
    conv = pl.pallas_call(
        functools.partial(rest_kernel, early),
        out_shape=pltpu.VMEM(conv.shape, jnp.float32),
        in_specs=[VMEM] * 3,
        out_specs=VMEM,
        input_output_aliases={0: 0},
        compiler_params=PARAMS,
        name="rest",
    )(*[pltpu.with_memory_space_constraint(x, pltpu.VMEM) for x in (conv, tiles)], kernel)
    parts = lax.axis_size("lon")
    hidden = w_in.shape[1]
    _, _, conv_grad, packed = pl.pallas_call(
        functools.partial(block_kernel, chunk),
        out_shape=(
            pltpu.VMEM(conv.shape, jnp.float32), pltpu.VMEM(tiles.shape, jnp.float32),
            jax.ShapeDtypeStruct(cells.shape, jnp.bfloat16),
            jax.ShapeDtypeStruct((parts, 1024 // parts + max(8, 2 * SMALL // parts), channels), jnp.bfloat16),
        ),
        in_specs=[SMEM] + [VMEM] * 12,
        out_specs=[VMEM] * 4,
        scratch_shapes=[
            pltpu.VMEM((2 * HALF, height + 2 * HALF + 2, channels), jnp.float32),
            pltpu.VMEM((80, channels), jnp.float32),
            pltpu.VMEM((chunk, SUB, SUB, channels), jnp.float32),
            pltpu.VMEM((chunk * 64, channels), jnp.float32),
            pltpu.VMEM((KS, KS, SUB, channels), jnp.float32),
            pltpu.VMEM((SMALL, channels), jnp.float32),
            pltpu.VMEM((SUB, channels), jnp.float32),
            pltpu.VMEM((SUB, channels), jnp.float32),
            pltpu.VMEM((SUB, channels), jnp.float32),
            pltpu.VMEM((channels + 16, hidden), jnp.float32),
            pltpu.VMEM((channels, hidden), jnp.float32),
        ],
        input_output_aliases={1: 0, 2: 1},
        name="block",
        compiler_params=PARAMS,
    )(
        even, *[pltpu.with_memory_space_constraint(x, pltpu.VMEM) for x in (conv, tiles)], keep, got, out_grad, kernel, conv_bias.reshape(1, -1), gain.reshape(1, -1),
        shift.reshape(1, -1), w_in, b_in.reshape(1, -1), w_out,
    )
    total = summed(packed)
    south, north = lat_halo(conv_grad[-HALF:], conv_grad[:HALF])
    keep, got = lon_halo(even, south, conv_grad, north)
    spread = pl.pallas_call(
        back_conv_kernel,
        out_shape=pltpu.VMEM((height * across, channels), jnp.float32),
        in_specs=[VMEM] * 4,
        out_specs=VMEM,
        scratch_shapes=[
            pltpu.VMEM(((height + 2 * HALF + 2) * WIDE * SUB, channels), jnp.float32),
            pltpu.VMEM((SUB * SUB + 2 * SUB, channels), jnp.float32),
        ],
        compiler_params=PARAMS,
        name="back_conv",
    )(south, conv_grad, north, kernel)
    _, cells_grad = pl.pallas_call(
        back_kernel,
        out_shape=(pltpu.VMEM(spread.shape, jnp.float32), jax.ShapeDtypeStruct(cells.shape, jnp.bfloat16)),
        in_specs=[SMEM] + [VMEM] * 6,
        out_specs=[VMEM] * 2,
        scratch_shapes=[
            pltpu.VMEM((2 * HALF, height + 2 * HALF + 2, channels), jnp.float32),
            pltpu.VMEM((80, channels), jnp.float32),
        ],
        input_output_aliases={1: 0},
        name="back",
        compiler_params=PARAMS,
    )(even, pltpu.with_memory_space_constraint(spread, pltpu.VMEM), keep, got, cotangent, ocean, kernel)
    count = height * across * lax.axis_size("lon") * lax.axis_size("lat")
    gk, gb, gg, gs, gi, gh, go = pl.pallas_call(
        functools.partial(unpack_kernel, count ** -0.5),
        out_shape=(
            f32(KS, KS, channels), f32(1, channels), f32(1, channels), f32(1, channels),
            f32(channels, hidden), f32(1, hidden), f32(hidden, channels),
        ),
        in_specs=[VMEM],
        out_specs=[VMEM] * 7,
        name="unpack",
        compiler_params=PARAMS,
    )(total)
    return cells_grad, gk, gb[0], gg[0], gs[0], gi, gh[0], go


def solution(mesh):
    whole = P("lat", "lon", None)
    in_specs = (whole, P("lat", "lon"), whole) + (P(),) * 7
    out_specs = (whole,) + (P(),) * 7
    return jax.shard_map(body, mesh=mesh, in_specs=in_specs, out_specs=out_specs, check_vma=False)
```

```python
import functools

import jax
import jax.numpy as jnp
from jax import lax
from jax.experimental import pallas as pl
from jax.experimental.pallas import tpu as pltpu
from jax.sharding import PartitionSpec as P


KS = 7
HALF = 3
SMALL = 64
WIDE = 14
SUB = 8
ROOT = 0.7978845608028654
CUBE = 0.044715
VMEM = pl.BlockSpec(memory_space=pltpu.VMEM)
PARAMS = pltpu.CompilerParams(vmem_limit_bytes=28 << 20)
SMEM = pl.BlockSpec(memory_space=pltpu.SMEM)


def spread_row(row_of, row, tiles_ref, buf_ref):
    buf_ref[HALF : HALF + 64, :] = row_of.astype(jnp.float32)
    for tap in range(WIDE):
        tiles_ref[pl.ds(row * (WIDE * SUB) + tap * SUB, SUB), :] = buf_ref[pl.ds(tap, SUB, stride=SUB), :]


def spread_all(south_ref, block_ref, north_ref, tiles_ref, buf_ref, rows=None):
    height = block_ref.shape[0]
    buf_ref[...] = jnp.zeros_like(buf_ref)
    for row in range(HALF):
        spread_row(south_ref[row], row, tiles_ref, buf_ref)
        if rows is None:
            spread_row(north_ref[row], height + HALF + row, tiles_ref, buf_ref)

    def one(row, _):
        spread_row(block_ref[row], row + HALF, tiles_ref, buf_ref)
        return 0

    lax.fori_loop(0, height if rows is None else rows, one, 0)
    if rows is not None:
        return
    last = (height + 2 * HALF) * WIDE * SUB
    tiles_ref[last:, :] = jnp.zeros((2 * WIDE * SUB, 128), jnp.float32)


def tile(tiles_ref, row, t):
    return tiles_ref[pl.ds(row * (WIDE * SUB) + t * SUB, SUB), :]


def tap_weight(kernel_ref, a, b, flip):
    if flip:
        a, b = KS - 1 - a, KS - 1 - b
    return jnp.broadcast_to(kernel_ref[a, b : b + 1, :], (SUB, 128))


def conv_rows(tiles_ref, kernel_ref, out_ref, start, stop, flip, base=0):
    def one(row, _):
        total = [None] * SUB
        for a in range(KS):
            cells = [tile(tiles_ref, row + a - base, t) for t in range(WIDE)]
            for b in range(KS):
                weight = tap_weight(kernel_ref, a, b, flip)
                for t in range(SUB):
                    term = weight * cells[t + b]
                    total[t] = term if total[t] is None else total[t] + term
        for t in range(SUB):
            out_ref[pl.ds(row * 64 + t * SUB, SUB), :] = total[t]
        return 0

    lax.fori_loop(start, stop, one, 0)


def edge_columns(even, keep_ref, got_ref, cols_ref):
    for c in range(HALF):
        keep = keep_ref[c].astype(jnp.float32)
        got = got_ref[c].astype(jnp.float32)
        cols_ref[c] = jnp.where(even, got, keep)
        cols_ref[HALF + c] = jnp.where(even, keep, got)


def add_edges(cols_ref, kernel_ref, out_ref, height, flip):
    for west in (True, False):
        for at in range(HALF):
            first = at * SUB if west else (SUB - HALF + at) * SUB + SUB - 1
            totals = [None] * (height // SUB)
            for a in range(KS):
                for b in range(KS):
                    c = at + b if west else at + b - HALF
                    if not ((0 <= c < HALF) if west else (HALF <= c < 2 * HALF)):
                        continue
                    weight = tap_weight(kernel_ref, a, b, flip)
                    for block in range(height // SUB):
                        term = weight * cols_ref[c, pl.ds(block * SUB + a, SUB), :]
                        totals[block] = term if totals[block] is None else totals[block] + term
            for block in range(height // SUB):
                place = pl.ds(block * SUB * 64 + first, SUB, stride=64)
                out_ref[place, :] = out_ref[place, :] + totals[block]


def gather_row(tiles, buf_ref):
    for t in range(SUB):
        buf_ref[pl.ds(t, SUB, stride=SUB), :] = tiles[t]
    return buf_ref[0 : SUB * SUB, :]


def mask_kernel(cells_ref, mask_ref, cot_ref, masked_ref, out_grad_ref, ocean_ref, top_ref, bottom_ref):
    height = cells_ref.shape[0]
    columns = mask_ref[...].astype(jnp.float32).T
    for row in range(height):
        ocean = jnp.broadcast_to(columns[:, row : row + 1], cells_ref.shape[1:])
        masked_ref[row] = (cells_ref[row].astype(jnp.float32) * ocean).astype(jnp.bfloat16)
        out_grad_ref[row] = (cot_ref[row].astype(jnp.float32) * ocean).astype(jnp.bfloat16)
        ocean_ref[row] = ocean.astype(jnp.bfloat16)
    top_ref[...] = masked_ref[height - HALF :]
    bottom_ref[...] = masked_ref[0:HALF]


def strip_kernel(even_ref, south_ref, block_ref, north_ref, out_ref, low_ref, high_ref):
    height = block_ref.shape[0]

    def put(at, row_of):
        low_ref[pl.ds(at * SUB, SUB), :] = row_of[0:SUB].astype(jnp.float32)
        high_ref[pl.ds(at * SUB, SUB), :] = row_of[64 - SUB : 64].astype(jnp.float32)

    for row in range(HALF):
        put(row, south_ref[row])
        put(row + height + HALF, north_ref[row])

    def one(step, _):
        for r in range(SUB):
            put(step * SUB + r + HALF, block_ref[step * SUB + r])
        return 0

    lax.fori_loop(0, height // SUB, one, 0)
    tall = height + 2 * HALF + 2
    low_ref[(tall - 2) * SUB :, :] = jnp.zeros((2 * SUB, 128), jnp.float32)
    high_ref[(tall - 2) * SUB :, :] = jnp.zeros((2 * SUB, 128), jnp.float32)
    even = even_ref[0] == 1
    for c in range(HALF):
        west = low_ref[pl.ds(c, tall, stride=SUB), :]
        east = high_ref[pl.ds(SUB - HALF + c, tall, stride=SUB), :]
        out_ref[0, c] = jnp.where(even, east, west).astype(jnp.bfloat16)
        out_ref[1, c] = jnp.where(even, west, east).astype(jnp.bfloat16)


def rest_kernel(start, flip, conv_in, tiles_ref, kernel_ref, out_ref):
    del conv_in
    conv_rows(tiles_ref, kernel_ref, out_ref, start, out_ref.shape[0] // 64, flip)


def back_rest_kernel(start, spread_in, block_ref, north_ref, kernel_ref, out_ref, tiles_ref, buf_ref):
    del spread_in
    height = block_ref.shape[0]
    buf_ref[...] = jnp.zeros_like(buf_ref)

    def one(row, _):
        spread_row(block_ref[row], row + HALF - start, tiles_ref, buf_ref)
        return 0

    lax.fori_loop(start - HALF, height, one, 0)
    for row in range(HALF):
        spread_row(north_ref[row], height + HALF + row - start, tiles_ref, buf_ref)
    conv_rows(tiles_ref, kernel_ref, out_ref, start, height, True, start)


def conv_kernel(rows, flip, south_ref, block_ref, north_ref, kernel_ref, out_ref, tiles_ref, buf_ref):
    spread_all(south_ref, block_ref, north_ref, tiles_ref, buf_ref, rows + HALF if flip else None)
    conv_rows(tiles_ref, kernel_ref, out_ref, 0, rows, flip)


def block_kernel(
    chunk,
    even_ref, conv_in, tiles_in, keep_ref, got_ref, out_grad_ref,
    kernel_ref, bias_ref, gain_ref, shift_ref, w_in_ref, b_in_ref, w_out_ref,
    conv_ref, tiles_ref, conv_grad_ref, top_ref, bottom_ref, packed_ref,
    cols_ref, buf_ref, og_tiles, round_ref, taps_ref, small_ref,
    bias_sum, gain_sum, shift_sum, grad_in, grad_out,
):
    del conv_in, tiles_in
    height = out_grad_ref.shape[0]
    cells = chunk * 64
    edge_columns(even_ref[0] == 1, keep_ref, got_ref, cols_ref)
    span = WIDE * SUB
    for c in range(HALF):
        for block in range((height + 2 * HALF + 2) // SUB):
            rows = pl.ds(block * SUB, SUB)
            start = block * SUB * span
            tiles_ref[pl.ds(start + c * SUB, SUB, stride=span), :] = cols_ref[c, rows, :]
            tiles_ref[pl.ds(start + (SUB + HALF + c) * SUB + SUB - 1, SUB, stride=span), :] = cols_ref[HALF + c, rows, :]
    add_edges(cols_ref, kernel_ref, conv_ref, height, False)
    for ref in (bias_sum, gain_sum, shift_sum, grad_in, grad_out, taps_ref):
        ref[...] = jnp.zeros_like(ref)
    bias = bias_ref[...]
    gain = gain_ref[...]
    shift = shift_ref[...]
    b_in = b_in_ref[...]
    w_half = w_out_ref[...] * jnp.bfloat16(0.5)

    ones = jnp.where(
        lax.broadcasted_iota(jnp.int32, (16, cells), 0) == 0, 1.0, 0.0
    ).astype(jnp.bfloat16)

    def taps(first):
        for r in range(chunk):
            row = first + r
            grads = [round_ref[r * 64 + t * SUB : r * 64 + (t + 1) * SUB, :] for t in range(SUB)]
            for a in range(KS):
                near = [tile(tiles_ref, row + a, t) for t in range(WIDE)]
                for b in range(KS):
                    total = taps_ref[a, b]
                    for t in range(SUB):
                        total = total + grads[t] * near[t + b]
                    taps_ref[a, b] = total

    def one(step, pending):
        first = step * chunk
        if pending is not None:
            taps(first - chunk)
        for r in range(chunk):
            buf_ref[0:64, :] = out_grad_ref[first + r].astype(jnp.float32)
            for t in range(SUB):
                og_tiles[r, t] = buf_ref[pl.ds(t, SUB, stride=SUB), :]
        conv = conv_ref[pl.ds(first * 64, cells), :] + bias
        out_grad = og_tiles[...].reshape(cells, 128).astype(jnp.bfloat16)
        average = jnp.mean(conv, axis=-1, keepdims=True)
        centred = conv - average
        variance = jnp.mean(centred * centred, axis=-1, keepdims=True)
        inverse = lax.rsqrt(variance + 1e-06)
        scaled = centred * inverse
        normed = (scaled * gain + shift).astype(jnp.bfloat16)
        v = jnp.dot(normed, w_in_ref[...], preferred_element_type=jnp.float32) + b_in
        act_grad = lax.dot_general(
            out_grad, w_half, (((1,), (1,)), ((), ())), preferred_element_type=jnp.float32
        )
        square = v * v
        curve = jnp.tanh(v * (ROOT + (ROOT * CUBE) * square))
        above = 1.0 + curve
        twice = (v * above).astype(jnp.bfloat16)
        rise = v * (ROOT + (3 * ROOT * CUBE) * square)
        hidden = (act_grad * (above * (1.0 + (1.0 - curve) * rise))).astype(jnp.bfloat16)
        grad_out[...] += lax.dot_general(
            out_grad, twice, (((0,), (0,)), ((), ())), preferred_element_type=jnp.float32
        )
        grad_in[...] += jnp.dot(
            jnp.concatenate([normed.T, ones], axis=0), hidden, preferred_element_type=jnp.float32
        )
        norm_grad = lax.dot_general(
            hidden, w_in_ref[...], (((1,), (1,)), ((), ())), preferred_element_type=jnp.float32
        )
        gain_sum[...] += jnp.sum((norm_grad * scaled).reshape(-1, SUB, 128), axis=0)
        shift_sum[...] += jnp.sum(norm_grad.reshape(-1, SUB, 128), axis=0)
        weighted = norm_grad * gain
        conv_grad = inverse * (
            weighted
            - jnp.mean(weighted, axis=-1, keepdims=True)
            - scaled * jnp.mean(weighted * scaled, axis=-1, keepdims=True)
        )
        rounded = conv_grad.astype(jnp.bfloat16).astype(jnp.float32)
        bias_sum[...] += jnp.sum(rounded.reshape(-1, SUB, 128), axis=0)
        round_ref[...] = rounded
        for r in range(chunk):
            natural = gather_row(
                [rounded[r * 64 + t * SUB : r * 64 + (t + 1) * SUB] for t in range(SUB)], buf_ref
            )
            conv_grad_ref[first + r] = natural.astype(jnp.bfloat16)
        return 0

    one(0, None)
    lax.fori_loop(1, height // chunk, one, 0)
    top_ref[...] = conv_grad_ref[height - HALF :]
    bottom_ref[...] = conv_grad_ref[0:HALF]
    taps(height - chunk)
    pack(taps_ref, bias_sum, gain_sum, shift_sum, grad_in, grad_out, packed_ref, small_ref)


def pack(taps_ref, bias_sum, gain_sum, shift_sum, grad_in, grad_out, out_ref, small_ref):
    small_ref[...] = jnp.zeros_like(small_ref)
    for a in range(KS):
        for b in range(KS):
            small_ref[a * KS + b] = jnp.sum(taps_ref[a, b], axis=0)
    for at, ref in enumerate((bias_sum, gain_sum, shift_sum)):
        small_ref[KS * KS + at] = jnp.sum(ref[...], axis=0)
    for q in range(4):
        small_ref[KS * KS + 3 + q] = grad_in[128, q * 128 : (q + 1) * 128]
    parts = out_ref.shape[0]
    rows = 1024 // parts
    each = 128 // rows
    for at, ref, scale in ((0, grad_in, 1.0), (4, grad_out, 0.5)):
        for q in range(4):
            block = ref[0:128, q * 128 : (q + 1) * 128].reshape(each, rows, 128)
            out_ref[(at + q) * each : (at + q + 1) * each, 0:rows, :] = (block * scale).astype(jnp.bfloat16)
    per = SMALL // parts
    spare = out_ref.shape[1] - rows - 2 * per
    small = small_ref[...].reshape(parts, per, 128)
    high = small.astype(jnp.bfloat16).astype(jnp.float32)
    pieces = [high, small - high] + ([jnp.zeros((parts, spare, 128), jnp.float32)] if spare else [])
    out_ref[:, rows:, :] = jnp.concatenate(pieces, axis=1).astype(jnp.bfloat16)


def back_kernel(even_ref, spread_in, keep_ref, got_ref, cot_ref, mask_ref, kernel_ref, spread_ref, out_ref, cols_ref, buf_ref):
    del spread_in
    height = cot_ref.shape[0]
    edge_columns(even_ref[0] == 1, keep_ref, got_ref, cols_ref)
    add_edges(cols_ref, kernel_ref, spread_ref, height, True)

    def one(step, _):
        for r in range(4):
            row = step * 4 + r
            for t in range(SUB):
                buf_ref[pl.ds(r * 64 + t, SUB, stride=SUB), :] = spread_ref[pl.ds(row * 64 + t * SUB, SUB), :]
        for r in range(4):
            row = step * 4 + r
            spread = buf_ref[r * 64 : (r + 1) * 64, :]
            out_ref[row] = (
                (cot_ref[row].astype(jnp.float32) + spread) * mask_ref[row].astype(jnp.float32)
            ).astype(jnp.bfloat16)
        return 0

    lax.fori_loop(0, height // 4, one, 0)


def fold_kernel(rows, per, parts_ref, out_ref):
    total = jnp.sum(parts_ref[...].astype(jnp.float32), axis=0)
    small = total[rows : rows + per] + total[rows + per : rows + 2 * per]
    high = small.astype(jnp.bfloat16).astype(jnp.float32)
    pieces = [total[0:rows], high, small - high]
    if total.shape[0] > rows + 2 * per:
        pieces.append(jnp.zeros((total.shape[0] - rows - 2 * per, 128), jnp.float32))
    total = jnp.concatenate(pieces, axis=0).astype(jnp.bfloat16)
    out_ref[...] = jnp.broadcast_to(total[None], out_ref.shape)


def unpack_kernel(factor, all_ref, kernel_ref, bias_ref, gain_ref, shift_ref, in_ref, b_ref, out_ref):
    parts = all_ref.shape[0]
    rows = 1024 // parts
    each = 128 // rows
    for q in range(4):
        block = all_ref[q * each : (q + 1) * each, 0:rows, :].astype(jnp.float32)
        in_ref[:, q * 128 : (q + 1) * 128] = block.reshape(128, 128) * factor
    for q in range(4):
        block = all_ref[(4 + q) * each : (5 + q) * each, 0:rows, :].astype(jnp.float32)
        out_ref[q * 128 : (q + 1) * 128, :] = block.reshape(128, 128).T * factor
    per = SMALL // parts
    both = all_ref[:, rows:, :].astype(jnp.float32)
    small = (both[:, 0:per] + both[:, per : 2 * per]) * factor

    def row(r):
        return small[r // (SMALL // parts), r % (SMALL // parts)]

    for a in range(KS):
        for b in range(KS):
            kernel_ref[a, b] = row(a * KS + b)
    for at, ref in enumerate((bias_ref, gain_ref, shift_ref)):
        ref[0] = row(KS * KS + at)
    for q in range(4):
        b_ref[0, q * 128 : (q + 1) * 128] = row(KS * KS + 3 + q)


def groups():
    count_lon, count_lat = lax.axis_size("lon"), lax.axis_size("lat")
    plane = [[[] for _ in range(count_lat // 2)] for _ in range(2)]
    column = [[[] for _ in range(2)] for _ in range(count_lon // 2)]
    for lon in range(count_lon):
        for lat in range(count_lat):
            at = lon * count_lat + lat
            plane[lon % 2][lat // 2].append(at)
            column[lon // 2][lat % 2].append(at)
    return [g for part in plane for g in part], [g for part in column for g in part]


def exchange(parts, members):
    return lax.all_to_all(parts, ("lon", "lat"), 0, 0, tiled=True, axis_index_groups=members)


def summed(packed):
    count_lon = lax.axis_size("lon")
    plane, column = groups()

    def fold(parts, count):
        return pl.pallas_call(
            functools.partial(fold_kernel, 1024 // count_lon, SMALL // count_lon),
            out_shape=jax.ShapeDtypeStruct((count,) + parts.shape[1:], jnp.bfloat16),
            in_specs=[VMEM],
            out_specs=VMEM,
            name="fold",
        compiler_params=PARAMS,
        )(parts)

    held = exchange(packed, plane)
    held = fold(held, len(column[0]))
    held = exchange(held, column)
    held = fold(held, len(plane[0]))
    return exchange(held, plane)


def lat_halo(top, bottom):
    count = lax.axis_size("lat")
    up = [(i, i + 1) for i in range(count - 1)]
    down = [(i + 1, i) for i in range(count - 1)]
    south = lax.ppermute(top, "lat", up)
    north = lax.ppermute(bottom, "lat", down)
    return south, north


def onward_pairs():
    count = lax.axis_size("lon")
    return [(i, (i + 2) % count) for i in range(0, count, 2)] + [(i, (i - 2) % count) for i in range(1, count, 2)]


def lon_halo(even, south, block, north):
    tall = block.shape[0] + 2 * HALF + 2
    strips = pl.pallas_call(
        strip_kernel,
        out_shape=jax.ShapeDtypeStruct((2, HALF, tall, 128), jnp.bfloat16),
        in_specs=[SMEM, VMEM, VMEM, VMEM],
        out_specs=VMEM,
        scratch_shapes=[pltpu.VMEM((tall * SUB, 128), jnp.float32)] * 2,
        name="strips",
        compiler_params=PARAMS,
    )(even, south, block, north)
    swapped = lax.ppermute(strips, "lon", [(i, i ^ 1) for i in range(lax.axis_size("lon"))])
    got = lax.ppermute(swapped[1], "lon", onward_pairs())
    return swapped[0], got


def first_conv(south, block, north, kernel, rows, flip):
    height, across, channels = block.shape
    tiles = pltpu.VMEM(((height + 2 * HALF + 2) * WIDE * SUB, channels), jnp.float32)
    out = pltpu.VMEM((height * across, channels), jnp.float32)
    buf = pltpu.VMEM((SUB * SUB + 2 * SUB, channels), jnp.float32)
    return pl.pallas_call(
        functools.partial(conv_kernel, rows, flip),
        out_shape=out if flip else (out, tiles),
        in_specs=[VMEM] * 4,
        out_specs=VMEM if flip else [VMEM] * 2,
        scratch_shapes=[tiles, buf] if flip else [buf],
        compiler_params=PARAMS,
        name="back_conv" if flip else "conv",
    )(south, block, north, kernel)


def last_conv(conv, tiles, kernel, rows, flip):
    return pl.pallas_call(
        functools.partial(rest_kernel, rows, flip),
        out_shape=pltpu.VMEM(conv.shape, jnp.float32),
        in_specs=[VMEM] * 3,
        out_specs=VMEM,
        input_output_aliases={0: 0},
        compiler_params=PARAMS,
        name="back_rest" if flip else "rest",
    )(*[pltpu.with_memory_space_constraint(x, pltpu.VMEM) for x in (conv, tiles)], kernel)


def f32(*shape):
    return jax.ShapeDtypeStruct(shape, jnp.float32)


def body(cells, ocean_mask, cotangent, kernel, conv_bias, gain, shift, w_in, b_in, w_out, chunk=8):
    height, across, channels = cells.shape
    whole = jax.ShapeDtypeStruct(cells.shape, jnp.bfloat16)
    strip = jax.ShapeDtypeStruct((HALF, across, channels), jnp.bfloat16)
    masked, out_grad, ocean, top, bottom = pl.pallas_call(
        mask_kernel,
        out_shape=(whole, whole, whole, strip, strip),
        in_specs=[VMEM] * 3,
        out_specs=[VMEM] * 5,
        compiler_params=PARAMS,
        name="mask",
    )(cells, ocean_mask, cotangent)
    even = (1 - lax.axis_index("lon") % 2).astype(jnp.int32).reshape(1)
    south, north = lat_halo(top, bottom)
    keep, got = lon_halo(even, south, masked, north)
    early = height * 9 // 16
    conv, tiles = first_conv(south, masked, north, kernel, early, False)
    conv = last_conv(conv, tiles, kernel, early, False)
    parts = lax.axis_size("lon")
    hidden = w_in.shape[1]
    _, _, conv_grad, top, bottom, packed = pl.pallas_call(
        functools.partial(block_kernel, chunk),
        out_shape=(
            pltpu.VMEM(conv.shape, jnp.float32), pltpu.VMEM(tiles.shape, jnp.float32),
            jax.ShapeDtypeStruct(cells.shape, jnp.bfloat16),
            strip, strip,
            jax.ShapeDtypeStruct((parts, 1024 // parts + max(8, 2 * SMALL // parts), channels), jnp.bfloat16),
        ),
        in_specs=[SMEM] + [VMEM] * 12,
        out_specs=[VMEM] * 6,
        scratch_shapes=[
            pltpu.VMEM((2 * HALF, height + 2 * HALF + 2, channels), jnp.float32),
            pltpu.VMEM((80, channels), jnp.float32),
            pltpu.VMEM((chunk, SUB, SUB, channels), jnp.float32),
            pltpu.VMEM((chunk * 64, channels), jnp.float32),
            pltpu.VMEM((KS, KS, SUB, channels), jnp.float32),
            pltpu.VMEM((SMALL, channels), jnp.float32),
            pltpu.VMEM((SUB, channels), jnp.float32),
            pltpu.VMEM((SUB, channels), jnp.float32),
            pltpu.VMEM((SUB, channels), jnp.float32),
            pltpu.VMEM((channels + 16, hidden), jnp.float32),
            pltpu.VMEM((channels, hidden), jnp.float32),
        ],
        input_output_aliases={1: 0, 2: 1},
        name="block",
        compiler_params=PARAMS,
    )(
        even, *[pltpu.with_memory_space_constraint(x, pltpu.VMEM) for x in (conv, tiles)], keep, got, out_grad, kernel, conv_bias.reshape(1, -1), gain.reshape(1, -1),
        shift.reshape(1, -1), w_in, b_in.reshape(1, -1), w_out,
    )
    total = summed(packed)
    south, north = lat_halo(top, bottom)
    keep, got = lon_halo(even, south, conv_grad, north)
    half = height * 15 // 32
    spread = first_conv(south, conv_grad, north, kernel, half, True)
    spread = pl.pallas_call(
        functools.partial(back_rest_kernel, half),
        out_shape=pltpu.VMEM(spread.shape, jnp.float32),
        in_specs=[VMEM] * 4,
        out_specs=VMEM,
        scratch_shapes=[
            pltpu.VMEM(((height + 2 * HALF - half) * WIDE * SUB, channels), jnp.float32),
            pltpu.VMEM((SUB * SUB + 2 * SUB, channels), jnp.float32),
        ],
        input_output_aliases={0: 0},
        compiler_params=PARAMS,
        name="back_rest",
    )(pltpu.with_memory_space_constraint(spread, pltpu.VMEM), conv_grad, north, kernel)
    _, cells_grad = pl.pallas_call(
        back_kernel,
        out_shape=(pltpu.VMEM(spread.shape, jnp.float32), jax.ShapeDtypeStruct(cells.shape, jnp.bfloat16)),
        in_specs=[SMEM] + [VMEM] * 6,
        out_specs=[VMEM] * 2,
        scratch_shapes=[
            pltpu.VMEM((2 * HALF, height + 2 * HALF + 2, channels), jnp.float32),
            pltpu.VMEM((4 * 64, channels), jnp.float32),
        ],
        input_output_aliases={1: 0},
        name="back",
        compiler_params=PARAMS,
    )(even, pltpu.with_memory_space_constraint(spread, pltpu.VMEM), keep, got, cotangent, ocean, kernel)
    count = height * across * lax.axis_size("lon") * lax.axis_size("lat")
    gk, gb, gg, gs, gi, gh, go = pl.pallas_call(
        functools.partial(unpack_kernel, count ** -0.5),
        out_shape=(
            f32(KS, KS, channels), f32(1, channels), f32(1, channels), f32(1, channels),
            f32(channels, hidden), f32(1, hidden), f32(hidden, channels),
        ),
        in_specs=[VMEM],
        out_specs=[VMEM] * 7,
        name="unpack",
        compiler_params=PARAMS,
    )(total)
    return cells_grad, gk, gb[0], gg[0], gs[0], gi, gh[0], go


def solution(mesh):
    whole = P("lat", "lon", None)
    in_specs = (whole, P("lat", "lon"), whole) + (P(),) * 7
    out_specs = (whole,) + (P(),) * 7
    return jax.shard_map(body, mesh=mesh, in_specs=in_specs, out_specs=out_specs, check_vma=False)
```

```python
import functools

import jax
import jax.numpy as jnp
from jax import lax
from jax.experimental import pallas as pl
from jax.experimental.pallas import tpu as pltpu
from jax.sharding import PartitionSpec as P


KS = 7
HALF = 3
SMALL = 64
WIDE = 14
SUB = 8
ROOT = 0.7978845608028654
CUBE = 0.044715
VMEM = pl.BlockSpec(memory_space=pltpu.VMEM)
PARAMS = pltpu.CompilerParams(vmem_limit_bytes=28 << 20)
CONV_PARAMS = pltpu.CompilerParams(vmem_limit_bytes=28 << 20)
SMEM = pl.BlockSpec(memory_space=pltpu.SMEM)


def spread_row(row_of, row, tiles_ref, buf_ref):
    buf_ref[HALF : HALF + 64, :] = row_of.astype(jnp.float32)
    for tap in range(WIDE):
        tiles_ref[pl.ds(row * (WIDE * SUB) + tap * SUB, SUB), :] = buf_ref[pl.ds(tap, SUB, stride=SUB), :]


def spread_all(south_ref, block_ref, north_ref, tiles_ref, buf_ref, rows=None):
    height = block_ref.shape[0]
    buf_ref[...] = jnp.zeros_like(buf_ref)
    for row in range(HALF):
        spread_row(south_ref[row], row, tiles_ref, buf_ref)
        if rows is None:
            spread_row(north_ref[row], height + HALF + row, tiles_ref, buf_ref)

    def one(row, _):
        spread_row(block_ref[row], row + HALF, tiles_ref, buf_ref)
        return 0

    lax.fori_loop(0, height if rows is None else rows, one, 0)
    if rows is not None:
        return
    last = (height + 2 * HALF) * WIDE * SUB
    tiles_ref[last:, :] = jnp.zeros((2 * WIDE * SUB, 128), jnp.float32)


def tile(tiles_ref, row, t):
    return tiles_ref[pl.ds(row * (WIDE * SUB) + t * SUB, SUB), :]


def tap_weight(kernel_ref, a, b, flip):
    if flip:
        a, b = KS - 1 - a, KS - 1 - b
    return jnp.broadcast_to(kernel_ref[a, b : b + 1, :], (SUB, 128))


def conv_rows(tiles_ref, kernel_ref, out_ref, start, stop, flip, base=0):
    def one(step, _):
        first = start + 2 * step
        totals = [[None] * SUB, [None] * SUB]
        for near in range(KS + 1):
            cells = [tile(tiles_ref, first + near - base, t) for t in range(WIDE)]
            for r in range(2):
                a = near - r
                if not 0 <= a < KS:
                    continue
                total = totals[r]
                for b in range(KS):
                    weight = tap_weight(kernel_ref, a, b, flip)
                    for t in range(SUB):
                        term = weight * cells[t + b]
                        total[t] = term if total[t] is None else total[t] + term
        for r in range(2):
            for t in range(SUB):
                out_ref[pl.ds((first + r) * 64 + t * SUB, SUB), :] = totals[r][t]
        return 0

    lax.fori_loop(0, (stop - start) // 2, one, 0)


def edge_columns(even, keep_ref, got_ref, cols_ref):
    for c in range(HALF):
        keep = keep_ref[0, c].astype(jnp.float32)
        got = got_ref[c].astype(jnp.float32)
        cols_ref[c] = jnp.where(even, got, keep)
        cols_ref[HALF + c] = jnp.where(even, keep, got)


def add_edges(cols_ref, kernel_ref, out_ref, height, flip):
    for west in (True, False):
        for at in range(HALF):
            first = at * SUB if west else (SUB - HALF + at) * SUB + SUB - 1
            totals = [None] * (height // SUB)
            for a in range(KS):
                for b in range(KS):
                    c = at + b if west else at + b - HALF
                    if not ((0 <= c < HALF) if west else (HALF <= c < 2 * HALF)):
                        continue
                    weight = tap_weight(kernel_ref, a, b, flip)
                    for block in range(height // SUB):
                        term = weight * cols_ref[c, pl.ds(block * SUB + a, SUB), :]
                        totals[block] = term if totals[block] is None else totals[block] + term
            for block in range(height // SUB):
                place = pl.ds(block * SUB * 64 + first, SUB, stride=64)
                out_ref[place, :] = out_ref[place, :] + totals[block]


def gather_row(tiles, buf_ref):
    for t in range(SUB):
        buf_ref[pl.ds(t, SUB, stride=SUB), :] = tiles[t]
    return buf_ref[0 : SUB * SUB, :]


def onward_kernel(both_ref, out_ref):
    out_ref[...] = both_ref[1]


def strip_kernel(even_ref, south_ref, block_ref, north_ref, out_ref, low_ref, high_ref):
    height = block_ref.shape[0]

    def put(at, row_of):
        low_ref[pl.ds(at * SUB, SUB), :] = row_of[0:SUB].astype(jnp.float32)
        high_ref[pl.ds(at * SUB, SUB), :] = row_of[64 - SUB : 64].astype(jnp.float32)

    for row in range(HALF):
        put(row, south_ref[row])
        put(row + height + HALF, north_ref[row])

    def one(step, _):
        for r in range(SUB):
            put(step * SUB + r + HALF, block_ref[step * SUB + r])
        return 0

    lax.fori_loop(0, height // SUB, one, 0)
    tall = height + 2 * HALF + 2
    low_ref[(tall - 2) * SUB :, :] = jnp.zeros((2 * SUB, 128), jnp.float32)
    high_ref[(tall - 2) * SUB :, :] = jnp.zeros((2 * SUB, 128), jnp.float32)
    even = even_ref[0] == 1
    for c in range(HALF):
        west = low_ref[pl.ds(c, tall, stride=SUB), :]
        east = high_ref[pl.ds(SUB - HALF + c, tall, stride=SUB), :]
        out_ref[0, c] = jnp.where(even, east, west).astype(jnp.bfloat16)
        out_ref[1, c] = jnp.where(even, west, east).astype(jnp.bfloat16)


def rest_kernel(start, flip, conv_in, tiles_ref, kernel_ref, out_ref):
    del conv_in
    conv_rows(tiles_ref, kernel_ref, out_ref, start, out_ref.shape[0] // 64, flip)


def back_rest_kernel(start, spread_in, block_ref, north_ref, kernel_ref, out_ref, tiles_ref, buf_ref):
    del spread_in
    height = block_ref.shape[0]
    buf_ref[...] = jnp.zeros_like(buf_ref)

    def one(row, _):
        spread_row(block_ref[row], row + HALF - start, tiles_ref, buf_ref)
        return 0

    lax.fori_loop(start - HALF, height, one, 0)
    for row in range(HALF):
        spread_row(north_ref[row], height + HALF + row - start, tiles_ref, buf_ref)
    conv_rows(tiles_ref, kernel_ref, out_ref, start, height, True, start)


def conv_kernel(rows, flip, south_ref, block_ref, north_ref, kernel_ref, out_ref, tiles_ref, buf_ref):
    spread_all(south_ref, block_ref, north_ref, tiles_ref, buf_ref, rows + HALF if flip else None)
    conv_rows(tiles_ref, kernel_ref, out_ref, 0, rows, flip)


def block_kernel(
    chunk,
    even_ref, conv_in, tiles_in, keep_ref, got_ref, out_grad_ref,
    kernel_ref, bias_ref, gain_ref, shift_ref, w_in_ref, b_in_ref, w_out_ref,
    conv_ref, tiles_ref, conv_grad_ref, top_ref, bottom_ref, packed_ref,
    cols_ref, buf_ref, og_tiles, round_ref, taps_ref, small_ref,
    bias_sum, gain_sum, shift_sum, grad_in, grad_out,
):
    del conv_in, tiles_in
    height = out_grad_ref.shape[0]
    cells = chunk * 64
    edge_columns(even_ref[0] == 1, keep_ref, got_ref, cols_ref)
    span = WIDE * SUB
    for c in range(HALF):
        for block in range((height + 2 * HALF + 2) // SUB):
            rows = pl.ds(block * SUB, SUB)
            start = block * SUB * span
            tiles_ref[pl.ds(start + c * SUB, SUB, stride=span), :] = cols_ref[c, rows, :]
            tiles_ref[pl.ds(start + (SUB + HALF + c) * SUB + SUB - 1, SUB, stride=span), :] = cols_ref[HALF + c, rows, :]
    add_edges(cols_ref, kernel_ref, conv_ref, height, False)
    for ref in (bias_sum, gain_sum, shift_sum, grad_in, grad_out, taps_ref):
        ref[...] = jnp.zeros_like(ref)
    bias = bias_ref[...]
    gain = gain_ref[...]
    shift = shift_ref[...]
    b_in = b_in_ref[...]
    w_half = w_out_ref[...] * jnp.bfloat16(0.5)

    ones = jnp.where(
        lax.broadcasted_iota(jnp.int32, (16, cells), 0) == 0, 1.0, 0.0
    ).astype(jnp.bfloat16)

    def taps(first):
        for r in range(chunk):
            row = first + r
            grads = [round_ref[r * 64 + t * SUB : r * 64 + (t + 1) * SUB, :] for t in range(SUB)]
            for a in range(KS):
                near = [tile(tiles_ref, row + a, t) for t in range(WIDE)]
                for b in range(KS):
                    total = taps_ref[a, b]
                    for t in range(SUB):
                        total = total + grads[t] * near[t + b]
                    taps_ref[a, b] = total

    def one(step, pending):
        first = step * chunk
        if pending is not None:
            taps(first - chunk)
        for r in range(chunk):
            buf_ref[0:64, :] = out_grad_ref[first + r].astype(jnp.float32)
            for t in range(SUB):
                og_tiles[r, t] = buf_ref[pl.ds(t, SUB, stride=SUB), :]
        conv = conv_ref[pl.ds(first * 64, cells), :] + bias
        out_grad = og_tiles[...].reshape(cells, 128).astype(jnp.bfloat16)
        average = jnp.mean(conv, axis=-1, keepdims=True)
        centred = conv - average
        variance = jnp.mean(centred * centred, axis=-1, keepdims=True)
        inverse = lax.rsqrt(variance + 1e-06)
        scaled = centred * inverse
        normed = (scaled * gain + shift).astype(jnp.bfloat16)
        v = jnp.dot(normed, w_in_ref[...], preferred_element_type=jnp.float32) + b_in
        act_grad = lax.dot_general(
            out_grad, w_half, (((1,), (1,)), ((), ())), preferred_element_type=jnp.float32
        )
        square = v * v
        curve = jnp.tanh(v * (ROOT + (ROOT * CUBE) * square))
        above = 1.0 + curve
        twice = (v * above).astype(jnp.bfloat16)
        rise = v * (ROOT + (3 * ROOT * CUBE) * square)
        hidden = (act_grad * (above * (1.0 + (1.0 - curve) * rise))).astype(jnp.bfloat16)
        grad_out[...] += lax.dot_general(
            out_grad, twice, (((0,), (0,)), ((), ())), preferred_element_type=jnp.float32
        )
        grad_in[...] += jnp.dot(
            jnp.concatenate([normed.T, ones], axis=0), hidden, preferred_element_type=jnp.float32
        )
        norm_grad = lax.dot_general(
            hidden, w_in_ref[...], (((1,), (1,)), ((), ())), preferred_element_type=jnp.float32
        )
        gain_sum[...] += jnp.sum((norm_grad * scaled).reshape(-1, SUB, 128), axis=0)
        shift_sum[...] += jnp.sum(norm_grad.reshape(-1, SUB, 128), axis=0)
        weighted = norm_grad * gain
        conv_grad = inverse * (
            weighted
            - jnp.mean(weighted, axis=-1, keepdims=True)
            - scaled * jnp.mean(weighted * scaled, axis=-1, keepdims=True)
        )
        rounded = conv_grad.astype(jnp.bfloat16).astype(jnp.float32)
        bias_sum[...] += jnp.sum(rounded.reshape(-1, SUB, 128), axis=0)
        round_ref[...] = rounded
        for r in range(chunk):
            natural = gather_row(
                [rounded[r * 64 + t * SUB : r * 64 + (t + 1) * SUB] for t in range(SUB)], buf_ref
            )
            conv_grad_ref[first + r] = natural.astype(jnp.bfloat16)
        return 0

    one(0, None)
    lax.fori_loop(1, height // chunk, one, 0)
    top_ref[...] = conv_grad_ref[height - HALF :]
    bottom_ref[...] = conv_grad_ref[0:HALF]
    taps(height - chunk)
    pack(taps_ref, bias_sum, gain_sum, shift_sum, grad_in, grad_out, packed_ref, small_ref)


def pack(taps_ref, bias_sum, gain_sum, shift_sum, grad_in, grad_out, out_ref, small_ref):
    small_ref[...] = jnp.zeros_like(small_ref)
    for a in range(KS):
        for b in range(KS):
            small_ref[a * KS + b] = jnp.sum(taps_ref[a, b], axis=0)
    for at, ref in enumerate((bias_sum, gain_sum, shift_sum)):
        small_ref[KS * KS + at] = jnp.sum(ref[...], axis=0)
    for q in range(4):
        small_ref[KS * KS + 3 + q] = grad_in[128, q * 128 : (q + 1) * 128]
    parts = out_ref.shape[0]
    rows = 1024 // parts
    each = 128 // rows
    for at, ref, scale in ((0, grad_in, 1.0), (4, grad_out, 0.5)):
        for q in range(4):
            block = ref[0:128, q * 128 : (q + 1) * 128].reshape(each, rows, 128)
            out_ref[(at + q) * each : (at + q + 1) * each, 0:rows, :] = (block * scale).astype(jnp.bfloat16)
    per = SMALL // parts
    spare = out_ref.shape[1] - rows - 2 * per
    small = small_ref[...].reshape(parts, per, 128)
    high = small.astype(jnp.bfloat16).astype(jnp.float32)
    pieces = [high, small - high] + ([jnp.zeros((parts, spare, 128), jnp.float32)] if spare else [])
    out_ref[:, rows:, :] = jnp.concatenate(pieces, axis=1).astype(jnp.bfloat16)


def back_kernel(even_ref, spread_in, keep_ref, got_ref, cot_ref, mask_ref, kernel_ref, spread_ref, out_ref, cols_ref, buf_ref):
    del spread_in
    height = cot_ref.shape[0]
    edge_columns(even_ref[0] == 1, keep_ref, got_ref, cols_ref)
    add_edges(cols_ref, kernel_ref, spread_ref, height, True)

    def one(step, _):
        for r in range(4):
            row = step * 4 + r
            for t in range(SUB):
                buf_ref[pl.ds(r * 64 + t, SUB, stride=SUB), :] = spread_ref[pl.ds(row * 64 + t * SUB, SUB), :]
        for r in range(4):
            row = step * 4 + r
            spread = buf_ref[r * 64 : (r + 1) * 64, :]
            out_ref[row] = (
                (cot_ref[row].astype(jnp.float32) + spread) * mask_ref[row].astype(jnp.float32)
            ).astype(jnp.bfloat16)
        return 0

    lax.fori_loop(0, height // 4, one, 0)


def fold_kernel(rows, per, parts_ref, out_ref):
    total = jnp.sum(parts_ref[...].astype(jnp.float32), axis=0)
    small = total[rows : rows + per] + total[rows + per : rows + 2 * per]
    high = small.astype(jnp.bfloat16).astype(jnp.float32)
    pieces = [total[0:rows], high, small - high]
    if total.shape[0] > rows + 2 * per:
        pieces.append(jnp.zeros((total.shape[0] - rows - 2 * per, 128), jnp.float32))
    total = jnp.concatenate(pieces, axis=0).astype(jnp.bfloat16)
    out_ref[...] = jnp.broadcast_to(total[None], out_ref.shape)


def unpack_kernel(factor, all_ref, kernel_ref, bias_ref, gain_ref, shift_ref, in_ref, b_ref, out_ref):
    parts = all_ref.shape[0]
    rows = 1024 // parts
    each = 128 // rows
    for q in range(4):
        block = all_ref[q * each : (q + 1) * each, 0:rows, :].astype(jnp.float32)
        in_ref[:, q * 128 : (q + 1) * 128] = block.reshape(128, 128) * factor
    for q in range(4):
        block = all_ref[(4 + q) * each : (5 + q) * each, 0:rows, :].astype(jnp.float32)
        out_ref[q * 128 : (q + 1) * 128, :] = block.reshape(128, 128).T * factor
    per = SMALL // parts
    both = all_ref[:, rows:, :].astype(jnp.float32)
    small = (both[:, 0:per] + both[:, per : 2 * per]) * factor

    def row(r):
        return small[r // (SMALL // parts), r % (SMALL // parts)]

    for a in range(KS):
        for b in range(KS):
            kernel_ref[a, b] = row(a * KS + b)
    for at, ref in enumerate((bias_ref, gain_ref, shift_ref)):
        ref[0] = row(KS * KS + at)
    for q in range(4):
        b_ref[0, q * 128 : (q + 1) * 128] = row(KS * KS + 3 + q)


def groups():
    count_lon, count_lat = lax.axis_size("lon"), lax.axis_size("lat")
    plane = [[[] for _ in range(count_lat // 2)] for _ in range(2)]
    column = [[[] for _ in range(2)] for _ in range(count_lon // 2)]
    for lon in range(count_lon):
        for lat in range(count_lat):
            at = lon * count_lat + lat
            plane[lon % 2][lat // 2].append(at)
            column[lon // 2][lat % 2].append(at)
    return [g for part in plane for g in part], [g for part in column for g in part]


def exchange(parts, members):
    return lax.all_to_all(parts, ("lon", "lat"), 0, 0, tiled=True, axis_index_groups=members)


def summed(packed):
    count_lon = lax.axis_size("lon")
    plane, column = groups()

    def fold(parts, count):
        return pl.pallas_call(
            functools.partial(fold_kernel, 1024 // count_lon, SMALL // count_lon),
            out_shape=jax.ShapeDtypeStruct((count,) + parts.shape[1:], jnp.bfloat16),
            in_specs=[VMEM],
            out_specs=VMEM,
            name="fold",
        compiler_params=PARAMS,
        )(parts)

    held = exchange(packed, plane)
    held = fold(held, len(column[0]))
    held = exchange(held, column)
    held = fold(held, len(plane[0]))
    return exchange(held, plane)


def lat_halo(top, bottom):
    count = lax.axis_size("lat")
    up = [(i, i + 1) for i in range(count - 1)]
    down = [(i + 1, i) for i in range(count - 1)]
    south = lax.ppermute(top, "lat", up)
    north = lax.ppermute(bottom, "lat", down)
    return south, north


def onward_pairs():
    count = lax.axis_size("lon")
    return [(i, (i + 2) % count) for i in range(0, count, 2)] + [(i, (i - 2) % count) for i in range(1, count, 2)]


def lon_halo(even, south, block, north):
    tall = block.shape[0] + 2 * HALF + 2
    strips = pl.pallas_call(
        strip_kernel,
        out_shape=jax.ShapeDtypeStruct((2, HALF, tall, 128), jnp.bfloat16),
        in_specs=[SMEM, VMEM, VMEM, VMEM],
        out_specs=VMEM,
        scratch_shapes=[pltpu.VMEM((tall * SUB, 128), jnp.float32)] * 2,
        name="strips",
        compiler_params=PARAMS,
    )(even, south, block, north)
    swapped = lax.ppermute(strips, "lon", [(i, i ^ 1) for i in range(lax.axis_size("lon"))])
    onward = pl.pallas_call(
        onward_kernel,
        out_shape=jax.ShapeDtypeStruct(swapped.shape[1:], jnp.bfloat16),
        in_specs=[VMEM],
        out_specs=VMEM,
        compiler_params=PARAMS,
        name="onward",
    )(swapped)
    got = lax.ppermute(onward, "lon", onward_pairs())
    return swapped, got


def first_conv(south, block, north, kernel, rows, flip):
    height, across, channels = block.shape
    tiles = pltpu.VMEM(((height + 2 * HALF + 2) * WIDE * SUB, channels), jnp.float32)
    out = pltpu.VMEM((height * across, channels), jnp.float32)
    buf = pltpu.VMEM((SUB * SUB + 2 * SUB, channels), jnp.float32)
    return pl.pallas_call(
        functools.partial(conv_kernel, rows, flip),
        out_shape=out if flip else (out, tiles),
        in_specs=[VMEM] * 4,
        out_specs=VMEM if flip else [VMEM] * 2,
        scratch_shapes=[tiles, buf] if flip else [buf],
        compiler_params=CONV_PARAMS,
        name="back_conv" if flip else "conv",
    )(south, block, north, kernel)


def last_conv(conv, tiles, kernel, rows, flip):
    return pl.pallas_call(
        functools.partial(rest_kernel, rows, flip),
        out_shape=pltpu.VMEM(conv.shape, jnp.float32),
        in_specs=[VMEM] * 3,
        out_specs=VMEM,
        input_output_aliases={0: 0},
        compiler_params=CONV_PARAMS,
        name="back_rest" if flip else "rest",
    )(*[pltpu.with_memory_space_constraint(x, pltpu.VMEM) for x in (conv, tiles)], kernel)


def f32(*shape):
    return jax.ShapeDtypeStruct(shape, jnp.float32)


def body(cells, ocean_mask, cotangent, kernel, conv_bias, gain, shift, w_in, b_in, w_out, chunk=8):
    height, across, channels = cells.shape
    ocean = jnp.broadcast_to(ocean_mask.astype(jnp.bfloat16)[..., None], cells.shape)
    masked = cells * ocean
    out_grad = cotangent * ocean
    strip = jax.ShapeDtypeStruct((HALF, across, channels), jnp.bfloat16)
    even = (1 - lax.axis_index("lon") % 2).astype(jnp.int32).reshape(1)
    south, north = lat_halo(masked[-HALF:], masked[:HALF])
    keep, got = lon_halo(even, south, masked, north)
    early = height * 9 // 16
    conv, tiles = first_conv(south, masked, north, kernel, early, False)
    conv = last_conv(conv, tiles, kernel, early, False)
    parts = lax.axis_size("lon")
    hidden = w_in.shape[1]
    _, _, conv_grad, top, bottom, packed = pl.pallas_call(
        functools.partial(block_kernel, chunk),
        out_shape=(
            pltpu.VMEM(conv.shape, jnp.float32), pltpu.VMEM(tiles.shape, jnp.float32),
            jax.ShapeDtypeStruct(cells.shape, jnp.bfloat16),
            strip, strip,
            jax.ShapeDtypeStruct((parts, 1024 // parts + max(8, 2 * SMALL // parts), channels), jnp.bfloat16),
        ),
        in_specs=[SMEM] + [VMEM] * 12,
        out_specs=[VMEM] * 6,
        scratch_shapes=[
            pltpu.VMEM((2 * HALF, height + 2 * HALF + 2, channels), jnp.float32),
            pltpu.VMEM((80, channels), jnp.float32),
            pltpu.VMEM((chunk, SUB, SUB, channels), jnp.float32),
            pltpu.VMEM((chunk * 64, channels), jnp.float32),
            pltpu.VMEM((KS, KS, SUB, channels), jnp.float32),
            pltpu.VMEM((SMALL, channels), jnp.float32),
            pltpu.VMEM((SUB, channels), jnp.float32),
            pltpu.VMEM((SUB, channels), jnp.float32),
            pltpu.VMEM((SUB, channels), jnp.float32),
            pltpu.VMEM((channels + 16, hidden), jnp.float32),
            pltpu.VMEM((channels, hidden), jnp.float32),
        ],
        input_output_aliases={1: 0, 2: 1},
        name="block",
        compiler_params=PARAMS,
    )(
        even, *[pltpu.with_memory_space_constraint(x, pltpu.VMEM) for x in (conv, tiles)], keep, got, out_grad, kernel, conv_bias.reshape(1, -1), gain.reshape(1, -1),
        shift.reshape(1, -1), w_in, b_in.reshape(1, -1), w_out,
    )
    total = summed(packed)
    south, north = lat_halo(top, bottom)
    keep, got = lon_halo(even, south, conv_grad, north)
    half = height * 9 // 16
    spread = first_conv(south, conv_grad, north, kernel, half, True)
    spread = pl.pallas_call(
        functools.partial(back_rest_kernel, half),
        out_shape=pltpu.VMEM(spread.shape, jnp.float32),
        in_specs=[VMEM] * 4,
        out_specs=VMEM,
        scratch_shapes=[
            pltpu.VMEM(((height + 2 * HALF - half) * WIDE * SUB, channels), jnp.float32),
            pltpu.VMEM((SUB * SUB + 2 * SUB, channels), jnp.float32),
        ],
        input_output_aliases={0: 0},
        compiler_params=CONV_PARAMS,
        name="back_rest",
    )(pltpu.with_memory_space_constraint(spread, pltpu.VMEM), conv_grad, north, kernel)
    _, cells_grad = pl.pallas_call(
        back_kernel,
        out_shape=(pltpu.VMEM(spread.shape, jnp.float32), jax.ShapeDtypeStruct(cells.shape, jnp.bfloat16)),
        in_specs=[SMEM] + [VMEM] * 6,
        out_specs=[VMEM] * 2,
        scratch_shapes=[
            pltpu.VMEM((2 * HALF, height + 2 * HALF + 2, channels), jnp.float32),
            pltpu.VMEM((4 * 64, channels), jnp.float32),
        ],
        input_output_aliases={1: 0},
        name="back",
        compiler_params=PARAMS,
    )(even, pltpu.with_memory_space_constraint(spread, pltpu.VMEM), keep, got, cotangent, ocean, kernel)
    count = height * across * lax.axis_size("lon") * lax.axis_size("lat")
    gk, gb, gg, gs, gi, gh, go = pl.pallas_call(
        functools.partial(unpack_kernel, count ** -0.5),
        out_shape=(
            f32(KS, KS, channels), f32(1, channels), f32(1, channels), f32(1, channels),
            f32(channels, hidden), f32(1, hidden), f32(hidden, channels),
        ),
        in_specs=[VMEM],
        out_specs=[VMEM] * 7,
        name="unpack",
        compiler_params=PARAMS,
    )(total)
    return cells_grad, gk, gb[0], gg[0], gs[0], gi, gh[0], go


def solution(mesh):
    whole = P("lat", "lon", None)
    in_specs = (whole, P("lat", "lon"), whole) + (P(),) * 7
    out_specs = (whole,) + (P(),) * 7
    return jax.shard_map(body, mesh=mesh, in_specs=in_specs, out_specs=out_specs, check_vma=False)
```

```python
import functools

import jax
import jax.numpy as jnp
from jax import lax
from jax.experimental import pallas as pl
from jax.experimental.pallas import tpu as pltpu
from jax.sharding import PartitionSpec as P


KS = 7
HALF = 3
SMALL = 64
WIDE = 14
SUB = 8
ROOT = 0.7978845608028654
CUBE = 0.044715
VMEM = pl.BlockSpec(memory_space=pltpu.VMEM)
PARAMS = pltpu.CompilerParams(vmem_limit_bytes=28 << 20)
CONV_PARAMS = pltpu.CompilerParams(vmem_limit_bytes=28 << 20)
SMEM = pl.BlockSpec(memory_space=pltpu.SMEM)


def spread_row(row_of, row, tiles_ref, buf_ref):
    buf_ref[HALF : HALF + 64, :] = row_of.astype(jnp.float32)
    for tap in range(WIDE):
        tiles_ref[pl.ds(row * (WIDE * SUB) + tap * SUB, SUB), :] = buf_ref[pl.ds(tap, SUB, stride=SUB), :]


def spread_all(south_ref, block_ref, north_ref, tiles_ref, buf_ref, rows=None):
    height = block_ref.shape[0]
    buf_ref[...] = jnp.zeros_like(buf_ref)
    for row in range(HALF):
        spread_row(south_ref[row], row, tiles_ref, buf_ref)
        if rows is None:
            spread_row(north_ref[row], height + HALF + row, tiles_ref, buf_ref)

    def one(row, _):
        spread_row(block_ref[row], row + HALF, tiles_ref, buf_ref)
        return 0

    lax.fori_loop(0, height if rows is None else rows, one, 0)
    if rows is not None:
        return
    last = (height + 2 * HALF) * WIDE * SUB
    tiles_ref[last:, :] = jnp.zeros((2 * WIDE * SUB, 128), jnp.float32)


def tile(tiles_ref, row, t):
    return tiles_ref[pl.ds(row * (WIDE * SUB) + t * SUB, SUB), :]


def tap_weight(kernel_ref, a, b, flip):
    if flip:
        a, b = KS - 1 - a, KS - 1 - b
    return jnp.broadcast_to(kernel_ref[a, b : b + 1, :], (SUB, 128))


def conv_rows(tiles_ref, kernel_ref, out_ref, start, stop, flip, base=0):
    def one(step, _):
        first = start + 2 * step
        totals = [[None] * SUB, [None] * SUB]
        for near in range(KS + 1):
            cells = [tile(tiles_ref, first + near - base, t) for t in range(WIDE)]
            for r in range(2):
                a = near - r
                if not 0 <= a < KS:
                    continue
                total = totals[r]
                for b in range(KS):
                    weight = tap_weight(kernel_ref, a, b, flip)
                    for t in range(SUB):
                        term = weight * cells[t + b]
                        total[t] = term if total[t] is None else total[t] + term
        for r in range(2):
            for t in range(SUB):
                out_ref[pl.ds((first + r) * 64 + t * SUB, SUB), :] = totals[r][t]
        return 0

    lax.fori_loop(0, (stop - start) // 2, one, 0)


def edge_columns(even, keep_ref, got_ref, cols_ref):
    for c in range(HALF):
        keep = keep_ref[0, c].astype(jnp.float32)
        got = got_ref[c].astype(jnp.float32)
        cols_ref[c] = jnp.where(even, got, keep)
        cols_ref[HALF + c] = jnp.where(even, keep, got)


def add_edges(cols_ref, kernel_ref, out_ref, height, flip):
    for west in (True, False):
        for at in range(HALF):
            first = at * SUB if west else (SUB - HALF + at) * SUB + SUB - 1
            totals = [None] * (height // SUB)
            for a in range(KS):
                for b in range(KS):
                    c = at + b if west else at + b - HALF
                    if not ((0 <= c < HALF) if west else (HALF <= c < 2 * HALF)):
                        continue
                    weight = tap_weight(kernel_ref, a, b, flip)
                    for block in range(height // SUB):
                        term = weight * cols_ref[c, pl.ds(block * SUB + a, SUB), :]
                        totals[block] = term if totals[block] is None else totals[block] + term
            for block in range(height // SUB):
                place = pl.ds(block * SUB * 64 + first, SUB, stride=64)
                out_ref[place, :] = out_ref[place, :] + totals[block]


def gather_row(tiles, buf_ref):
    for t in range(SUB):
        buf_ref[pl.ds(t, SUB, stride=SUB), :] = tiles[t]
    return buf_ref[0 : SUB * SUB, :]


def onward_kernel(both_ref, out_ref):
    out_ref[...] = both_ref[1]


def strip_kernel(even_ref, south_ref, block_ref, north_ref, out_ref, low_ref, high_ref):
    height = block_ref.shape[0]

    def put(at, row_of):
        low_ref[pl.ds(at * SUB, SUB), :] = row_of[0:SUB].astype(jnp.float32)
        high_ref[pl.ds(at * SUB, SUB), :] = row_of[64 - SUB : 64].astype(jnp.float32)

    for row in range(HALF):
        put(row, south_ref[row])
        put(row + height + HALF, north_ref[row])

    def one(step, _):
        for r in range(SUB):
            put(step * SUB + r + HALF, block_ref[step * SUB + r])
        return 0

    lax.fori_loop(0, height // SUB, one, 0)
    tall = height + 2 * HALF + 2
    low_ref[(tall - 2) * SUB :, :] = jnp.zeros((2 * SUB, 128), jnp.float32)
    high_ref[(tall - 2) * SUB :, :] = jnp.zeros((2 * SUB, 128), jnp.float32)
    even = even_ref[0] == 1
    for c in range(HALF):
        west = low_ref[pl.ds(c, tall, stride=SUB), :]
        east = high_ref[pl.ds(SUB - HALF + c, tall, stride=SUB), :]
        out_ref[0, c] = jnp.where(even, east, west).astype(jnp.bfloat16)
        out_ref[1, c] = jnp.where(even, west, east).astype(jnp.bfloat16)


def rest_kernel(start, flip, conv_in, tiles_ref, kernel_ref, out_ref):
    del conv_in
    conv_rows(tiles_ref, kernel_ref, out_ref, start, out_ref.shape[0] // 64, flip)


def conv_kernel(rows, flip, south_ref, block_ref, north_ref, kernel_ref, out_ref, tiles_ref, buf_ref):
    spread_all(south_ref, block_ref, north_ref, tiles_ref, buf_ref, None)
    conv_rows(tiles_ref, kernel_ref, out_ref, 0, rows, flip)


def block_kernel(
    chunk,
    even_ref, conv_in, tiles_in, keep_ref, got_ref, out_grad_ref,
    kernel_ref, bias_ref, gain_ref, shift_ref, w_in_ref, b_in_ref, w_out_ref,
    conv_ref, tiles_ref, conv_grad_ref, top_ref, bottom_ref, packed_ref,
    cols_ref, buf_ref, og_tiles, round_ref, taps_ref, small_ref,
    bias_sum, gain_sum, shift_sum, grad_in, grad_out,
):
    del conv_in, tiles_in
    height = out_grad_ref.shape[0]
    cells = chunk * 64
    edge_columns(even_ref[0] == 1, keep_ref, got_ref, cols_ref)
    span = WIDE * SUB
    for c in range(HALF):
        for block in range((height + 2 * HALF + 2) // SUB):
            rows = pl.ds(block * SUB, SUB)
            start = block * SUB * span
            tiles_ref[pl.ds(start + c * SUB, SUB, stride=span), :] = cols_ref[c, rows, :]
            tiles_ref[pl.ds(start + (SUB + HALF + c) * SUB + SUB - 1, SUB, stride=span), :] = cols_ref[HALF + c, rows, :]
    add_edges(cols_ref, kernel_ref, conv_ref, height, False)
    for ref in (bias_sum, gain_sum, shift_sum, grad_in, grad_out, taps_ref):
        ref[...] = jnp.zeros_like(ref)
    bias = bias_ref[...]
    gain = gain_ref[...]
    shift = shift_ref[...]
    b_in = b_in_ref[...]
    w_half = w_out_ref[...] * jnp.bfloat16(0.5)

    ones = jnp.where(
        lax.broadcasted_iota(jnp.int32, (16, cells), 0) == 0, 1.0, 0.0
    ).astype(jnp.bfloat16)

    def taps(first):
        for r in range(chunk):
            row = first + r
            grads = [round_ref[r * 64 + t * SUB : r * 64 + (t + 1) * SUB, :] for t in range(SUB)]
            for a in range(KS):
                near = [tile(tiles_ref, row + a, t) for t in range(WIDE)]
                for b in range(KS):
                    total = taps_ref[a, b]
                    for t in range(SUB):
                        total = total + grads[t] * near[t + b]
                    taps_ref[a, b] = total

    def one(step, pending):
        first = step * chunk
        if pending is not None:
            taps(first - chunk)
        for r in range(chunk):
            buf_ref[0:64, :] = out_grad_ref[first + r].astype(jnp.float32)
            for t in range(SUB):
                og_tiles[r, t] = buf_ref[pl.ds(t, SUB, stride=SUB), :]
        conv = conv_ref[pl.ds(first * 64, cells), :] + bias
        out_grad = og_tiles[...].reshape(cells, 128).astype(jnp.bfloat16)
        average = jnp.mean(conv, axis=-1, keepdims=True)
        centred = conv - average
        variance = jnp.mean(centred * centred, axis=-1, keepdims=True)
        inverse = lax.rsqrt(variance + 1e-06)
        scaled = centred * inverse
        normed = (scaled * gain + shift).astype(jnp.bfloat16)
        v = jnp.dot(normed, w_in_ref[...], preferred_element_type=jnp.float32) + b_in
        act_grad = lax.dot_general(
            out_grad, w_half, (((1,), (1,)), ((), ())), preferred_element_type=jnp.float32
        )
        square = v * v
        curve = jnp.tanh(v * (ROOT + (ROOT * CUBE) * square))
        above = 1.0 + curve
        twice = (v * above).astype(jnp.bfloat16)
        rise = v * (ROOT + (3 * ROOT * CUBE) * square)
        hidden = (act_grad * (above * (1.0 + (1.0 - curve) * rise))).astype(jnp.bfloat16)
        grad_out[...] += lax.dot_general(
            out_grad, twice, (((0,), (0,)), ((), ())), preferred_element_type=jnp.float32
        )
        grad_in[...] += jnp.dot(
            jnp.concatenate([normed.T, ones], axis=0), hidden, preferred_element_type=jnp.float32
        )
        norm_grad = lax.dot_general(
            hidden, w_in_ref[...], (((1,), (1,)), ((), ())), preferred_element_type=jnp.float32
        )
        gain_sum[...] += jnp.sum((norm_grad * scaled).reshape(-1, SUB, 128), axis=0)
        shift_sum[...] += jnp.sum(norm_grad.reshape(-1, SUB, 128), axis=0)
        weighted = norm_grad * gain
        conv_grad = inverse * (
            weighted
            - jnp.mean(weighted, axis=-1, keepdims=True)
            - scaled * jnp.mean(weighted * scaled, axis=-1, keepdims=True)
        )
        rounded = conv_grad.astype(jnp.bfloat16).astype(jnp.float32)
        bias_sum[...] += jnp.sum(rounded.reshape(-1, SUB, 128), axis=0)
        round_ref[...] = rounded
        for r in range(chunk):
            natural = gather_row(
                [rounded[r * 64 + t * SUB : r * 64 + (t + 1) * SUB] for t in range(SUB)], buf_ref
            )
            conv_grad_ref[first + r] = natural.astype(jnp.bfloat16)
        return 0

    one(0, None)
    lax.fori_loop(1, height // chunk, one, 0)
    top_ref[...] = conv_grad_ref[height - HALF :]
    bottom_ref[...] = conv_grad_ref[0:HALF]
    taps(height - chunk)
    pack(taps_ref, bias_sum, gain_sum, shift_sum, grad_in, grad_out, packed_ref, small_ref)


def pack(taps_ref, bias_sum, gain_sum, shift_sum, grad_in, grad_out, out_ref, small_ref):
    small_ref[...] = jnp.zeros_like(small_ref)
    for a in range(KS):
        for b in range(KS):
            small_ref[a * KS + b] = jnp.sum(taps_ref[a, b], axis=0)
    for at, ref in enumerate((bias_sum, gain_sum, shift_sum)):
        small_ref[KS * KS + at] = jnp.sum(ref[...], axis=0)
    for q in range(4):
        small_ref[KS * KS + 3 + q] = grad_in[128, q * 128 : (q + 1) * 128]
    parts = out_ref.shape[0]
    rows = 1024 // parts
    each = 128 // rows
    for at, ref, scale in ((0, grad_in, 1.0), (4, grad_out, 0.5)):
        for q in range(4):
            block = ref[0:128, q * 128 : (q + 1) * 128].reshape(each, rows, 128)
            out_ref[(at + q) * each : (at + q + 1) * each, 0:rows, :] = (block * scale).astype(jnp.bfloat16)
    per = SMALL // parts
    spare = out_ref.shape[1] - rows - 2 * per
    small = small_ref[...].reshape(parts, per, 128)
    high = small.astype(jnp.bfloat16).astype(jnp.float32)
    pieces = [high, small - high] + ([jnp.zeros((parts, spare, 128), jnp.float32)] if spare else [])
    out_ref[:, rows:, :] = jnp.concatenate(pieces, axis=1).astype(jnp.bfloat16)


def back_kernel(even_ref, spread_in, keep_ref, got_ref, cot_ref, mask_ref, kernel_ref, spread_ref, out_ref, cols_ref, buf_ref):
    del spread_in
    height = cot_ref.shape[0]
    edge_columns(even_ref[0] == 1, keep_ref, got_ref, cols_ref)
    add_edges(cols_ref, kernel_ref, spread_ref, height, True)

    def one(step, _):
        for r in range(4):
            row = step * 4 + r
            for t in range(SUB):
                buf_ref[pl.ds(r * 64 + t, SUB, stride=SUB), :] = spread_ref[pl.ds(row * 64 + t * SUB, SUB), :]
        for r in range(4):
            row = step * 4 + r
            spread = buf_ref[r * 64 : (r + 1) * 64, :]
            out_ref[row] = (
                (cot_ref[row].astype(jnp.float32) + spread) * mask_ref[row].astype(jnp.float32)
            ).astype(jnp.bfloat16)
        return 0

    lax.fori_loop(0, height // 4, one, 0)


def fold_kernel(rows, per, parts_ref, out_ref):
    total = jnp.sum(parts_ref[...].astype(jnp.float32), axis=0)
    small = total[rows : rows + per] + total[rows + per : rows + 2 * per]
    high = small.astype(jnp.bfloat16).astype(jnp.float32)
    pieces = [total[0:rows], high, small - high]
    if total.shape[0] > rows + 2 * per:
        pieces.append(jnp.zeros((total.shape[0] - rows - 2 * per, 128), jnp.float32))
    total = jnp.concatenate(pieces, axis=0).astype(jnp.bfloat16)
    out_ref[...] = jnp.broadcast_to(total[None], out_ref.shape)


def unpack_kernel(factor, all_ref, kernel_ref, bias_ref, gain_ref, shift_ref, in_ref, b_ref, out_ref):
    parts = all_ref.shape[0]
    rows = 1024 // parts
    each = 128 // rows
    for q in range(4):
        block = all_ref[q * each : (q + 1) * each, 0:rows, :].astype(jnp.float32)
        in_ref[:, q * 128 : (q + 1) * 128] = block.reshape(128, 128) * factor
    for q in range(4):
        block = all_ref[(4 + q) * each : (5 + q) * each, 0:rows, :].astype(jnp.float32)
        out_ref[q * 128 : (q + 1) * 128, :] = block.reshape(128, 128).T * factor
    per = SMALL // parts
    both = all_ref[:, rows:, :].astype(jnp.float32)
    small = (both[:, 0:per] + both[:, per : 2 * per]) * factor

    def row(r):
        return small[r // (SMALL // parts), r % (SMALL // parts)]

    for a in range(KS):
        for b in range(KS):
            kernel_ref[a, b] = row(a * KS + b)
    for at, ref in enumerate((bias_ref, gain_ref, shift_ref)):
        ref[0] = row(KS * KS + at)
    for q in range(4):
        b_ref[0, q * 128 : (q + 1) * 128] = row(KS * KS + 3 + q)


def groups():
    count_lon, count_lat = lax.axis_size("lon"), lax.axis_size("lat")
    plane = [[[] for _ in range(count_lat // 2)] for _ in range(2)]
    column = [[[] for _ in range(2)] for _ in range(count_lon // 2)]
    for lon in range(count_lon):
        for lat in range(count_lat):
            at = lon * count_lat + lat
            plane[lon % 2][lat // 2].append(at)
            column[lon // 2][lat % 2].append(at)
    return [g for part in plane for g in part], [g for part in column for g in part]


def exchange(parts, members):
    return lax.all_to_all(parts, ("lon", "lat"), 0, 0, tiled=True, axis_index_groups=members)


def summed(packed):
    count_lon = lax.axis_size("lon")
    plane, column = groups()

    def fold(parts, count):
        return pl.pallas_call(
            functools.partial(fold_kernel, 1024 // count_lon, SMALL // count_lon),
            out_shape=jax.ShapeDtypeStruct((count,) + parts.shape[1:], jnp.bfloat16),
            in_specs=[VMEM],
            out_specs=VMEM,
            name="fold",
        compiler_params=PARAMS,
        )(parts)

    held = exchange(packed, plane)
    held = fold(held, len(column[0]))
    held = exchange(held, column)
    held = fold(held, len(plane[0]))
    return exchange(held, plane)


def lat_halo(top, bottom):
    count = lax.axis_size("lat")
    up = [(i, i + 1) for i in range(count - 1)]
    down = [(i + 1, i) for i in range(count - 1)]
    south = lax.ppermute(top, "lat", up)
    north = lax.ppermute(bottom, "lat", down)
    return south, north


def onward_pairs():
    count = lax.axis_size("lon")
    return [(i, (i + 2) % count) for i in range(0, count, 2)] + [(i, (i - 2) % count) for i in range(1, count, 2)]


def lon_halo(even, south, block, north):
    tall = block.shape[0] + 2 * HALF + 2
    strips = pl.pallas_call(
        strip_kernel,
        out_shape=jax.ShapeDtypeStruct((2, HALF, tall, 128), jnp.bfloat16),
        in_specs=[SMEM, VMEM, VMEM, VMEM],
        out_specs=VMEM,
        scratch_shapes=[pltpu.VMEM((tall * SUB, 128), jnp.float32)] * 2,
        name="strips",
        compiler_params=PARAMS,
    )(even, south, block, north)
    swapped = lax.ppermute(strips, "lon", [(i, i ^ 1) for i in range(lax.axis_size("lon"))])
    onward = pl.pallas_call(
        onward_kernel,
        out_shape=jax.ShapeDtypeStruct(swapped.shape[1:], jnp.bfloat16),
        in_specs=[VMEM],
        out_specs=VMEM,
        compiler_params=PARAMS,
        name="onward",
    )(swapped)
    got = lax.ppermute(onward, "lon", onward_pairs())
    return swapped, got


def first_conv(south, block, north, kernel, rows, flip):
    height, across, channels = block.shape
    tiles = pltpu.VMEM(((height + 2 * HALF + 2) * WIDE * SUB, channels), jnp.float32)
    out = pltpu.VMEM((height * across, channels), jnp.float32)
    buf = pltpu.VMEM((SUB * SUB + 2 * SUB, channels), jnp.float32)
    return pl.pallas_call(
        functools.partial(conv_kernel, rows, flip),
        out_shape=out if flip else (out, tiles),
        in_specs=[VMEM] * 4,
        out_specs=VMEM if flip else [VMEM] * 2,
        scratch_shapes=[tiles, buf] if flip else [buf],
        compiler_params=CONV_PARAMS,
        name="back_conv" if flip else "conv",
    )(south, block, north, kernel)


def last_conv(conv, tiles, kernel, rows, flip):
    return pl.pallas_call(
        functools.partial(rest_kernel, rows, flip),
        out_shape=pltpu.VMEM(conv.shape, jnp.float32),
        in_specs=[VMEM] * 3,
        out_specs=VMEM,
        input_output_aliases={0: 0},
        compiler_params=CONV_PARAMS,
        name="back_rest" if flip else "rest",
    )(*[pltpu.with_memory_space_constraint(x, pltpu.VMEM) for x in (conv, tiles)], kernel)


def f32(*shape):
    return jax.ShapeDtypeStruct(shape, jnp.float32)


def body(cells, ocean_mask, cotangent, kernel, conv_bias, gain, shift, w_in, b_in, w_out, chunk=8):
    height, across, channels = cells.shape
    ocean = jnp.broadcast_to(ocean_mask.astype(jnp.bfloat16)[..., None], cells.shape)
    masked = cells * ocean
    out_grad = cotangent * ocean
    strip = jax.ShapeDtypeStruct((HALF, across, channels), jnp.bfloat16)
    even = (1 - lax.axis_index("lon") % 2).astype(jnp.int32).reshape(1)
    south, north = lat_halo(masked[-HALF:], masked[:HALF])
    keep, got = lon_halo(even, south, masked, north)
    early = height * 9 // 16
    conv, tiles = first_conv(south, masked, north, kernel, early, False)
    conv = last_conv(conv, tiles, kernel, early, False)
    parts = lax.axis_size("lon")
    hidden = w_in.shape[1]
    _, _, conv_grad, top, bottom, packed = pl.pallas_call(
        functools.partial(block_kernel, chunk),
        out_shape=(
            pltpu.VMEM(conv.shape, jnp.float32), pltpu.VMEM(tiles.shape, jnp.float32),
            jax.ShapeDtypeStruct(cells.shape, jnp.bfloat16),
            strip, strip,
            jax.ShapeDtypeStruct((parts, 1024 // parts + max(8, 2 * SMALL // parts), channels), jnp.bfloat16),
        ),
        in_specs=[SMEM] + [VMEM] * 12,
        out_specs=[VMEM] * 6,
        scratch_shapes=[
            pltpu.VMEM((2 * HALF, height + 2 * HALF + 2, channels), jnp.float32),
            pltpu.VMEM((80, channels), jnp.float32),
            pltpu.VMEM((chunk, SUB, SUB, channels), jnp.float32),
            pltpu.VMEM((chunk * 64, channels), jnp.float32),
            pltpu.VMEM((KS, KS, SUB, channels), jnp.float32),
            pltpu.VMEM((SMALL, channels), jnp.float32),
            pltpu.VMEM((SUB, channels), jnp.float32),
            pltpu.VMEM((SUB, channels), jnp.float32),
            pltpu.VMEM((SUB, channels), jnp.float32),
            pltpu.VMEM((channels + 16, hidden), jnp.float32),
            pltpu.VMEM((channels, hidden), jnp.float32),
        ],
        input_output_aliases={1: 0, 2: 1},
        name="block",
        compiler_params=PARAMS,
    )(
        even, *[pltpu.with_memory_space_constraint(x, pltpu.VMEM) for x in (conv, tiles)], keep, got, out_grad, kernel, conv_bias.reshape(1, -1), gain.reshape(1, -1),
        shift.reshape(1, -1), w_in, b_in.reshape(1, -1), w_out,
    )
    total = summed(packed)
    south, north = lat_halo(top, bottom)
    keep, got = lon_halo(even, south, conv_grad, north)
    spread = first_conv(south, conv_grad, north, kernel, height, True)
    _, cells_grad = pl.pallas_call(
        back_kernel,
        out_shape=(pltpu.VMEM(spread.shape, jnp.float32), jax.ShapeDtypeStruct(cells.shape, jnp.bfloat16)),
        in_specs=[SMEM] + [VMEM] * 6,
        out_specs=[VMEM] * 2,
        scratch_shapes=[
            pltpu.VMEM((2 * HALF, height + 2 * HALF + 2, channels), jnp.float32),
            pltpu.VMEM((4 * 64, channels), jnp.float32),
        ],
        input_output_aliases={1: 0},
        name="back",
        compiler_params=PARAMS,
    )(even, pltpu.with_memory_space_constraint(spread, pltpu.VMEM), keep, got, cotangent, ocean, kernel)
    count = height * across * lax.axis_size("lon") * lax.axis_size("lat")
    gk, gb, gg, gs, gi, gh, go = pl.pallas_call(
        functools.partial(unpack_kernel, count ** -0.5),
        out_shape=(
            f32(KS, KS, channels), f32(1, channels), f32(1, channels), f32(1, channels),
            f32(channels, hidden), f32(1, hidden), f32(hidden, channels),
        ),
        in_specs=[VMEM],
        out_specs=[VMEM] * 7,
        name="unpack",
        compiler_params=PARAMS,
    )(total)
    return cells_grad, gk, gb[0], gg[0], gs[0], gi, gh[0], go


def solution(mesh):
    whole = P("lat", "lon", None)
    in_specs = (whole, P("lat", "lon"), whole) + (P(),) * 7
    out_specs = (whole,) + (P(),) * 7
    return jax.shard_map(body, mesh=mesh, in_specs=in_specs, out_specs=out_specs, check_vma=False)
```
